32 devices in a mesh: section: 4 (over y, core), expert: 8 (over z, x).
Axes of the slice: x: 2, y: 2, z: 4, core: 2. Of those that a mesh axis runs over, the one named last changes fastest.
Arguments:
- acts: bfloat16 [4, 512, 2048], P('section', 'expert'), may hold values from -6 to 6
- norm_gains: float32 [4, 2, 2048], P('section'), may hold values from 0.5 to 5.5
- w_query: bfloat16 [4, 2048, 1024], P('section', None, 'expert'), may hold values from -0.125 to 0.125
- w_keyval: bfloat16 [4, 2048, 4, 256], P('section', 'expert'), may hold values from -0.125 to 0.125
- w_out: bfloat16 [4, 1024, 2048], P('section', 'expert'), may hold values from -0.5 to 0.5
- w_gate_up: bfloat16 [4, 32, 2048, 1536], P('section', 'expert'), may hold values from -0.125 to 0.125
- w_down: bfloat16 [4, 32, 768, 2048], P('section', 'expert'), may hold values from -0.21875 to 0.21875
- expert_ids: int32 [4, 512, 8], P('section', 'expert'), may hold values from 0 to 31, all different within a row; in each aligned block of 64 rows (0 to 63, 64 to 127, ..., all dimensions but the last counted through in order) at most 24 rows name the same one
- gate_weights: float32 [4, 512, 8], P('section', 'expert'), may hold values from 0.05 to 0.3
- segment_ids: int32 [4, 512], P('section'), may hold values from 0 to 15, never falling along the last dimension, each value on 1 to 128 neighbouring positions
Outputs:
- handed: bfloat16 [4, 512, 2048], P('section', 'expert')
The draws below stay inside these ranges and needn't reach their ends.
Inputs may be any that keep to these rules, and one draw needn't show every extreme that they name: `expert_ids`: A token names 8 different experts. In each section the tokens of one index of expert (aligned blocks of 64 tokens) name no expert more than 24 times, a bound that some block reaches. `segment_ids`: never falling along a section's positions; a segment holds at most 128 positions, and one exactly that many.
All inputs are finite; a program needn't handle non-finite values.
Results may differ from the reference program's by a relative error of at most 0.015.
The reference program's roundings to bfloat16 on the way count: a program that leaves them out, or rounds other values in their place, can miss the bound.
Values may be sent and summed in bfloat16 or wider, within the bound.
A program may use at most 128 MiB of HBM per device.

```python
import math
import jax
import jax.numpy as jnp
import numpy as np
from jax import lax

D = 2048
HD = 128
HEAD_DEV = 1
KV = 4
FF = 768
EXPERTS = 32
TOPK = 8
TOK_DEV = 64
HEADS = 8
CAP = 24
TOKENS = 512
SECTIONS = 4
N_EXPERT = 8


def draw_norm_gains(key, part):
    first_key, second_key = jax.random.split(key)
    attention_gain = jax.random.uniform(first_key, (SECTIONS, 1, D), jnp.float32, 0.6, 1.4)
    mixer_gain = jax.random.uniform(second_key, (SECTIONS, 1, D), jnp.float32, 0.6, 1.4)
    return jnp.concatenate([attention_gain, mixer_gain], axis=1)


def shard_levels(stream_key, dims, shards, low, high):
    factor_of, own = 1.0, jax.random.fold_in(stream_key, 6)
    for axis_at, blocks in shards:
        steps = jnp.exp(jax.random.uniform(jax.random.fold_in(own, axis_at), (blocks,), jnp.float32, low / len(shards), high / len(shards)))
        factor_of = factor_of * jnp.repeat(steps, dims[axis_at] // blocks).reshape([-1 if axis == axis_at else 1 for axis in range(len(dims))])
    return factor_of


def length_profile(count, total, limit, slope):
    loads = [(1 << 20) // math.isqrt(rank ** slope) + 1 for rank in range(2, count + 1)]
    rest, holding = total - limit - (count - 1), [1] * (count - 1)
    while rest > 0:
        movable = [i for i in range(count - 1) if holding[i] < limit]
        whole, left = sum([loads[i] for i in movable]), rest
        for i in movable:
            more = min(limit - holding[i], max(1, left * loads[i] // whole), rest)
            holding[i] = holding[i] + more
            rest = rest - more
    return np.array([limit] + holding)


def ragged_sizes(own_key, count, total, bound, slope):
    if count == 2:
        one = jax.random.randint(own_key, (), max(1, total - bound), min(bound, total - 1) + 1)
        return jnp.stack([one, total - one])
    lengths = jnp.asarray(length_profile(count, total, bound, slope), jnp.int32)
    twos = (count - 1) // 2
    donor, taker = lengths[1:1 + 2 * twos:2], lengths[2:2 + 2 * twos:2]
    room = jnp.minimum(donor - 1, bound - taker)
    moved = jax.random.randint(jax.random.fold_in(own_key, 1), (twos,), 0, 1 << 20) % (room + 1)
    lengths = lengths.at[1:1 + 2 * twos:2].set(donor - moved).at[2:2 + 2 * twos:2].set(taker + moved)
    return lengths[jax.random.permutation(jax.random.fold_in(own_key, 2), count)]


def shared_out(key, own, number, rows, number_of, top, bound, skew):
    order = jax.random.permutation(key, number_of)
    crowded, usual = portions_of(number_of, rows * top, bound, skew, True), portions_of(number_of, rows * top, bound, skew, False)
    places = jnp.arange(number_of)

    def named(lengths, offset_by):
        used = int((lengths > 0).sum())
        fixed = max(1, used // 4)
        passed = fixed + (places - fixed + offset_by * (used - fixed)) % max(1, number_of - fixed)
        return jnp.zeros((number_of,), jnp.int32).at[order[jnp.where(places < fixed, places, passed)]].set(jnp.asarray(lengths, jnp.int32))

    lengths = jnp.where(number % 4 == 0, named(crowded, number // 4), named(usual, number - number // 4 - 1))
    mixed = jax.random.permutation(jax.random.fold_in(own, 3), number_of)
    source_of, taker = mixed[0:number_of // 2 * 2:2], mixed[1:number_of // 2 * 2:2]
    slack = jnp.minimum(lengths[source_of] - 1, bound - lengths[taker]) // 2
    slack = jnp.where((source_of == order[0]) | (taker == order[0]) | (lengths[taker] == 0), 0, jnp.maximum(slack, 0))
    passed = jax.random.randint(jax.random.fold_in(own, 4), (number_of // 2,), 0, 1 << 20) % (slack + 1)
    lengths = lengths.at[source_of].add(-passed).at[taker].add(passed)
    members = jnp.searchsorted(jnp.cumsum(lengths), jnp.arange(rows * top), side="right").astype(jnp.int32)
    grid = members.reshape(top, rows).T
    grid = grid[jax.random.permutation(jax.random.fold_in(own, 1), rows)]
    offset_by = jax.random.randint(jax.random.fold_in(own, 2), (rows, 1), 0, top)
    return jnp.take_along_axis(grid, (jnp.arange(top)[None, :] + offset_by) % top, axis=1)


def portions_of(number_of, total, limit, slope, full):
    weights = [(1 << 20) // math.isqrt(standing ** slope) + 1 for standing in range(1, number_of + 1)]
    largest = limit if full else min(limit, max(-(-total // number_of), total * weights[0] // sum(weights)))
    least = 1 if total - largest >= number_of - 1 else 0
    given, spare = [largest] + [least] * (number_of - 1), total - largest - least * (number_of - 1)
    while spare > 0:
        free = [i for i in range(1, number_of) if given[i] < largest] or [i for i in range(1, number_of) if given[i] < limit]
        whole, remaining = sum([weights[i] for i in free]), spare
        for i in free:
            extra = min(limit - given[i], max(1, remaining * weights[i] // whole), spare)
            given[i] = given[i] + extra
            spare = spare - extra
    return np.array(given)


def normal_values(stream_key, dims, width, reach, cuts=(), kind=jnp.bfloat16):
    array = width * jax.random.normal(stream_key, dims, jnp.float32)
    if cuts:
        array = array * shard_levels(stream_key, dims, cuts, -0.22, 0.18)
    return jnp.clip(array, -reach, reach).astype(kind)


def setup_inputs(seed: int = 0) -> dict:
    key_list = jax.random.split(jax.random.key(seed), 11)
    acts = normal_values(key_list[0], (SECTIONS, TOKENS, D), 1.0, 6.0, ((0, 4), (1, 8)))
    norm_gains = draw_norm_gains(jax.random.fold_in(key_list[10], 71), 0)
    w_query = normal_values(key_list[2], (SECTIONS, D, HEADS * HD), D ** -0.5, 0.125, ((0, 4), (2, 8)))
    w_keyval = normal_values(key_list[3], (SECTIONS, D, KV, 2 * HD), D ** -0.5, 0.125, ((0, 4), (1, 8)))
    w_out = normal_values(key_list[4], (SECTIONS, HEADS * HD, D), HD ** -0.5, 0.5, ((0, 4), (1, 8)))
    w_gate_up = normal_values(key_list[5], (SECTIONS, EXPERTS, D, 2 * FF), D ** -0.5, 0.125, ((0, 4), (1, 8)))
    w_down = normal_values(key_list[6], (SECTIONS, EXPERTS, FF, D), FF ** -0.5, 0.21875, ((0, 4), (1, 8)))
    expert_ids_keys = jax.random.split(jax.random.fold_in(key_list[7], 1), SECTIONS * TOKENS // TOK_DEV)
    expert_ids_turns = jax.random.permutation(jax.random.fold_in(key_list[7], 3), SECTIONS * TOKENS // TOK_DEV)
    expert_ids = jax.vmap(lambda own, number: shared_out(jax.random.fold_in(key_list[7], 2), own, number, TOK_DEV, EXPERTS, TOPK, CAP, 2))(expert_ids_keys, expert_ids_turns).reshape((SECTIONS, TOKENS, TOPK))
    gate_weights = jnp.clip(0.05 + 0.25 * jax.random.uniform(key_list[8], (SECTIONS, TOKENS, TOPK), jnp.float32) ** shard_levels(key_list[8], (SECTIONS, TOKENS, TOPK), ((0, 4), (1, 8)), -0.2, 0.2), 0.05, 0.3)
    segment_ids = jax.vmap(lambda own: jnp.searchsorted(jnp.cumsum(ragged_sizes(own, 16, TOKENS, TOKENS // 4, 2)), jnp.arange(TOKENS), side="right"))(jax.random.split(key_list[9], SECTIONS)).reshape((SECTIONS, TOKENS)).astype(jnp.int32)
    return dict(acts=acts, norm_gains=norm_gains, w_query=w_query, w_keyval=w_keyval, w_out=w_out, w_gate_up=w_gate_up, w_down=w_down, expert_ids=expert_ids, gate_weights=gate_weights, segment_ids=segment_ids)


EPS = 1e-06
ROPE_BASE = 1000000.0

def rms_scale(values, gain_row):
    mean_sq = lax.optimization_barrier(jnp.mean(values * values, axis=-1, keepdims=True))
    return values * lax.rsqrt(mean_sq + EPS) * gain_row

def rotate(values, positions):
    half_width = values.shape[-1] // 2
    frequency = ROPE_BASE ** (-jnp.arange(half_width, dtype=jnp.float32) * 2.0 / values.shape[-1])
    angles = positions[:, None] * frequency[None, :]
    cosines = jnp.cos(angles)[:, None, :]
    sine_table = jnp.sin(angles)[:, None, :]
    leading = values[..., :half_width]
    trailing = values[..., half_width:]
    return jnp.concatenate([leading * cosines - trailing * sine_table, trailing * cosines + leading * sine_table], axis=-1)

def section_layer(inputs, gains, w_query, w_keyval, w_out, w_gate_up, w_down, expert_ids, gate_weights, segment_ids):
    tokens = inputs.shape[0]
    x_wide = inputs.astype(jnp.float32)
    normed = rms_scale(x_wide, gains[0]).astype(jnp.bfloat16)
    positions = jnp.arange(tokens).astype(jnp.float32)
    queries = jnp.dot(normed, w_query, preferred_element_type=jnp.float32).reshape(tokens, HEADS, HD)
    queries = rotate(queries, positions).astype(jnp.bfloat16)
    keyval = jnp.dot(normed, w_keyval.reshape(D, KV * 2 * HD), preferred_element_type=jnp.float32).reshape(tokens, KV, 2 * HD)
    key_rows = rotate(keyval[:, :, :HD], positions).astype(jnp.bfloat16)
    value_rows = keyval[:, :, HD:].astype(jnp.bfloat16)
    token_order = jnp.arange(tokens)
    allowed = (segment_ids[:, None] == segment_ids[None, :]) & (token_order[None, :] <= token_order[:, None])
    group_size = HEADS // KV
    score_scale = 1.0 / math.sqrt(HD)
    queries_by_head = queries.transpose(1, 0, 2)
    keys_by_head = key_rows.transpose(1, 0, 2)
    values_by_head = value_rows.transpose(1, 0, 2)

    def one_head(head_pack):
        q_head, head_index = head_pack
        kv_index = head_index // group_size
        k_head = lax.dynamic_index_in_dim(keys_by_head, kv_index, 0, keepdims=False)
        v_head = lax.dynamic_index_in_dim(values_by_head, kv_index, 0, keepdims=False)
        scores = jnp.dot(q_head, k_head.T, preferred_element_type=jnp.float32) * score_scale
        scores = jnp.where(allowed, scores, -1e+30)
        row_max = lax.optimization_barrier(jnp.max(scores, axis=-1, keepdims=True))
        shifted = jnp.exp(scores - row_max)
        probability = (shifted / lax.optimization_barrier(jnp.sum(shifted, axis=-1, keepdims=True))).astype(jnp.bfloat16)
        return jnp.dot(probability, v_head, preferred_element_type=jnp.float32).astype(jnp.bfloat16)
    heads_out = lax.map(one_head, (queries_by_head, jnp.arange(HEADS).astype(jnp.int32)))

    def add_share(total, share_pair):
        head_part, weights = share_pair
        flat_heads = head_part.transpose(1, 0, 2).reshape(tokens, HEAD_DEV * HD)
        partial_value = jnp.dot(flat_heads, weights, preferred_element_type=jnp.float32).astype(jnp.bfloat16)
        partial_value = lax.optimization_barrier(partial_value)
        return (total + partial_value.astype(jnp.float32), None)
    attention, _ = lax.scan(add_share, jnp.zeros((tokens, D), jnp.float32), (heads_out.reshape(N_EXPERT, HEAD_DEV, tokens, HD), w_out.reshape(N_EXPERT, HEAD_DEV * HD, D)))
    middle = (x_wide + attention).astype(jnp.bfloat16)
    middle_wide = middle.astype(jnp.float32)
    mixer_in = rms_scale(middle_wide, gains[1]).astype(jnp.bfloat16)
    rows_dev = TOK_DEV * TOPK
    routes_flat = expert_ids.reshape(N_EXPERT, rows_dev)
    onehot = (routes_flat[:, :, None] == jnp.arange(EXPERTS, dtype=jnp.int32)[None, None, :]).astype(jnp.int32)
    earlier = jnp.cumsum(onehot, axis=1) - onehot
    slot_rank = lax.optimization_barrier(jnp.sum(earlier * onehot, axis=2))
    source = jnp.arange(N_EXPERT, dtype=jnp.int32)[:, None]
    slot_index = ((routes_flat * N_EXPERT + source) * CAP + slot_rank).reshape(-1)
    routed = jnp.repeat(mixer_in, TOPK, axis=0)
    buffer = jnp.zeros((EXPERTS * N_EXPERT * CAP, D), jnp.bfloat16).at[slot_index].set(routed)
    buffer = buffer.reshape(EXPERTS, N_EXPERT * CAP, D)

    def run_expert(expert_pack):
        slot_rows, gate_up, down_proj = expert_pack
        gate_up_out = jnp.dot(slot_rows, gate_up, preferred_element_type=jnp.float32)
        hidden = (jax.nn.silu(gate_up_out[:, :FF]) * gate_up_out[:, FF:]).astype(jnp.bfloat16)
        return jnp.dot(hidden, down_proj, preferred_element_type=jnp.float32).astype(jnp.bfloat16)
    outputs = lax.map(run_expert, (buffer, w_gate_up, w_down))
    picked = outputs.reshape(-1, D)[slot_index].astype(jnp.float32).reshape(tokens, TOPK, D)
    mixed = lax.optimization_barrier(jnp.sum(picked * gate_weights[:, :, None], axis=1))
    return (middle_wide + mixed).astype(jnp.bfloat16)

def reference(acts, norm_gains, w_query, w_keyval, w_out, w_gate_up, w_down, expert_ids, gate_weights, segment_ids):
    results = []
    for section_index in range(acts.shape[0]):
        results.append(section_layer(acts[section_index], norm_gains[section_index], w_query[section_index], w_keyval[section_index], w_out[section_index], w_gate_up[section_index], w_down[section_index], expert_ids[section_index], gate_weights[section_index], segment_ids[section_index]))
    return jnp.roll(jnp.stack(results), 1, axis=0)
```

```python
import math

import jax
import jax.numpy as jnp
from jax import lax
from jax.experimental import pallas as pl
from jax.experimental.pallas import tpu as pltpu
from jax.sharding import PartitionSpec as P

MESH = pl.DeviceIdType.MESH

HD = 128
KV = 4
EXPERTS = 32
TOPK = 8
CAP = 24


EPS = 1e-06
ROPE_BASE = 1000000.0


def shifted_2(x, axis, by):
    length = lax.axis_size(axis)
    return lax.ppermute(x, axis, [(i, (i + by) % length) for i in range(length)])


def rms_scale(values, gain_row):
    mean_sq = jnp.mean(values * values, axis=-1, keepdims=True)
    return values * lax.rsqrt(mean_sq + EPS) * gain_row


def rotate(values, positions):
    half_width = values.shape[-1] // 2
    frequency = ROPE_BASE ** (-jnp.arange(half_width, dtype=jnp.float32) * 2.0 / values.shape[-1])
    angles = positions[:, None] * frequency[None, :]
    cosines = jnp.cos(angles)[:, None, :]
    sine_table = jnp.sin(angles)[:, None, :]
    leading = values[..., :half_width]
    trailing = values[..., half_width:]
    return jnp.concatenate(
        [leading * cosines - trailing * sine_table, trailing * cosines + leading * sine_table],
        axis=-1,
    )


def head_block(q_block, key_rows, value_rows, seg_block, seg_all, pos_block, pos_all, score_scale):
    scores = (
        jnp.einsum("qhd,kd->hqk", q_block, key_rows, preferred_element_type=jnp.float32)
        * score_scale
    )
    allowed = (seg_block[:, None] == seg_all[None, :]) & (pos_all[None, :] <= pos_block[:, None])
    scores = jnp.where(allowed[None], scores, -1e30)
    row_max = jnp.max(scores, axis=-1, keepdims=True)
    shifted = jnp.exp(scores - row_max)
    probability = (shifted / jnp.sum(shifted, axis=-1, keepdims=True)).astype(jnp.bfloat16)
    return jnp.einsum(
        "hqk,kd->qhd", probability, value_rows, preferred_element_type=jnp.float32
    ).astype(jnp.bfloat16)


def expert_rows(grouped, gate_up, down_proj):
    gate_up_out = jnp.einsum("necd,edf->necf", grouped, gate_up, preferred_element_type=jnp.float32)
    half_width = down_proj.shape[1]
    hidden = (jax.nn.silu(gate_up_out[..., :half_width]) * gate_up_out[..., half_width:]).astype(
        jnp.bfloat16
    )
    return jnp.einsum(
        "necf,efd->necd", hidden, down_proj, preferred_element_type=jnp.float32
    ).astype(jnp.bfloat16)


def send_back(results):
    return lax.all_to_all(results, "expert", split_axis=0, concat_axis=0, tiled=True)


def per_device_general(
    acts,
    norm_gains,
    w_query,
    w_keyval,
    w_out,
    w_gate_up,
    w_down,
    expert_ids,
    gate_weights,
    segment_ids,
):
    device_count = lax.axis_size("expert")
    my_index = lax.axis_index("expert")
    tok_rows = acts.shape[1]
    width = acts.shape[2]
    head_dev = w_query.shape[2] // HD
    local_experts = w_gate_up.shape[1]
    heads_total = head_dev * device_count
    gains = norm_gains[0]
    x_wide = acts[0].astype(jnp.float32)
    normed = rms_scale(x_wide, gains[0]).astype(jnp.bfloat16)
    kv_index = my_index * head_dev // (heads_total // KV)
    query_weight = w_query[0]
    gathered_keyval = lax.all_gather(w_keyval[0], "expert", axis=0, tiled=True)
    head_keyval = lax.dynamic_index_in_dim(gathered_keyval, kv_index, 1, keepdims=False)
    row_piece = lax.all_gather(normed, "expert", axis=0, tiled=True)
    piece_rows = row_piece.shape[0]
    positions = jnp.arange(piece_rows).astype(jnp.float32)
    query_piece_rows = row_piece.shape[0]
    query_positions = jnp.arange(query_piece_rows).astype(jnp.float32)
    queries = jnp.dot(row_piece, query_weight, preferred_element_type=jnp.float32).reshape(
        query_piece_rows, head_dev, HD
    )
    queries = (
        rotate(queries, query_positions)
        .astype(jnp.bfloat16)
        .reshape(query_piece_rows, head_dev * HD)
    )
    keyval = jnp.dot(row_piece, head_keyval, preferred_element_type=jnp.float32)
    key_rows = rotate(keyval[:, None, :HD], positions).astype(jnp.bfloat16).reshape(piece_rows, HD)
    value_rows = keyval[:, HD:].astype(jnp.bfloat16)
    projected = jnp.concatenate([queries, key_rows, value_rows], axis=1)
    tokens = projected.shape[0]
    all_queries = projected[:, : head_dev * HD].reshape(tokens, head_dev, HD)
    all_keys = projected[:, head_dev * HD : (head_dev + 1) * HD]
    all_values = projected[:, (head_dev + 1) * HD :]
    segments = segment_ids[0]
    all_positions = jnp.arange(tokens)
    q_rows = min(512, tokens)
    score_scale = 1.0 / math.sqrt(HD)

    def attend(first_row):
        q_block = lax.dynamic_slice_in_dim(all_queries, first_row, q_rows, 0)
        seg_block = lax.dynamic_slice_in_dim(segments, first_row, q_rows, 0)
        pos_block = first_row + jnp.arange(q_rows)
        return head_block(
            q_block,
            all_keys,
            all_values,
            seg_block,
            segments,
            pos_block,
            all_positions,
            score_scale,
        )

    block_starts = jnp.arange(tokens // q_rows) * q_rows
    attended = lax.map(attend, block_starts).reshape(tokens, head_dev * HD)
    out_weight = w_out[0]
    attention = lax.psum_scatter(
        jnp.dot(attended, out_weight, preferred_element_type=jnp.float32).astype(jnp.bfloat16),
        "expert",
        scatter_dimension=0,
        tiled=True,
    ).astype(jnp.float32)
    middle_wide = (x_wide + attention).astype(jnp.bfloat16).astype(jnp.float32)
    mixer_in = rms_scale(middle_wide, gains[1]).astype(jnp.bfloat16)
    routes_flat = expert_ids[0].reshape(-1)
    onehot = routes_flat[:, None] == jnp.arange(EXPERTS, dtype=jnp.int32)[None, :]
    order = jnp.arange(routes_flat.shape[0])
    below = (order[None, :] < order[:, None]).astype(jnp.bfloat16)
    earlier = jnp.dot(below, onehot.astype(jnp.bfloat16), preferred_element_type=jnp.float32)
    slot_rank = jnp.sum(jnp.where(onehot, earlier, 0.0), axis=1).astype(jnp.int32)
    slot_index = routes_flat * CAP + slot_rank
    routed = jnp.repeat(mixer_in, TOPK, axis=0)
    send_rows = (
        jnp.zeros((EXPERTS * CAP, width), jnp.bfloat16)
        .at[slot_index]
        .set(routed)
        .reshape(EXPERTS, CAP, width)
    )
    gate_up = w_gate_up[0]
    down_proj = w_down[0]
    received = lax.all_to_all(send_rows, "expert", split_axis=0, concat_axis=0, tiled=True)
    source_count = received.shape[0] // local_experts
    grouped = received.reshape(source_count, local_experts, received.shape[1], width)
    outputs = expert_rows(grouped, gate_up, down_proj)
    returned = send_back(outputs.reshape(received.shape))
    picked = (
        returned.reshape(EXPERTS * CAP, width)[slot_index]
        .astype(jnp.float32)
        .reshape(tok_rows, TOPK, width)
    )
    mixed = jnp.sum(picked * gate_weights[0][:, :, None], axis=1)
    result = (middle_wide + mixed).astype(jnp.bfloat16)
    handed = shifted_2(result, "section", 1)
    return handed[None]


LINE = 4
GROUP = 8
PARTS = 2


def greet(section_too):
    section, me = lax.axis_index("section"), lax.axis_index("expert")
    barrier = pltpu.get_barrier_semaphore()
    for step in range(1, GROUP):
        other = lax.rem(me + step, GROUP)
        pl.semaphore_signal(barrier, inc=1, device_id=(section, other), device_id_type=MESH)
    count = GROUP - 1
    if section_too:
        sections = lax.axis_size("section")
        for step in (1, sections - 1):
            other = lax.rem(section + step, sections)
            pl.semaphore_signal(barrier, inc=1, device_id=(other, me), device_id_type=MESH)
        count += 2
    pl.semaphore_wait(barrier, count)


LINE_ORDER = ((3, 2, 1, 0), (3, 0, 2, 1), (0, 3, 1, 2), (0, 1, 2, 3))


def scatter_line(z, terms, from_pair, from_below, from_above, outgoing, pair_send, pair_recv,
                 line_send, below_recv, above_recv, ready):
    section, me = lax.axis_index("section"), lax.axis_index("expert")
    x = lax.rem(me, 2)
    own = z * 2 + x
    partner = z * 2 + 1 - x
    order = [(place, part) for place in LINE_ORDER[z] for part in range(PARTS)]
    pair_copies = {
        (place, part): remote(
            terms.at[place * 2 + 1 - x, part], from_pair.at[place, part],
            pair_send.at[place, part], pair_recv.at[place, part], partner,
        )
        for place, part in order
    }
    for item in order:
        pair_copies[item].start()

    def line_copy(place, part, up):
        landing, sems = (from_below, below_recv) if up else (from_above, above_recv)
        return remote(
            outgoing.at[place, part], landing.at[place, part], line_send.at[place, part],
            sems.at[place, part], own + 2 if up else own - 2,
        )

    sent = []
    for place, part in order:
        pair_copies[place, part].wait_recv()
        pieces = [from_pair.at[place, part]]
        if place >= z and z > 0:
            line_copy(place, part, True).wait_recv()
            pieces.append(from_below.at[place, part])
        if place <= z and z < LINE - 1:
            line_copy(place, part, False).wait_recv()
            pieces.append(from_above.at[place, part])
        value = terms[place * 2 + x, part].astype(jnp.float32)
        for piece in pieces:
            value = value + piece[...].astype(jnp.float32)
        if place == z:
            ready(part, value)
        else:
            outgoing[place, part] = value.astype(jnp.bfloat16)
            out = line_copy(place, part, place > z)
            out.start()
            sent.append(out)
    return list(pair_copies.values()) + sent


def scatter_scratch(rows, width):
    slots = pltpu.VMEM((LINE, PARTS, rows // PARTS, width), jnp.bfloat16)
    sems = pltpu.SemaphoreType.DMA((LINE, PARTS))
    return [slots] * 4 + [sems] * 5


def remote(src, dst, send_sem, recv_sem, expert, section=None):
    if section is None:
        section = lax.axis_index("section")
    return pltpu.make_async_remote_copy(
        src_ref=src,
        dst_ref=dst,
        send_sem=send_sem,
        recv_sem=recv_sem,
        device_id=(section, expert),
        device_id_type=MESH,
    )


def at_place(body):
    me = lax.axis_index("expert")
    x = lax.rem(me, 2)
    for z in range(LINE):

        @pl.when(me // 2 == z)
        def _(z=z):
            body(z, x, z * 2 + x, z * 2 + 1 - x)


class Gather:
    def __init__(self, rows, send_sems, recv_sems):
        self.rows, self.send_sems, self.recv_sems = rows, send_sems, recv_sems

    def copy(self, chunk, shard, to, way):
        return remote(
            self.rows.at[shard, chunk], self.rows.at[shard, chunk],
            self.send_sems.at[chunk, shard, way], self.recv_sems.at[chunk, shard], to,
        )

    def first(self, chunk, z, own, partner):
        out = []
        if z < LINE - 1:
            out.append(self.copy(chunk, own, own + 2, 0))
        if z > 0:
            out.append(self.copy(chunk, own, own - 2, 1))
        return out + [self.copy(chunk, own, partner, 2)]

    def passing(self, chunk, z, x, own, partner):
        out = []
        for far in range(1, LINE):
            if z - far >= 0:
                shard = (z - far) * 2 + x
                onward = [self.copy(chunk, shard, own + 2, 0)] if z < LINE - 1 else []
                out.append((shard, onward + [self.copy(chunk, shard, partner, 2)]))
            if z + far < LINE:
                shard = (z + far) * 2 + x
                onward = [self.copy(chunk, shard, own - 2, 1)] if z > 0 else []
                out.append((shard, onward + [self.copy(chunk, shard, partner, 2)]))
        return out

    def start(self, chunk, z, x, own, partner):
        for out in self.first(chunk, z, own, partner):
            out.start()

    def forward(self, chunk, z, x, own, partner):
        for shard, onward in self.passing(chunk, z, x, own, partner):
            self.copy(chunk, shard, partner, 2).wait_recv()
            for out in onward:
                out.start()

    def arrive(self, chunk, z, x, own, partner):
        for place in range(LINE):
            self.copy(chunk, place * 2 + 1 - x, partner, 2).wait_recv()

    def drain(self, chunk, z, x, own, partner):
        for out in self.first(chunk, z, own, partner):
            out.wait_send()
        for _, onward in self.passing(chunk, z, x, own, partner):
            for out in onward:
                out.wait_send()


def opening_kernel(acts, gains, keyval, gates, rows, weights, all_gates,
                   send_sems, recv_sems, keyval_send, keyval_recv, pass_send, gate_send,
                   gate_recv, local_sem):
    section, me = lax.axis_index("section"), lax.axis_index("expert")
    for part in range(PARTS):
        rows[me, part] = rms_scale(acts[part].astype(jnp.float32), gains[0:1, :]).astype(
            jnp.bfloat16
        )
    greet(False)
    gather = Gather(rows, send_sems, recv_sems)
    own_gates = pltpu.make_async_copy(gates.at[me], all_gates.at[me], local_sem.at[1])
    own_weights = pltpu.make_async_copy(keyval.at[me // 2], weights.at[me], local_sem.at[0])
    gate_copies = []
    for step in range(1, GROUP):
        other = lax.rem(me + step, GROUP)
        gate_copies.append(
            remote(gates.at[other], all_gates.at[me], gate_send.at[step], gate_recv.at[step], other)
        )

    def line_weights(place, z, own):
        return remote(
            keyval.at[place], weights.at[own], keyval_send.at[place], keyval_recv.at[own],
            own + 2 * (place - z),
        )

    def pass_weights(place, z, x, partner):
        shard = place * 2 + x
        source = keyval.at[z] if place == z else weights.at[shard]
        return remote(source, weights.at[shard], pass_send.at[place], keyval_recv.at[shard], partner)

    def begin(z, x, own, partner):
        for part in range(PARTS):
            gather.start(part, z, x, own, partner)
        for place in LINE_ORDER[z]:
            if place != z:
                line_weights(place, z, own).start()
        pass_weights(z, z, x, partner).start()

    def through(z, x, own, partner):
        nearest = sorted((p for p in range(LINE) if p != z), key=lambda p: abs(p - z))
        hops = [gather.passing(part, z, x, own, partner) for part in range(PARTS)]
        for place, *arrivals in zip(nearest, *hops):
            for part, (shard, onward) in enumerate(arrivals):
                gather.copy(part, shard, partner, 2).wait_recv()
                for out in onward:
                    out.start()
            source = place * 2 + x
            remote(
                weights.at[source], weights.at[source], pass_send.at[place],
                keyval_recv.at[source], partner,
            ).wait_recv()
            pass_weights(place, z, x, partner).start()
        for part in range(PARTS):
            gather.arrive(part, z, x, own, partner)
        for place in range(LINE):
            source = place * 2 + 1 - x
            remote(
                weights.at[source], weights.at[source], pass_send.at[place],
                keyval_recv.at[source], partner,
            ).wait_recv()
        for part in range(PARTS):
            gather.drain(part, z, x, own, partner)
        for place in range(LINE):
            if place != z:
                line_weights(place, z, own).wait_send()
            pass_weights(place, z, x, partner).wait_send()

    at_place(begin)
    own_weights.start()
    own_gates.start()
    for out in gate_copies:
        out.start()
    at_place(through)
    for out in gate_copies:
        out.wait_recv()
    for out in gate_copies:
        out.wait_send()
    own_weights.wait()
    own_gates.wait()


def turning_kernel(terms, acts, gains, rows, middle,
                   from_pair, from_below, from_above, outgoing, pair_send, pair_recv,
                   line_send, below_recv, above_recv, send_sems, recv_sems):
    me = lax.axis_index("expert")
    greet(False)
    gather = Gather(rows, send_sems, recv_sems)

    def body(z, x, own, partner):
        def ready(part, total):
            joined = (acts[part].astype(jnp.float32) + total).astype(jnp.bfloat16)
            middle[part] = joined
            rows[me, part] = rms_scale(joined.astype(jnp.float32), gains[1:2, :]).astype(
                jnp.bfloat16
            )
            gather.start(part, z, x, own, partner)

        sent = scatter_line(z, terms, from_pair, from_below, from_above, outgoing, pair_send,
                            pair_recv, line_send, below_recv, above_recv, ready)
        for arrivals in zip(*(gather.passing(p, z, x, own, partner) for p in range(PARTS))):
            for part, (shard, onward) in enumerate(arrivals):
                gather.copy(part, shard, partner, 2).wait_recv()
                for out in onward:
                    out.start()
        for part in range(PARTS):
            gather.arrive(part, z, x, own, partner)
        for part in range(PARTS):
            gather.drain(part, z, x, own, partner)
        for out in sent:
            out.wait_send()

    at_place(body)


def closing_kernel(terms, middle, handed,
                   from_pair, from_below, from_above, outgoing, pair_send, pair_recv,
                   line_send, below_recv, above_recv, result, hand_send, hand_recv):
    section, me = lax.axis_index("section"), lax.axis_index("expert")
    greet(True)

    def hand(part):
        return remote(
            result.at[part], handed.at[part], hand_send.at[part], hand_recv.at[part],
            me, lax.rem(section + 1, lax.axis_size("section")),
        )

    def ready(part, total):
        result[part] = (middle[part].astype(jnp.float32) + total).astype(jnp.bfloat16)
        hand(part).start()

    def body(z, x, own, partner):
        sent = scatter_line(z, terms, from_pair, from_below, from_above, outgoing, pair_send,
                            pair_recv, line_send, below_recv, above_recv, ready)
        for out in sent:
            out.wait_send()

    at_place(body)
    for part in range(PARTS):
        hand(part).wait()


def in_vmem(count):
    return [pl.BlockSpec(memory_space=pltpu.VMEM)] * count


def remote_params(collective_id, mebibytes):
    return pltpu.CompilerParams(
        collective_id=collective_id, has_side_effects=True, vmem_limit_bytes=mebibytes << 20
    )


def per_device(
    acts,
    norm_gains,
    w_query,
    w_keyval,
    w_out,
    w_gate_up,
    w_down,
    expert_ids,
    gate_weights,
    segment_ids,
):
    tok_rows, width = acts.shape[1:]
    head_dev = w_query.shape[2] // HD
    local_experts = w_gate_up.shape[1]
    gains = norm_gains[0]
    own_acts = acts[0].reshape(PARTS, tok_rows // PARTS, width)
    tokens = tok_rows * GROUP
    keyval = w_keyval[0].transpose(1, 0, 2)
    keyval_rows = keyval.shape[1]
    named = expert_ids[0][:, :, None] == jnp.arange(EXPERTS, dtype=jnp.int32)[None, None, :]
    dense_gates = jnp.sum(jnp.where(named, gate_weights[0][:, :, None], 0.0), axis=1)
    dense_gates = dense_gates.T.reshape(GROUP, local_experts, tok_rows)
    dma = pltpu.SemaphoreType.DMA
    row_piece, head_keyval, all_gates = pl.pallas_call(
        opening_kernel,
        out_shape=[
            jax.ShapeDtypeStruct((GROUP, PARTS, tok_rows // PARTS, width), jnp.bfloat16),
            jax.ShapeDtypeStruct((GROUP, keyval_rows, 2 * HD), jnp.bfloat16),
            jax.ShapeDtypeStruct(dense_gates.shape, jnp.float32),
        ],
        in_specs=in_vmem(4),
        out_specs=in_vmem(3),
        scratch_shapes=[
            dma((PARTS, GROUP, 3)), dma((PARTS, GROUP)), dma((LINE,)), dma((GROUP,)), dma((LINE,)),
            dma((GROUP,)), dma((GROUP,)), dma((2,)),
        ],
        compiler_params=remote_params(0, 8),
    )(own_acts, gains, keyval, dense_gates)
    row_piece = row_piece.reshape(tokens, width)
    head_keyval = head_keyval.reshape(width, 2 * HD)

    positions = jnp.arange(tokens).astype(jnp.float32)
    queries = jnp.dot(row_piece, w_query[0], preferred_element_type=jnp.float32)
    queries = rotate(queries.reshape(tokens, head_dev, HD), positions).astype(jnp.bfloat16)
    keyval_out = jnp.dot(row_piece, head_keyval, preferred_element_type=jnp.float32)
    key_rows = rotate(keyval_out[:, None, :HD], positions).astype(jnp.bfloat16).reshape(tokens, HD)
    value_rows = keyval_out[:, HD:].astype(jnp.bfloat16)
    segments = segment_ids[0]
    token_order = jnp.arange(tokens)
    attended = head_block(
        queries, key_rows, value_rows, segments, segments, token_order, token_order,
        1.0 / math.sqrt(HD),
    ).reshape(tokens, head_dev * HD)
    terms = jnp.dot(attended, w_out[0], preferred_element_type=jnp.float32).astype(jnp.bfloat16)
    mixer_rows, middle = pl.pallas_call(
        turning_kernel,
        out_shape=[
            jax.ShapeDtypeStruct((GROUP, PARTS, tok_rows // PARTS, width), jnp.bfloat16),
            jax.ShapeDtypeStruct(own_acts.shape, jnp.bfloat16),
        ],
        in_specs=in_vmem(3),
        out_specs=in_vmem(2),
        scratch_shapes=scatter_scratch(tok_rows, width) + [dma((PARTS, GROUP, 3)), dma((PARTS, GROUP))],
        compiler_params=remote_params(1, 12),
    )(terms.reshape(GROUP, PARTS, tok_rows // PARTS, width), own_acts, gains)
    mixer_rows = mixer_rows.reshape(tokens, width)

    gates = all_gates.transpose(1, 0, 2).reshape(local_experts, tokens)
    member = gates > 0
    before = (token_order[:, None] < token_order[None, :]).astype(jnp.bfloat16)
    rank = jnp.dot(member.astype(jnp.bfloat16), before, preferred_element_type=jnp.float32)
    slots = GROUP * CAP
    slot_of = jnp.where(member, rank.astype(jnp.int32), -1)
    places = jnp.arange(slots, dtype=jnp.int32)
    chosen = slot_of[:, None, :] == places[None, :, None]
    slot_gates = jnp.sum(jnp.where(chosen, gates[:, None, :], 0.0), axis=2)
    chosen = chosen.astype(jnp.bfloat16)
    grouped = jnp.einsum(
        "est,td->esd", chosen, mixer_rows, preferred_element_type=jnp.float32
    ).astype(jnp.bfloat16)
    gate_up_out = jnp.einsum(
        "esd,edf->esf", grouped, w_gate_up[0], preferred_element_type=jnp.float32
    )
    ff = w_down.shape[2]
    hidden = (jax.nn.silu(gate_up_out[..., :ff]) * gate_up_out[..., ff:]).astype(jnp.bfloat16)
    outputs = jnp.einsum("esf,efd->esd", hidden, w_down[0], preferred_element_type=jnp.float32)
    outputs = (outputs * slot_gates[:, :, None]).astype(jnp.bfloat16)
    mixed = jnp.dot(
        chosen.reshape(local_experts * slots, tokens).T,
        outputs.reshape(local_experts * slots, width),
        preferred_element_type=jnp.float32,
    ).astype(jnp.bfloat16)

    handed = pl.pallas_call(
        closing_kernel,
        out_shape=jax.ShapeDtypeStruct(own_acts.shape, jnp.bfloat16),
        in_specs=in_vmem(2),
        out_specs=pl.BlockSpec(memory_space=pltpu.VMEM),
        scratch_shapes=scatter_scratch(tok_rows, width)
        + [pltpu.VMEM(own_acts.shape, jnp.bfloat16), dma((PARTS,)), dma((PARTS,))],
        compiler_params=remote_params(2, 10),
    )(mixed.reshape(GROUP, PARTS, tok_rows // PARTS, width), middle)
    return handed.reshape(1, tok_rows, width)


def solution(mesh):
    placed = (
        P("section", "expert", None),
        P("section", None, None),
        P("section", None, "expert"),
        P("section", "expert", None, None),
        P("section", "expert", None),
        P("section", "expert", None, None),
        P("section", "expert", None, None),
        P("section", "expert", None),
        P("section", "expert", None),
        P("section", None),
    )
    return jax.shard_map(
        per_device if mesh.shape["expert"] == GROUP else per_device_general,
        mesh=mesh,
        in_specs=placed,
        out_specs=P("section", "expert", None),
        check_vma=False,
    )
```

```python
import functools
import math

import jax
import jax.numpy as jnp
import numpy as np
from jax import lax
from jax.experimental import pallas as pl
from jax.experimental.pallas import tpu as pltpu
from jax.sharding import PartitionSpec as P

MESH = pl.DeviceIdType.MESH

HD = 128
KV = 4
EXPERTS = 32
TOPK = 8
CAP = 24


EPS = 1e-06
ROPE_BASE = 1000000.0


def shifted_2(x, axis, by):
    length = lax.axis_size(axis)
    return lax.ppermute(x, axis, [(i, (i + by) % length) for i in range(length)])


def rms_scale(values, gain_row):
    mean_sq = jnp.mean(values * values, axis=-1, keepdims=True)
    return values * lax.rsqrt(mean_sq + EPS) * gain_row


def rotate(values, positions):
    half_width = values.shape[-1] // 2
    frequency = ROPE_BASE ** (-jnp.arange(half_width, dtype=jnp.float32) * 2.0 / values.shape[-1])
    angles = positions[:, None] * frequency[None, :]
    cosines = jnp.cos(angles)[:, None, :]
    sine_table = jnp.sin(angles)[:, None, :]
    leading = values[..., :half_width]
    trailing = values[..., half_width:]
    return jnp.concatenate(
        [leading * cosines - trailing * sine_table, trailing * cosines + leading * sine_table],
        axis=-1,
    )


def head_block(q_block, key_rows, value_rows, seg_block, seg_all, pos_block, pos_all, score_scale):
    scores = (
        jnp.einsum("qhd,kd->hqk", q_block, key_rows, preferred_element_type=jnp.float32)
        * score_scale
    )
    allowed = (seg_block[:, None] == seg_all[None, :]) & (pos_all[None, :] <= pos_block[:, None])
    scores = jnp.where(allowed[None], scores, -1e30)
    row_max = jnp.max(scores, axis=-1, keepdims=True)
    shifted = jnp.exp(scores - row_max)
    probability = (shifted / jnp.sum(shifted, axis=-1, keepdims=True)).astype(jnp.bfloat16)
    return jnp.einsum(
        "hqk,kd->qhd", probability, value_rows, preferred_element_type=jnp.float32
    ).astype(jnp.bfloat16)


def expert_rows(grouped, gate_up, down_proj):
    gate_up_out = jnp.einsum("necd,edf->necf", grouped, gate_up, preferred_element_type=jnp.float32)
    half_width = down_proj.shape[1]
    hidden = (jax.nn.silu(gate_up_out[..., :half_width]) * gate_up_out[..., half_width:]).astype(
        jnp.bfloat16
    )
    return jnp.einsum(
        "necf,efd->necd", hidden, down_proj, preferred_element_type=jnp.float32
    ).astype(jnp.bfloat16)


def send_back(results):
    return lax.all_to_all(results, "expert", split_axis=0, concat_axis=0, tiled=True)


def per_device_general(
    acts,
    norm_gains,
    w_query,
    w_keyval,
    w_out,
    w_gate_up,
    w_down,
    expert_ids,
    gate_weights,
    segment_ids,
):
    device_count = lax.axis_size("expert")
    my_index = lax.axis_index("expert")
    tok_rows = acts.shape[1]
    width = acts.shape[2]
    head_dev = w_query.shape[2] // HD
    local_experts = w_gate_up.shape[1]
    heads_total = head_dev * device_count
    gains = norm_gains[0]
    x_wide = acts[0].astype(jnp.float32)
    normed = rms_scale(x_wide, gains[0]).astype(jnp.bfloat16)
    kv_index = my_index * head_dev // (heads_total // KV)
    query_weight = w_query[0]
    gathered_keyval = lax.all_gather(w_keyval[0], "expert", axis=0, tiled=True)
    head_keyval = lax.dynamic_index_in_dim(gathered_keyval, kv_index, 1, keepdims=False)
    row_piece = lax.all_gather(normed, "expert", axis=0, tiled=True)
    piece_rows = row_piece.shape[0]
    positions = jnp.arange(piece_rows).astype(jnp.float32)
    query_piece_rows = row_piece.shape[0]
    query_positions = jnp.arange(query_piece_rows).astype(jnp.float32)
    queries = jnp.dot(row_piece, query_weight, preferred_element_type=jnp.float32).reshape(
        query_piece_rows, head_dev, HD
    )
    queries = (
        rotate(queries, query_positions)
        .astype(jnp.bfloat16)
        .reshape(query_piece_rows, head_dev * HD)
    )
    keyval = jnp.dot(row_piece, head_keyval, preferred_element_type=jnp.float32)
    key_rows = rotate(keyval[:, None, :HD], positions).astype(jnp.bfloat16).reshape(piece_rows, HD)
    value_rows = keyval[:, HD:].astype(jnp.bfloat16)
    projected = jnp.concatenate([queries, key_rows, value_rows], axis=1)
    tokens = projected.shape[0]
    all_queries = projected[:, : head_dev * HD].reshape(tokens, head_dev, HD)
    all_keys = projected[:, head_dev * HD : (head_dev + 1) * HD]
    all_values = projected[:, (head_dev + 1) * HD :]
    segments = segment_ids[0]
    all_positions = jnp.arange(tokens)
    q_rows = min(512, tokens)
    score_scale = 1.0 / math.sqrt(HD)

    def attend(first_row):
        q_block = lax.dynamic_slice_in_dim(all_queries, first_row, q_rows, 0)
        seg_block = lax.dynamic_slice_in_dim(segments, first_row, q_rows, 0)
        pos_block = first_row + jnp.arange(q_rows)
        return head_block(
            q_block,
            all_keys,
            all_values,
            seg_block,
            segments,
            pos_block,
            all_positions,
            score_scale,
        )

    block_starts = jnp.arange(tokens // q_rows) * q_rows
    attended = lax.map(attend, block_starts).reshape(tokens, head_dev * HD)
    out_weight = w_out[0]
    attention = lax.psum_scatter(
        jnp.dot(attended, out_weight, preferred_element_type=jnp.float32).astype(jnp.bfloat16),
        "expert",
        scatter_dimension=0,
        tiled=True,
    ).astype(jnp.float32)
    middle_wide = (x_wide + attention).astype(jnp.bfloat16).astype(jnp.float32)
    mixer_in = rms_scale(middle_wide, gains[1]).astype(jnp.bfloat16)
    routes_flat = expert_ids[0].reshape(-1)
    onehot = routes_flat[:, None] == jnp.arange(EXPERTS, dtype=jnp.int32)[None, :]
    order = jnp.arange(routes_flat.shape[0])
    below = (order[None, :] < order[:, None]).astype(jnp.bfloat16)
    earlier = jnp.dot(below, onehot.astype(jnp.bfloat16), preferred_element_type=jnp.float32)
    slot_rank = jnp.sum(jnp.where(onehot, earlier, 0.0), axis=1).astype(jnp.int32)
    slot_index = routes_flat * CAP + slot_rank
    routed = jnp.repeat(mixer_in, TOPK, axis=0)
    send_rows = (
        jnp.zeros((EXPERTS * CAP, width), jnp.bfloat16)
        .at[slot_index]
        .set(routed)
        .reshape(EXPERTS, CAP, width)
    )
    gate_up = w_gate_up[0]
    down_proj = w_down[0]
    received = lax.all_to_all(send_rows, "expert", split_axis=0, concat_axis=0, tiled=True)
    source_count = received.shape[0] // local_experts
    grouped = received.reshape(source_count, local_experts, received.shape[1], width)
    outputs = expert_rows(grouped, gate_up, down_proj)
    returned = send_back(outputs.reshape(received.shape))
    picked = (
        returned.reshape(EXPERTS * CAP, width)[slot_index]
        .astype(jnp.float32)
        .reshape(tok_rows, TOPK, width)
    )
    mixed = jnp.sum(picked * gate_weights[0][:, :, None], axis=1)
    result = (middle_wide + mixed).astype(jnp.bfloat16)
    handed = shifted_2(result, "section", 1)
    return handed[None]


LINE = 4
GROUP = 8
SIDES = 2
PIECES = 4
VMEM_MIB = 62
BF16 = jnp.bfloat16
F32 = jnp.float32


def remote(src, dst, send_sem, recv_sem, expert, section=None):
    if section is None:
        section = lax.axis_index("section")
    return pltpu.make_async_remote_copy(
        src_ref=src,
        dst_ref=dst,
        send_sem=send_sem,
        recv_sem=recv_sem,
        device_id=(section, expert),
        device_id_type=MESH,
    )


class Refs:
    def __init__(self, names, refs):
        for name, ref in zip(names, refs, strict=True):
            setattr(self, name, ref)


ARGS = (
    "acts", "gains", "ids", "gates", "segs", "table", "w_query", "keyval", "w_out", "w_gate_up",
    "w_down", "handed",
)


def scratch_of(tok_rows, width, kv_rows, local_experts, ff):
    piece = width // PIECES
    slots = LINE * CAP
    vmem, dma = pltpu.VMEM, pltpu.SemaphoreType.DMA
    return {
        "acts_v": vmem((tok_rows, width), BF16),
        "gains_v": vmem((2, width), F32),
        "ids_v": vmem((TOPK, tok_rows), jnp.int32),
        "gates_v": vmem((TOPK, tok_rows), F32),
        "segs_v": vmem((1, tok_rows * GROUP), jnp.int32),
        "table_v": vmem((2, GROUP, tok_rows, HD), F32),
        "wide_ids": vmem((TOPK, 128), jnp.int32),
        "wide_gates": vmem((TOPK, 128), F32),
        "own_gates": vmem((GROUP, local_experts, 128), F32),
        "all_gates": vmem((GROUP, local_experts, 128), F32),
        "allowed": vmem((LINE, tok_rows, 4 * tok_rows), F32),
        "rows": vmem((LINE, tok_rows, width), BF16),
        "kv_weights": vmem((GROUP, kv_rows, 2 * HD), BF16),
        "q_weights": vmem((SIDES, width, HD), BF16),
        "out_weights": vmem((SIDES, HD, width), BF16),
        "queries": vmem((LINE, SIDES, tok_rows, HD), BF16),
        "key_values": vmem((GROUP, tok_rows, 2 * HD), BF16),
        "attended": vmem((LINE, tok_rows, SIDES * HD), BF16),
        "terms": vmem((PIECES, LINE, tok_rows, piece), BF16),
        "landed": vmem((PIECES, LINE + 1, tok_rows, piece), BF16),
        "total": vmem((tok_rows, piece), F32),
        "middle": vmem((PIECES, tok_rows, piece), BF16),
        "mixer": vmem((PIECES, SIDES, LINE, tok_rows, piece), BF16),
        "select": vmem((SIDES, local_experts * slots, LINE * tok_rows), BF16),
        "spread": vmem((SIDES, LINE * tok_rows, local_experts * slots), BF16),
        "slot_gates": vmem((local_experts, SIDES * slots, 1), F32),
        "squares": vmem((local_experts, SIDES * slots, 1), F32),
        "grouped": vmem((local_experts, SIDES * slots, piece), BF16),
        "sums": vmem((local_experts, SIDES * slots, 2 * ff), F32),
        "hidden": vmem((local_experts, SIDES * slots, ff), BF16),
        "outputs": vmem((SIDES, local_experts, slots, piece), BF16),
        "shares": vmem((PIECES, SIDES, LINE, tok_rows, piece), BF16),
        "paired": vmem((PIECES, LINE, tok_rows, piece), BF16),
        "landed_back": vmem((PIECES, LINE + 1, tok_rows, piece), BF16),
        "result": vmem((tok_rows, width), BF16),
        "up_w": vmem((local_experts, width, 2 * ff), BF16),
        "down_w": vmem((local_experts, ff, width), BF16),
        "local_sem": dma((9 + 2 * local_experts,)),
        "rows_send": dma((LINE, 2)),
        "rows_recv": dma((LINE,)),
        "kv_send": dma((LINE,)),
        "pass_send": dma((LINE,)),
        "kv_recv": dma((GROUP,)),
        "q_sem": dma((2,)),
        "out_sem": dma((2,)),
        "gate_send": dma((GROUP,)),
        "gate_recv": dma((GROUP,)),
        "swap_send": dma((LINE,)),
        "swap_recv": dma((LINE,)),
        "term_send": dma((PIECES, LINE)),
        "term_recv": dma((PIECES, LINE + 1)),
        "mixer_send": dma((PIECES, LINE, 3)),
        "mixer_recv": dma((PIECES, SIDES, LINE)),
        "pair_send": dma((PIECES, LINE)),
        "pair_recv": dma((PIECES, LINE)),
        "share_send": dma((PIECES, LINE)),
        "share_recv": dma((PIECES, LINE + 1)),
        "hand_send": dma((PIECES,)),
        "hand_recv": dma((PIECES,)),
    }


def turned(values, cosines, sines):
    return values * cosines + pltpu.roll(values, HD // 2, 1) * sines


def layer_kernel(names, *refs):
    r = Refs(names, refs)
    section, me = lax.axis_index("section"), lax.axis_index("expert")
    z, x = lax.div(me, 2), lax.rem(me, 2)
    partner = me + 1 - 2 * x
    can_up, can_down = z < LINE - 1, z > 0
    tok_rows, width = r.acts_v.shape
    piece = width // PIECES
    column = LINE * tok_rows
    local_experts, ff = r.down_w.shape[:2]
    slots = LINE * CAP
    pending = []

    def columns(c):
        return pl.ds(c * piece, piece)

    def send(condition, copy):
        pending.append((condition, copy))
        if condition is None:
            copy.start()
        else:
            pl.when(condition)(copy.start)

    def drain():
        for condition, copy in pending:
            if condition is None:
                copy.wait_send()
            else:
                pl.when(condition)(copy.wait_send)

    sections = lax.axis_size("section")
    barrier = pltpu.get_barrier_semaphore()
    for step in range(1, GROUP):
        other = lax.rem(me + step, GROUP)
        pl.semaphore_signal(barrier, inc=1, device_id=(section, other), device_id_type=MESH)
    for step in (1, sections - 1):
        other = lax.rem(section + step, sections)
        pl.semaphore_signal(barrier, inc=1, device_id=(other, me), device_id_type=MESH)

    loads = []

    def load(src, dst):
        copy = pltpu.make_async_copy(src, dst, r.local_sem.at[len(loads)])
        copy.start()
        loads.append(copy)
        return copy

    acts_in = load(r.acts.at[0], r.acts_v)
    gains_in = load(r.gains.at[0], r.gains_v)
    ids_in = load(r.ids, r.ids_v)
    gates_in = load(r.gates, r.gates_v)
    segs_in = load(r.segs, r.segs_v)
    kv_in = load(r.keyval.at[z], r.kv_weights.at[me])
    q_in = load(r.w_query.at[0], r.q_weights.at[x])
    table_in = load(r.table, r.table_v)
    out_in = load(r.w_out.at[0], r.out_weights.at[x])
    up_in = [load(r.w_gate_up.at[0, e], r.up_w.at[e]) for e in range(local_experts)]
    down_in = [load(r.w_down.at[0, e], r.down_w.at[e]) for e in range(local_experts)]

    acts_in.wait()
    gains_in.wait()
    r.rows[z] = rms_scale(r.acts_v[...].astype(F32), r.gains_v[0:1, :]).astype(BF16)
    pl.semaphore_wait(barrier, GROUP + 1)

    def kv_pass(place, source):
        shard = place * 2 + x
        return remote(source, r.kv_weights.at[shard], r.pass_send.at[place], r.kv_recv.at[shard], partner)

    def kv_arrived(shard):
        remote(r.kv_weights.at[shard], r.kv_weights.at[shard], r.pass_send.at[0],
               r.kv_recv.at[shard], partner).wait_recv()

    def rows_copy(shard, up):
        return remote(r.rows.at[shard], r.rows.at[shard], r.rows_send.at[shard, 0 if up else 1],
                      r.rows_recv.at[shard], me + 2 if up else me - 2)

    send(None, kv_pass(z, r.keyval.at[z]))
    for far in range(1, LINE):
        for place, there in ((z + far, z + far < LINE), (z - far, z - far >= 0)):
            send(there, remote(r.keyval.at[place], r.kv_weights.at[me], r.kv_send.at[place],
                               r.kv_recv.at[me], place * 2 + x))
        if far == 1:
            send(can_up, rows_copy(z, True))
            send(can_down, rows_copy(z, False))
    q_swap = remote(r.w_query.at[0], r.q_weights.at[x], r.q_sem.at[0], r.q_sem.at[1], partner)
    send(None, q_swap)

    ids_in.wait()
    gates_in.wait()
    r.wide_ids[...] = jnp.full_like(r.wide_ids, -1)
    r.wide_gates[...] = jnp.zeros_like(r.wide_gates)
    r.wide_ids[:, :tok_rows] = r.ids_v[...]
    r.wide_gates[:, :tok_rows] = r.gates_v[...]
    wide_ids, wide_gates = r.wide_ids[...], r.wide_gates[...]
    experts = GROUP * local_experts
    numbers = lax.broadcasted_iota(jnp.int32, (experts, 128), 0)
    dense = jnp.zeros((experts, 128), F32)
    for k in range(TOPK):
        dense += jnp.where(wide_ids[k : k + 1] == numbers, wide_gates[k : k + 1], 0.0)
    dense = jnp.where(lax.rem(z, 2) == 1, pltpu.roll(dense, tok_rows, 1), dense)
    for j in range(GROUP):
        r.own_gates[j] = dense[j * local_experts : (j + 1) * local_experts]
    r.all_gates[me] = r.own_gates[me]

    def gate_copy(step):
        other = lax.rem(me + step, GROUP)
        return remote(r.own_gates.at[other], r.all_gates.at[me], r.gate_send.at[step],
                      r.gate_recv.at[step], other)

    for step in range(1, GROUP):
        send(None, gate_copy(step))

    segs_in.wait()
    seg_wide = jnp.broadcast_to(r.segs_v[...].astype(F32), (128, tok_rows * GROUP))
    seg_tall = seg_wide.T.reshape(GROUP, tok_rows, 128)
    window = 4 * tok_rows
    firsts = [2 * max(place - 1, 0) for place in range(LINE)]
    for place, first in enumerate(firsts):
        own_segs = jnp.where(x == 0, seg_tall[2 * place], seg_tall[2 * place + 1])
        own_segs = jnp.concatenate([own_segs] * (window // 128), axis=1)
        near_segs = seg_wide[:tok_rows, first * tok_rows : first * tok_rows + window]
        q_position = (place * 2 + x) * tok_rows + lax.broadcasted_iota(jnp.int32, (tok_rows, window), 0)
        k_position = first * tok_rows + lax.broadcasted_iota(jnp.int32, (tok_rows, window), 1)
        allowed = (own_segs == near_segs) & (k_position <= q_position)
        r.allowed[place] = jnp.where(allowed, 1.0, 0.0)

    for far in range(1, LINE):
        for place, there, onward, up in (
            (z - far, z - far >= 0, can_up, True),
            (z + far, z + far < LINE, can_down, False),
        ):
            pl.when(there)(lambda place=place, up=up: rows_copy(place, up).wait_recv())
            send(there & onward, rows_copy(place, up))
            pl.when(there)(lambda place=place: kv_arrived(place * 2 + x))
            send(there, kv_pass(place, r.kv_weights.at[place * 2 + x]))
    out_swap = remote(r.w_out.at[0], r.out_weights.at[x], r.out_sem.at[0], r.out_sem.at[1], partner)
    send(None, out_swap)

    kv_in.wait()
    table_in.wait()
    for place in range(LINE):
        kv_arrived(place * 2 + 1 - x)
    all_rows = r.rows[...].reshape(column, width)
    kv_out = jnp.dot(all_rows, r.kv_weights[...].reshape(width, 2 * HD), preferred_element_type=F32)

    def kv_swap(place, side):
        block = place * 2 + side
        return remote(r.key_values.at[block], r.key_values.at[block], r.swap_send.at[place],
                      r.swap_recv.at[place], partner)

    for place in range(LINE):
        block = place * 2 + x
        own = kv_out[place * tok_rows : (place + 1) * tok_rows]
        keys = turned(own[:, :HD], r.table_v[0, block], r.table_v[1, block])
        r.key_values[block, :, :HD] = keys.astype(BF16)
        r.key_values[block, :, HD:] = own[:, HD:].astype(BF16)
        send(None, kv_swap(place, x))
    q_in.wait()
    q_swap.wait_recv()
    for side in range(SIDES):
        q_out = jnp.dot(all_rows, r.q_weights[side], preferred_element_type=F32)
        for place in range(LINE):
            block = place * 2 + x
            own = q_out[place * tok_rows : (place + 1) * tok_rows]
            r.queries[place, side] = turned(own, r.table_v[0, block], r.table_v[1, block]).astype(BF16)
    for place in range(LINE):
        kv_swap(place, 1 - x).wait_recv()

    for place, first in enumerate(firsts):
        near = r.key_values[first : first + 4].reshape(window, 2 * HD)
        scores = lax.dot_general(
            r.queries[place].reshape(SIDES * tok_rows, HD), near[:, :HD], (((1,), (1,)), ((), ())),
            preferred_element_type=F32,
        ) * (1.0 / math.sqrt(HD))
        scores = jnp.where(r.allowed[place][None] > 0, scores.reshape(SIDES, tok_rows, window), -1e30)
        shifted = jnp.exp(scores - jnp.max(scores, axis=-1, keepdims=True))
        probability = (shifted / jnp.sum(shifted, axis=-1, keepdims=True)).astype(BF16)
        heads = jnp.dot(probability.reshape(SIDES * tok_rows, window), near[:, HD:],
                        preferred_element_type=F32).astype(BF16)
        for side in range(SIDES):
            r.attended[place, :, side * HD : (side + 1) * HD] = heads[side * tok_rows : (side + 1) * tok_rows]

    out_in.wait()
    out_swap.wait_recv()

    def relay(c, far, up, own, landing, send_sem, recv_sem, extra=None):
        place = z + far if up else z - far
        there = place < LINE if up else place >= 0
        behind = can_down if up else can_up
        slot = place if up or far > 1 else LINE
        out = remote(own(place), landing.at[c, slot], send_sem.at[c, place], recv_sem.at[c, slot],
                     me + 2 if up else me - 2)

        @pl.when(there)
        def _():
            ref = own(place)
            if extra is not None:
                ref[...] = (ref[...].astype(F32) + extra(place)[...].astype(F32)).astype(BF16)

            @pl.when(behind)
            def _():
                remote(own(place), landing.at[c, place], send_sem.at[c, place],
                       recv_sem.at[c, place], partner).wait_recv()
                ref[...] = (ref[...].astype(F32) + landing[c, place].astype(F32)).astype(BF16)

            out.start()

        pending.append((there, out))

    def settle(c, base, landing, recv_sem):
        r.total[...] = base

        @pl.when(can_down)
        def _():
            remote(landing.at[c, z], landing.at[c, z], r.hand_send.at[0], recv_sem.at[c, z],
                   partner).wait_recv()
            r.total[...] += landing[c, z].astype(F32)

        @pl.when(can_up)
        def _():
            remote(landing.at[c, LINE], landing.at[c, LINE], r.hand_send.at[0],
                   recv_sem.at[c, LINE], partner).wait_recv()
            r.total[...] += landing[c, LINE].astype(F32)

        return r.total[...]

    def mixer_copy(c, place, way):
        to = (me + 2, me - 2, partner)[way]
        return remote(r.mixer.at[c, x, place], r.mixer.at[c, x, place], r.mixer_send.at[c, place, way],
                      r.mixer_recv.at[c, x, place], to)

    def mixer_arrived(c, side, place):
        remote(r.mixer.at[c, side, place], r.mixer.at[c, side, place], r.hand_send.at[0],
               r.mixer_recv.at[c, side, place], partner).wait_recv()

    def term_start(c):
        made = jnp.dot(r.attended[...].reshape(column, SIDES * HD),
                       r.out_weights[:, :, columns(c)].reshape(SIDES * HD, piece),
                       preferred_element_type=F32)
        r.terms[c] = made.astype(BF16).reshape(LINE, tok_rows, piece)

    def term_hop(c, far):
        for up in (True, False):
            relay(c, far, up, lambda place: r.terms.at[c, place], r.landed, r.term_send, r.term_recv)

    def term_end(c):
        base = r.acts_v[:, columns(c)].astype(F32) + r.terms[c, z].astype(F32)
        joined = settle(c, base, r.landed, r.term_recv).astype(BF16)
        r.middle[c] = joined
        r.mixer[c, x, z] = joined
        send(can_up, mixer_copy(c, z, 0))
        send(can_down, mixer_copy(c, z, 1))
        send(None, mixer_copy(c, z, 2))

    def mixer_hop(c, far):
        for place, there, onward, way in (
            (z - far, z - far >= 0, can_up, 0), (z + far, z + far < LINE, can_down, 1),
        ):
            pl.when(there)(lambda place=place: mixer_arrived(c, x, place))
            send(there & onward, mixer_copy(c, place, way))
            send(there, mixer_copy(c, place, 2))

    def route():
        for step in range(1, GROUP):
            gate_copy(step).wait_recv()
        row = lax.broadcasted_iota(jnp.int32, (column, column), 0)
        lane = lax.broadcasted_iota(jnp.int32, (column, column), 1)
        before = (row < lane) & (lax.div(row, tok_rows) == lax.div(lane, tok_rows))
        before = jnp.where(before, 1.0, 0.0).astype(BF16)
        first_slot = lax.div(lax.broadcasted_iota(jnp.int32, (local_experts, column), 1), tok_rows) * CAP
        numbers = lax.broadcasted_iota(jnp.int32, (slots, column), 0)
        for side in range(SIDES):
            gates = jnp.concatenate(
                [r.all_gates[2 * j + side] + r.all_gates[2 * j + 2 + side] for j in range(0, LINE, 2)], axis=1
            )
            member = gates > 0
            rank = jnp.dot(jnp.where(member, 1.0, 0.0).astype(BF16), before, preferred_element_type=F32)
            slot_of = jnp.where(member, rank.astype(jnp.int32) + first_slot, -1)
            chosen = []
            for e in range(local_experts):
                mine = slot_of[e : e + 1] == numbers
                chosen.append(jnp.where(mine, 1.0, 0.0))
                r.slot_gates[e, side * slots : (side + 1) * slots] = jnp.sum(
                    jnp.where(mine, gates[e : e + 1], 0.0), axis=1, keepdims=True
                )
            chosen = jnp.concatenate(chosen, axis=0)
            r.select[side] = chosen.astype(BF16)
            r.spread[side] = chosen.T.astype(BF16)

    def gate_up(c):
        for place in range(LINE):
            mixer_arrived(c, 1 - x, place)
        if c == 0:
            for copy in up_in:
                copy.wait()
        gain = r.gains_v[1:2, columns(c)]
        for side in range(SIDES):
            held = jnp.dot(r.select[side], r.mixer[c, side].reshape(column, piece), preferred_element_type=F32)
            square = jnp.sum(held * held, axis=1, keepdims=True)
            scaled = (held * gain).astype(BF16)
            for e in range(local_experts):
                at = slice(side * slots, (side + 1) * slots)
                old = 0.0 if c == 0 else r.squares[e, at]
                r.squares[e, at] = old + square[e * slots : (e + 1) * slots]
                r.grouped[e, at] = scaled[e * slots : (e + 1) * slots]
        tile = min(256, ff)

        def one(e, carry):
            taken = r.grouped[e]
            for n in range(ff // tile):
                halves = []
                for half in range(2):
                    at = pl.ds(half * ff + n * tile, tile)
                    part = jnp.dot(taken, r.up_w[e, columns(c), at], preferred_element_type=F32)
                    if c > 0:
                        part = part + r.sums[e, :, at]
                    if c < PIECES - 1:
                        r.sums[e, :, at] = part
                    halves.append(part)
                if c == PIECES - 1:
                    scale = lax.rsqrt(r.squares[e] * (1.0 / width) + EPS)
                    a, b = halves[0] * scale, halves[1] * scale
                    r.hidden[e, :, n * tile : (n + 1) * tile] = (jax.nn.silu(a) * b).astype(BF16)
            return carry

        lax.fori_loop(0, local_experts, one, 0)

    def ticks(stages, after=None):
        for tick in range(PIECES + len(stages) - 1):
            for stage, todo in enumerate(stages):
                if 0 <= tick - stage < PIECES:
                    todo(tick - stage)
            if after is not None and tick in after:
                after[tick]()

    hops = range(LINE - 1, 0, -1)

    def hop_stages(hop):
        return [lambda c, far=far: hop(c, far) for far in hops]

    def first_hop(c):
        term_start(c)
        term_hop(c, LINE - 1)

    ticks(
        [first_hop] + hop_stages(term_hop)[1:] + [term_end]
        + [lambda c, far=far: mixer_hop(c, far) for far in range(1, LINE)] + [gate_up],
        {0: route},
    )

    def hand(c):
        return remote(r.result.at[:, columns(c)], r.handed.at[:, columns(c)], r.hand_send.at[c],
                      r.hand_recv.at[c], me, lax.rem(section + 1, sections))

    def pair_copy(c, place):
        return remote(r.shares.at[c, 1 - x, place], r.paired.at[c, place], r.pair_send.at[c, place],
                      r.pair_recv.at[c, place], partner)

    def share_start(c):
        if c == 0:
            for copy in down_in:
                copy.wait()

        def one(e, carry):
            made = jnp.dot(r.hidden[e], r.down_w[e, :, columns(c)], preferred_element_type=F32)
            made = (made * r.slot_gates[e]).astype(BF16)
            for side in range(SIDES):
                r.outputs[side, e] = made[side * slots : (side + 1) * slots]
            return carry

        lax.fori_loop(0, local_experts, one, 0)
        for side in range(SIDES):
            mixed = jnp.dot(r.spread[side], r.outputs[side].reshape(local_experts * slots, piece),
                            preferred_element_type=F32)
            r.shares[c, side] = mixed.astype(BF16).reshape(LINE, tok_rows, piece)
        for place in (0, 3, 1, 2):
            send(None, pair_copy(c, place))

    def pair_arrived(c, place):
        pair_copy(c, place).wait_recv()
        return r.paired.at[c, place]

    def share_hop(c, far):
        for up in (True, False):
            relay(c, far, up, lambda place: r.shares.at[c, x, place], r.landed_back, r.share_send,
                  r.share_recv, lambda place: pair_arrived(c, place))

    def share_end(c):
        base = r.middle[c].astype(F32) + r.shares[c, x, z].astype(F32)
        base = base + pair_arrived(c, z)[...].astype(F32)
        r.result[:, columns(c)] = settle(c, base, r.landed_back, r.share_recv).astype(BF16)
        send(None, hand(c))

    ticks([share_start] + hop_stages(share_hop) + [share_end])
    for c in range(PIECES):
        hand(c).wait_recv()
    drain()


def rope_tables(tokens, tok_rows):
    half = HD // 2
    frequency = np.float32(ROPE_BASE) ** (-np.arange(half, dtype=np.float32) * np.float32(2.0 / HD))
    angles = np.arange(tokens, dtype=np.float32)[:, None] * frequency.astype(np.float32)[None, :]
    cosines, sines = np.cos(angles), np.sin(angles)
    tables = np.stack([np.concatenate([cosines, cosines], 1), np.concatenate([-sines, sines], 1)])
    return tables.astype(np.float32).reshape(2, tokens // tok_rows, tok_rows, HD)


def per_device(
    acts,
    norm_gains,
    w_query,
    w_keyval,
    w_out,
    w_gate_up,
    w_down,
    expert_ids,
    gate_weights,
    segment_ids,
):
    tok_rows, width = acts.shape[1:]
    keyval = w_keyval[0].transpose(1, 0, 2)
    scratch = scratch_of(tok_rows, width, keyval.shape[1], w_gate_up.shape[1], w_down.shape[2])
    anywhere = pl.BlockSpec(memory_space=pl.ANY)
    handed = pl.pallas_call(
        functools.partial(layer_kernel, ARGS + tuple(scratch)),
        out_shape=jax.ShapeDtypeStruct((tok_rows, width), BF16),
        in_specs=[anywhere] * (len(ARGS) - 1),
        out_specs=pl.BlockSpec(memory_space=pltpu.VMEM),
        scratch_shapes=list(scratch.values()),
        compiler_params=pltpu.CompilerParams(
            collective_id=0, has_side_effects=True, vmem_limit_bytes=VMEM_MIB << 20
        ),
    )(
        acts, norm_gains, expert_ids[0].T, gate_weights[0].T, segment_ids,
        jnp.asarray(rope_tables(tok_rows * GROUP, tok_rows)), w_query, keyval, w_out, w_gate_up, w_down,
    )
    return handed[None]


def solution(mesh):
    placed = (
        P("section", "expert", None),
        P("section", None, None),
        P("section", None, "expert"),
        P("section", "expert", None, None),
        P("section", "expert", None),
        P("section", "expert", None, None),
        P("section", "expert", None, None),
        P("section", "expert", None),
        P("section", "expert", None),
        P("section", None),
    )
    return jax.shard_map(
        per_device if mesh.shape["expert"] == GROUP else per_device_general,
        mesh=mesh,
        in_specs=placed,
        out_specs=P("section", "expert", None),
        check_vma=False,
    )
```

```python
import functools
import math

import jax
import jax.numpy as jnp
import numpy as np
from jax import lax
from jax.experimental import pallas as pl
from jax.experimental.pallas import tpu as pltpu
from jax.sharding import PartitionSpec as P

MESH = pl.DeviceIdType.MESH

HD = 128
KV = 4
EXPERTS = 32
TOPK = 8
CAP = 24


EPS = 1e-06
ROPE_BASE = 1000000.0


def shifted_2(x, axis, by):
    length = lax.axis_size(axis)
    return lax.ppermute(x, axis, [(i, (i + by) % length) for i in range(length)])


def rms_scale(values, gain_row):
    mean_sq = jnp.mean(values * values, axis=-1, keepdims=True)
    return values * lax.rsqrt(mean_sq + EPS) * gain_row


def rotate(values, positions):
    half_width = values.shape[-1] // 2
    frequency = ROPE_BASE ** (-jnp.arange(half_width, dtype=jnp.float32) * 2.0 / values.shape[-1])
    angles = positions[:, None] * frequency[None, :]
    cosines = jnp.cos(angles)[:, None, :]
    sine_table = jnp.sin(angles)[:, None, :]
    leading = values[..., :half_width]
    trailing = values[..., half_width:]
    return jnp.concatenate(
        [leading * cosines - trailing * sine_table, trailing * cosines + leading * sine_table],
        axis=-1,
    )


def head_block(q_block, key_rows, value_rows, seg_block, seg_all, pos_block, pos_all, score_scale):
    scores = (
        jnp.einsum("qhd,kd->hqk", q_block, key_rows, preferred_element_type=jnp.float32)
        * score_scale
    )
    allowed = (seg_block[:, None] == seg_all[None, :]) & (pos_all[None, :] <= pos_block[:, None])
    scores = jnp.where(allowed[None], scores, -1e30)
    row_max = jnp.max(scores, axis=-1, keepdims=True)
    shifted = jnp.exp(scores - row_max)
    probability = (shifted / jnp.sum(shifted, axis=-1, keepdims=True)).astype(jnp.bfloat16)
    return jnp.einsum(
        "hqk,kd->qhd", probability, value_rows, preferred_element_type=jnp.float32
    ).astype(jnp.bfloat16)


def expert_rows(grouped, gate_up, down_proj):
    gate_up_out = jnp.einsum("necd,edf->necf", grouped, gate_up, preferred_element_type=jnp.float32)
    half_width = down_proj.shape[1]
    hidden = (jax.nn.silu(gate_up_out[..., :half_width]) * gate_up_out[..., half_width:]).astype(
        jnp.bfloat16
    )
    return jnp.einsum(
        "necf,efd->necd", hidden, down_proj, preferred_element_type=jnp.float32
    ).astype(jnp.bfloat16)


def send_back(results):
    return lax.all_to_all(results, "expert", split_axis=0, concat_axis=0, tiled=True)


def per_device_general(
    acts,
    norm_gains,
    w_query,
    w_keyval,
    w_out,
    w_gate_up,
    w_down,
    expert_ids,
    gate_weights,
    segment_ids,
):
    device_count = lax.axis_size("expert")
    my_index = lax.axis_index("expert")
    tok_rows = acts.shape[1]
    width = acts.shape[2]
    head_dev = w_query.shape[2] // HD
    local_experts = w_gate_up.shape[1]
    heads_total = head_dev * device_count
    gains = norm_gains[0]
    x_wide = acts[0].astype(jnp.float32)
    normed = rms_scale(x_wide, gains[0]).astype(jnp.bfloat16)
    kv_index = my_index * head_dev // (heads_total // KV)
    query_weight = w_query[0]
    gathered_keyval = lax.all_gather(w_keyval[0], "expert", axis=0, tiled=True)
    head_keyval = lax.dynamic_index_in_dim(gathered_keyval, kv_index, 1, keepdims=False)
    row_piece = lax.all_gather(normed, "expert", axis=0, tiled=True)
    piece_rows = row_piece.shape[0]
    positions = jnp.arange(piece_rows).astype(jnp.float32)
    query_piece_rows = row_piece.shape[0]
    query_positions = jnp.arange(query_piece_rows).astype(jnp.float32)
    queries = jnp.dot(row_piece, query_weight, preferred_element_type=jnp.float32).reshape(
        query_piece_rows, head_dev, HD
    )
    queries = (
        rotate(queries, query_positions)
        .astype(jnp.bfloat16)
        .reshape(query_piece_rows, head_dev * HD)
    )
    keyval = jnp.dot(row_piece, head_keyval, preferred_element_type=jnp.float32)
    key_rows = rotate(keyval[:, None, :HD], positions).astype(jnp.bfloat16).reshape(piece_rows, HD)
    value_rows = keyval[:, HD:].astype(jnp.bfloat16)
    projected = jnp.concatenate([queries, key_rows, value_rows], axis=1)
    tokens = projected.shape[0]
    all_queries = projected[:, : head_dev * HD].reshape(tokens, head_dev, HD)
    all_keys = projected[:, head_dev * HD : (head_dev + 1) * HD]
    all_values = projected[:, (head_dev + 1) * HD :]
    segments = segment_ids[0]
    all_positions = jnp.arange(tokens)
    q_rows = min(512, tokens)
    score_scale = 1.0 / math.sqrt(HD)

    def attend(first_row):
        q_block = lax.dynamic_slice_in_dim(all_queries, first_row, q_rows, 0)
        seg_block = lax.dynamic_slice_in_dim(segments, first_row, q_rows, 0)
        pos_block = first_row + jnp.arange(q_rows)
        return head_block(
            q_block,
            all_keys,
            all_values,
            seg_block,
            segments,
            pos_block,
            all_positions,
            score_scale,
        )

    block_starts = jnp.arange(tokens // q_rows) * q_rows
    attended = lax.map(attend, block_starts).reshape(tokens, head_dev * HD)
    out_weight = w_out[0]
    attention = lax.psum_scatter(
        jnp.dot(attended, out_weight, preferred_element_type=jnp.float32).astype(jnp.bfloat16),
        "expert",
        scatter_dimension=0,
        tiled=True,
    ).astype(jnp.float32)
    middle_wide = (x_wide + attention).astype(jnp.bfloat16).astype(jnp.float32)
    mixer_in = rms_scale(middle_wide, gains[1]).astype(jnp.bfloat16)
    routes_flat = expert_ids[0].reshape(-1)
    onehot = routes_flat[:, None] == jnp.arange(EXPERTS, dtype=jnp.int32)[None, :]
    order = jnp.arange(routes_flat.shape[0])
    below = (order[None, :] < order[:, None]).astype(jnp.bfloat16)
    earlier = jnp.dot(below, onehot.astype(jnp.bfloat16), preferred_element_type=jnp.float32)
    slot_rank = jnp.sum(jnp.where(onehot, earlier, 0.0), axis=1).astype(jnp.int32)
    slot_index = routes_flat * CAP + slot_rank
    routed = jnp.repeat(mixer_in, TOPK, axis=0)
    send_rows = (
        jnp.zeros((EXPERTS * CAP, width), jnp.bfloat16)
        .at[slot_index]
        .set(routed)
        .reshape(EXPERTS, CAP, width)
    )
    gate_up = w_gate_up[0]
    down_proj = w_down[0]
    received = lax.all_to_all(send_rows, "expert", split_axis=0, concat_axis=0, tiled=True)
    source_count = received.shape[0] // local_experts
    grouped = received.reshape(source_count, local_experts, received.shape[1], width)
    outputs = expert_rows(grouped, gate_up, down_proj)
    returned = send_back(outputs.reshape(received.shape))
    picked = (
        returned.reshape(EXPERTS * CAP, width)[slot_index]
        .astype(jnp.float32)
        .reshape(tok_rows, TOPK, width)
    )
    mixed = jnp.sum(picked * gate_weights[0][:, :, None], axis=1)
    result = (middle_wide + mixed).astype(jnp.bfloat16)
    handed = shifted_2(result, "section", 1)
    return handed[None]


LINE = 4
GROUP = 8
SIDES = 2
PIECES = 4
VMEM_MIB = 62
EARLY = 2
BF16 = jnp.bfloat16
F32 = jnp.float32


def remote(src, dst, send_sem, recv_sem, expert, section=None):
    if section is None:
        section = lax.axis_index("section")
    return pltpu.make_async_remote_copy(
        src_ref=src,
        dst_ref=dst,
        send_sem=send_sem,
        recv_sem=recv_sem,
        device_id=(section, expert),
        device_id_type=MESH,
    )


class Refs:
    def __init__(self, names, refs):
        for name, ref in zip(names, refs, strict=True):
            setattr(self, name, ref)


ARGS = (
    "acts", "gains", "ids", "gates", "segs", "table", "w_query", "keyval", "w_out", "w_gate_up",
    "w_down", "handed",
)


def scratch_of(tok_rows, width, kv_rows, local_experts, ff):
    piece = width // PIECES
    slots = LINE * CAP
    vmem, dma = pltpu.VMEM, pltpu.SemaphoreType.DMA
    return {
        "acts_v": vmem((tok_rows, width), BF16),
        "gains_v": vmem((2, 8, width), F32),
        "ids_v": vmem((TOPK, tok_rows), jnp.int32),
        "gates_v": vmem((TOPK, tok_rows), F32),
        "segs_v": vmem((8, tok_rows * GROUP), jnp.int32),
        "table_v": vmem((2, GROUP, tok_rows, HD), F32),
        "wide_ids": vmem((TOPK, 128), jnp.int32),
        "wide_gates": vmem((TOPK, 128), F32),
        "own_gates": vmem((GROUP, 8, 128), F32),
        "all_gates": vmem((GROUP, 8, 128), F32),
        "allowed": vmem((LINE, tok_rows, 4 * tok_rows), F32),
        "rows": vmem((LINE, tok_rows, width), BF16),
        "kv_weights": vmem((GROUP, kv_rows, 2 * HD), BF16),
        "q_weights": vmem((SIDES, width, HD), BF16),
        "out_weights": vmem((SIDES, HD, width), BF16),
        "queries": vmem((LINE, SIDES, tok_rows, HD), BF16),
        "key_values": vmem((GROUP, tok_rows, 2 * HD), BF16),
        "attended": vmem((LINE, tok_rows, SIDES * HD), BF16),
        "terms": vmem((PIECES, LINE, tok_rows, piece), BF16),
        "landed": vmem((PIECES, LINE + 1, tok_rows, piece), BF16),
        "total": vmem((tok_rows, piece), F32),
        "middle": vmem((PIECES, tok_rows, piece), BF16),
        "mixer": vmem((PIECES, SIDES, LINE, tok_rows, piece), BF16),
        "select": vmem((SIDES, local_experts * slots, LINE * tok_rows), BF16),
        "spread": vmem((SIDES, LINE * tok_rows, local_experts * slots), BF16),
        "slot_gates": vmem((local_experts, SIDES * slots, 1), F32),
        "squares": vmem((local_experts, SIDES * slots, 1), F32),
        "sums": vmem((local_experts, SIDES * slots, 2 * ff), F32),
        "hidden": vmem((local_experts, SIDES * slots, ff), BF16),
        "packed": vmem((SIDES, local_experts, slots, piece), BF16),
        "shares": vmem((PIECES, SIDES, LINE, tok_rows, piece), BF16),
        "paired": vmem((PIECES, LINE, tok_rows, piece), BF16),
        "landed_back": vmem((PIECES, LINE + 1, tok_rows, piece), BF16),
        "result": vmem((tok_rows, width), BF16),
        "up_w": vmem((local_experts, width, 2 * ff), BF16),
        "down_w": vmem((local_experts, ff, width), BF16),
        "local_sem": dma((17 + 2 * local_experts,)),
        "rows_send": dma((LINE, 2)),
        "rows_recv": dma((LINE,)),
        "kv_send": dma((LINE,)),
        "pass_send": dma((LINE,)),
        "kv_recv": dma((GROUP,)),
        "q_sem": dma((2,)),
        "out_send": dma((PIECES,)),
        "out_recv": dma((PIECES,)),
        "gate_send": dma((GROUP,)),
        "gate_recv": dma((GROUP,)),
        "swap_send": dma((LINE,)),
        "swap_recv": dma((LINE,)),
        "term_send": dma((PIECES, LINE)),
        "term_recv": dma((PIECES, LINE + 1)),
        "mixer_send": dma((PIECES, LINE, 3)),
        "mixer_recv": dma((PIECES, SIDES, LINE)),
        "pair_send": dma((PIECES, LINE)),
        "pair_recv": dma((PIECES, LINE)),
        "share_send": dma((PIECES, LINE)),
        "share_recv": dma((PIECES, LINE + 1)),
        "hand_send": dma((PIECES,)),
        "hand_recv": dma((PIECES,)),
    }


def turned(values, cosines, sines):
    return values * cosines + pltpu.roll(values, HD // 2, 1) * sines


def layer_kernel(names, *refs):
    r = Refs(names, refs)
    section, me = lax.axis_index("section"), lax.axis_index("expert")
    z, x = lax.div(me, 2), lax.rem(me, 2)
    partner = me + 1 - 2 * x
    can_up, can_down = z < LINE - 1, z > 0
    tok_rows, width = r.acts_v.shape
    piece = width // PIECES
    column = LINE * tok_rows
    local_experts, ff = r.down_w.shape[:2]
    slots = LINE * CAP
    pending = []

    def columns(c):
        return pl.ds(c * piece, piece)

    def send(condition, copy):
        pending.append((condition, copy))
        if condition is None:
            copy.start()
        else:
            pl.when(condition)(copy.start)

    def drain():
        for condition, copy in pending:
            if condition is None:
                copy.wait_send()
            else:
                pl.when(condition)(copy.wait_send)

    sections = lax.axis_size("section")
    barrier = pltpu.get_barrier_semaphore()
    for step in range(1, GROUP):
        other = lax.rem(me + step, GROUP)
        pl.semaphore_signal(barrier, inc=1, device_id=(section, other), device_id_type=MESH)
    for step in (1, sections - 1):
        other = lax.rem(section + step, sections)
        pl.semaphore_signal(barrier, inc=1, device_id=(other, me), device_id_type=MESH)

    loads = []

    def load(src, dst):
        copy = pltpu.make_async_copy(src, dst, r.local_sem.at[len(loads)])
        copy.start()
        loads.append(copy)
        return copy

    acts_in = load(r.acts.at[0], r.acts_v)
    gains_in = [load(r.gains.at[0, pl.ds(g, 1)], r.gains_v.at[g, pl.ds(0, 1)]) for g in range(2)]
    ids_in = load(r.ids, r.ids_v)
    gates_in = load(r.gates, r.gates_v)
    segs_in = [load(r.segs, r.segs_v.at[pl.ds(row, 1)]) for row in range(8)]
    kv_in = load(r.keyval.at[z], r.kv_weights.at[me])
    q_in = load(r.w_query.at[0], r.q_weights.at[x])
    table_in = load(r.table, r.table_v)
    out_in = load(r.w_out.at[0], r.out_weights.at[x])
    up_in = [load(r.w_gate_up.at[0, e], r.up_w.at[e]) for e in range(local_experts)]
    down_in = [load(r.w_down.at[0, e], r.down_w.at[e]) for e in range(local_experts)]

    acts_in.wait()
    for copy in gains_in:
        copy.wait()
    r.rows[z] = rms_scale(r.acts_v[...].astype(F32), r.gains_v[0, 0:1, :]).astype(BF16)
    pl.semaphore_wait(barrier, GROUP + 1)

    def kv_pass(place, source):
        shard = place * 2 + x
        return remote(source, r.kv_weights.at[shard], r.pass_send.at[place], r.kv_recv.at[shard], partner)

    def kv_arrived(shard):
        remote(r.kv_weights.at[shard], r.kv_weights.at[shard], r.pass_send.at[0],
               r.kv_recv.at[shard], partner).wait_recv()

    def rows_copy(shard, up):
        return remote(r.rows.at[shard], r.rows.at[shard], r.rows_send.at[shard, 0 if up else 1],
                      r.rows_recv.at[shard], me + 2 if up else me - 2)

    send(None, kv_pass(z, r.keyval.at[z]))
    for far in range(1, LINE):
        for place, there in ((z + far, z + far < LINE), (z - far, z - far >= 0)):
            send(there, remote(r.keyval.at[place], r.kv_weights.at[me], r.kv_send.at[place],
                               r.kv_recv.at[me], place * 2 + x))
    send(can_up, rows_copy(z, True))
    send(can_down, rows_copy(z, False))
    q_swap = remote(r.w_query.at[0], r.q_weights.at[x], r.q_sem.at[0], r.q_sem.at[1], partner)
    send(None, q_swap)

    ids_in.wait()
    gates_in.wait()
    r.wide_ids[...] = jnp.full_like(r.wide_ids, -1)
    r.wide_gates[...] = jnp.zeros_like(r.wide_gates)
    r.wide_ids[:, :tok_rows] = r.ids_v[...]
    r.wide_gates[:, :tok_rows] = r.gates_v[...]
    wide_ids, wide_gates = r.wide_ids[...], r.wide_gates[...]
    row = lax.broadcasted_iota(jnp.int32, (GROUP * 8, 128), 0)
    numbers = jnp.where(lax.rem(row, 8) < local_experts, lax.div(row, 8) * local_experts + lax.rem(row, 8), -2)
    dense = jnp.zeros((GROUP * 8, 128), F32)
    for k in range(TOPK):
        dense += jnp.where(wide_ids[k : k + 1] == numbers, wide_gates[k : k + 1], 0.0)
    dense = jnp.where(lax.rem(z, 2) == 1, pltpu.roll(dense, tok_rows, 1), dense)
    for j in range(GROUP):
        r.own_gates[j] = dense[j * 8 : (j + 1) * 8]
    r.all_gates[me] = r.own_gates[me]

    def gate_copy(step):
        other = lax.rem(me + step, GROUP)
        return remote(r.own_gates.at[other], r.all_gates.at[me], r.gate_send.at[step],
                      r.gate_recv.at[step], other)

    for step in range(1, GROUP):
        send(None, gate_copy(step))

    for copy in segs_in:
        copy.wait()
    seg_wide = jnp.concatenate([r.segs_v[...].astype(F32)] * 16, axis=0)
    seg_tall = seg_wide.T.reshape(GROUP, tok_rows, 128)
    window = 4 * tok_rows
    firsts = [2 * max(place - 1, 0) for place in range(LINE)]
    for place, first in enumerate(firsts):
        own_segs = jnp.where(x == 0, seg_tall[2 * place], seg_tall[2 * place + 1])
        own_segs = jnp.concatenate([own_segs] * (window // 128), axis=1)
        near_segs = seg_wide[:tok_rows, first * tok_rows : first * tok_rows + window]
        q_position = (place * 2 + x) * tok_rows + lax.broadcasted_iota(jnp.int32, (tok_rows, window), 0)
        k_position = first * tok_rows + lax.broadcasted_iota(jnp.int32, (tok_rows, window), 1)
        allowed = (own_segs == near_segs) & (k_position <= q_position)
        r.allowed[place] = jnp.where(allowed, 1.0, 0.0)

    for far in range(1, LINE):
        for place, there in ((z - far, z - far >= 0), (z + far, z + far < LINE)):
            pl.when(there)(lambda place=place: kv_arrived(place * 2 + x))
            send(there, kv_pass(place, r.kv_weights.at[place * 2 + x]))

    def out_swap(c):
        part = r.out_weights.at[x, :, columns(c)]
        return remote(r.w_out.at[0, :, columns(c)], part, r.out_send.at[c], r.out_recv.at[c], partner)

    for c in range(EARLY):
        send(None, out_swap(c))
    for far in range(1, LINE):
        for place, there, onward, up in (
            (z - far, z - far >= 0, can_up, True),
            (z + far, z + far < LINE, can_down, False),
        ):
            pl.when(there)(lambda place=place, up=up: rows_copy(place, up).wait_recv())
            send(there & onward, rows_copy(place, up))

    kv_in.wait()
    table_in.wait()
    for place in range(LINE):
        kv_arrived(place * 2 + 1 - x)
    all_rows = r.rows[...].reshape(column, width)
    kv_out = jnp.dot(all_rows, r.kv_weights[...].reshape(width, 2 * HD), preferred_element_type=F32)

    def kv_swap(place, side):
        block = place * 2 + side
        return remote(r.key_values.at[block], r.key_values.at[block], r.swap_send.at[place],
                      r.swap_recv.at[place], partner)

    for place in range(LINE):
        block = place * 2 + x
        own = kv_out[place * tok_rows : (place + 1) * tok_rows]
        keys = turned(own[:, :HD], r.table_v[0, block], r.table_v[1, block])
        r.key_values[block, :, :HD] = keys.astype(BF16)
        r.key_values[block, :, HD:] = own[:, HD:].astype(BF16)
        send(None, kv_swap(place, x))
    for c in range(EARLY, PIECES):
        send(None, out_swap(c))
    q_in.wait()
    q_swap.wait_recv()
    for side in range(SIDES):
        q_out = jnp.dot(all_rows, r.q_weights[side], preferred_element_type=F32)
        for place in range(LINE):
            block = place * 2 + x
            own = q_out[place * tok_rows : (place + 1) * tok_rows]
            r.queries[place, side] = turned(own, r.table_v[0, block], r.table_v[1, block]).astype(BF16)
    for place in range(LINE):
        kv_swap(place, 1 - x).wait_recv()

    for place, first in enumerate(firsts):
        near = r.key_values[first : first + 4].reshape(window, 2 * HD)
        scores = lax.dot_general(
            r.queries[place].reshape(SIDES * tok_rows, HD), near[:, :HD], (((1,), (1,)), ((), ())),
            preferred_element_type=F32,
        ) * (1.0 / math.sqrt(HD))
        scores = jnp.where(r.allowed[place][None] > 0, scores.reshape(SIDES, tok_rows, window), -1e30)
        shifted = jnp.exp(scores - jnp.max(scores, axis=-1, keepdims=True))
        probability = (shifted / jnp.sum(shifted, axis=-1, keepdims=True)).astype(BF16)
        heads = jnp.dot(probability.reshape(SIDES * tok_rows, window), near[:, HD:],
                        preferred_element_type=F32).astype(BF16)
        for side in range(SIDES):
            r.attended[place, :, side * HD : (side + 1) * HD] = heads[side * tok_rows : (side + 1) * tok_rows]

    out_in.wait()

    def relay(c, far, up, own, landing, send_sem, recv_sem, extra=None):
        place = z + far if up else z - far
        there = place < LINE if up else place >= 0
        behind = can_down if up else can_up
        slot = place if up or far > 1 else LINE
        out = remote(own(place), landing.at[c, slot], send_sem.at[c, place], recv_sem.at[c, slot],
                     me + 2 if up else me - 2)

        @pl.when(there)
        def _():
            ref = own(place)
            if extra is not None:
                ref[...] = (ref[...].astype(F32) + extra(place)[...].astype(F32)).astype(BF16)

            @pl.when(behind)
            def _():
                remote(own(place), landing.at[c, place], send_sem.at[c, place],
                       recv_sem.at[c, place], partner).wait_recv()
                ref[...] = (ref[...].astype(F32) + landing[c, place].astype(F32)).astype(BF16)

            out.start()

        pending.append((there, out))

    def settle(c, base, landing, recv_sem):
        r.total[...] = base

        @pl.when(can_down)
        def _():
            remote(landing.at[c, z], landing.at[c, z], r.hand_send.at[0], recv_sem.at[c, z],
                   partner).wait_recv()
            r.total[...] += landing[c, z].astype(F32)

        @pl.when(can_up)
        def _():
            remote(landing.at[c, LINE], landing.at[c, LINE], r.hand_send.at[0],
                   recv_sem.at[c, LINE], partner).wait_recv()
            r.total[...] += landing[c, LINE].astype(F32)

        return r.total[...]

    def mixer_copy(c, place, way):
        to = (me + 2, me - 2, partner)[way]
        return remote(r.mixer.at[c, x, place], r.mixer.at[c, x, place], r.mixer_send.at[c, place, way],
                      r.mixer_recv.at[c, x, place], to)

    def mixer_arrived(c, side, place):
        remote(r.mixer.at[c, side, place], r.mixer.at[c, side, place], r.hand_send.at[0],
               r.mixer_recv.at[c, side, place], partner).wait_recv()

    def term_start(c):
        out_swap(c).wait_recv()
        made = jnp.dot(r.attended[...].reshape(column, SIDES * HD),
                       r.out_weights[:, :, columns(c)].reshape(SIDES * HD, piece),
                       preferred_element_type=F32)
        r.terms[c] = made.astype(BF16).reshape(LINE, tok_rows, piece)

    def term_hop(c, far):
        for up in (True, False):
            relay(c, far, up, lambda place: r.terms.at[c, place], r.landed, r.term_send, r.term_recv)

    def term_end(c):
        base = r.acts_v[:, columns(c)].astype(F32) + r.terms[c, z].astype(F32)
        joined = settle(c, base, r.landed, r.term_recv).astype(BF16)
        r.middle[c] = joined
        r.mixer[c, x, z] = joined
        send(can_up, mixer_copy(c, z, 0))
        send(can_down, mixer_copy(c, z, 1))
        send(None, mixer_copy(c, z, 2))

    def mixer_hop(c, far):
        for place, there, onward, way in (
            (z - far, z - far >= 0, can_up, 0), (z + far, z + far < LINE, can_down, 1),
        ):
            pl.when(there)(lambda place=place: mixer_arrived(c, x, place))
            send(there & onward, mixer_copy(c, place, way))
            send(there, mixer_copy(c, place, 2))

    def route():
        for step in range(1, GROUP):
            gate_copy(step).wait_recv()
        row = lax.broadcasted_iota(jnp.int32, (column, column), 0)
        lane = lax.broadcasted_iota(jnp.int32, (column, column), 1)
        before = (row < lane) & (lax.div(row, tok_rows) == lax.div(lane, tok_rows))
        before = jnp.where(before, 1.0, 0.0).astype(BF16)
        first_slot = lax.div(lax.broadcasted_iota(jnp.int32, (8, column), 1), tok_rows) * CAP
        numbers = lax.broadcasted_iota(jnp.int32, (slots, column), 0)
        for side in range(SIDES):
            gates = jnp.concatenate(
                [r.all_gates[2 * j + side] + r.all_gates[2 * j + 2 + side] for j in range(0, LINE, 2)], axis=1
            )
            member = gates > 0
            rank = jnp.dot(jnp.where(member, 1.0, 0.0).astype(BF16), before, preferred_element_type=F32)
            slot_of = jnp.where(member, rank.astype(jnp.int32) + first_slot, -1)
            chosen = []
            for e in range(local_experts):
                mine = slot_of[e : e + 1] == numbers
                chosen.append(jnp.where(mine, 1.0, 0.0))
                r.slot_gates[e, side * slots : (side + 1) * slots] = jnp.sum(
                    jnp.where(mine, gates[e : e + 1], 0.0), axis=1, keepdims=True
                )
            chosen = jnp.concatenate(chosen, axis=0)
            r.select[side] = chosen.astype(BF16)
            r.spread[side] = chosen.T.astype(BF16)

    def gate_up(c):
        for place in range(LINE):
            mixer_arrived(c, 1 - x, place)
        if c == 0:
            for copy in up_in:
                copy.wait()
        gain = r.gains_v[1, 0:1, columns(c)]
        for side in range(SIDES):
            held = jnp.dot(r.select[side], r.mixer[c, side].reshape(column, piece), preferred_element_type=F32)
            square = jnp.sum(held * held, axis=1, keepdims=True)
            scaled = (held * gain).astype(BF16)
            for e in range(local_experts):
                at = slice(side * slots, (side + 1) * slots)
                old = 0.0 if c == 0 else r.squares[e, at]
                r.squares[e, at] = old + square[e * slots : (e + 1) * slots]
                r.packed[side, e] = scaled[e * slots : (e + 1) * slots]
        tile = min(256, ff)

        def one(e, carry):
            taken = r.packed[:, e].reshape(SIDES * slots, piece)
            for n in range(ff // tile):
                halves = []
                for half in range(2):
                    at = pl.ds(half * ff + n * tile, tile)
                    part = jnp.dot(taken, r.up_w[e, columns(c), at], preferred_element_type=F32)
                    if c > 0:
                        part = part + r.sums[e, :, at]
                    if c < PIECES - 1:
                        r.sums[e, :, at] = part
                    halves.append(part)
                if c == PIECES - 1:
                    scale = lax.rsqrt(r.squares[e] * (1.0 / width) + EPS)
                    a, b = halves[0] * scale, halves[1] * scale
                    r.hidden[e, :, n * tile : (n + 1) * tile] = (jax.nn.silu(a) * b).astype(BF16)
            return carry

        lax.fori_loop(0, local_experts, one, 0)

    def ticks(stages, after=None):
        for tick in range(PIECES + len(stages) - 1):
            for stage, todo in enumerate(stages):
                if 0 <= tick - stage < PIECES:
                    todo(tick - stage)
            if after is not None and tick in after:
                after[tick]()

    hops = range(LINE - 1, 0, -1)

    def hop_stages(hop):
        return [lambda c, far=far: hop(c, far) for far in hops]

    def first_hop(c):
        term_start(c)
        term_hop(c, LINE - 1)

    ticks(
        [first_hop] + hop_stages(term_hop)[1:] + [term_end]
        + [lambda c, far=far: mixer_hop(c, far) for far in range(1, LINE)] + [gate_up],
        {0: route},
    )

    def hand(c):
        return remote(r.result.at[:, columns(c)], r.handed.at[:, columns(c)], r.hand_send.at[c],
                      r.hand_recv.at[c], me, lax.rem(section + 1, sections))

    def pair_copy(c, place):
        return remote(r.shares.at[c, 1 - x, place], r.paired.at[c, place], r.pair_send.at[c, place],
                      r.pair_recv.at[c, place], partner)

    def share_start(c):
        if c == 0:
            for copy in down_in:
                copy.wait()

        def one(e, carry):
            made = jnp.dot(r.hidden[e], r.down_w[e, :, columns(c)], preferred_element_type=F32)
            made = (made * r.slot_gates[e]).astype(BF16)
            for side in range(SIDES):
                r.packed[side, e] = made[side * slots : (side + 1) * slots]
            return carry

        lax.fori_loop(0, local_experts, one, 0)
        for side in range(SIDES):
            mixed = jnp.dot(r.spread[side], r.packed[side].reshape(local_experts * slots, piece),
                            preferred_element_type=F32)
            r.shares[c, side] = mixed.astype(BF16).reshape(LINE, tok_rows, piece)
        for place in (0, 3, 1, 2):
            send(None, pair_copy(c, place))

    def pair_arrived(c, place):
        pair_copy(c, place).wait_recv()
        return r.paired.at[c, place]

    def share_hop(c, far):
        for up in (True, False):
            relay(c, far, up, lambda place: r.shares.at[c, x, place], r.landed_back, r.share_send,
                  r.share_recv, lambda place: pair_arrived(c, place))

    def share_end(c):
        base = r.middle[c].astype(F32) + r.shares[c, x, z].astype(F32)
        base = base + pair_arrived(c, z)[...].astype(F32)
        r.result[:, columns(c)] = settle(c, base, r.landed_back, r.share_recv).astype(BF16)
        send(None, hand(c))

    ticks([share_start] + hop_stages(share_hop) + [share_end])
    for c in range(PIECES):
        hand(c).wait_recv()
    drain()


def rope_tables(tokens, tok_rows):
    half = HD // 2
    frequency = np.float32(ROPE_BASE) ** (-np.arange(half, dtype=np.float32) * np.float32(2.0 / HD))
    angles = np.arange(tokens, dtype=np.float32)[:, None] * frequency.astype(np.float32)[None, :]
    cosines, sines = np.cos(angles), np.sin(angles)
    tables = np.stack([np.concatenate([cosines, cosines], 1), np.concatenate([-sines, sines], 1)])
    return tables.astype(np.float32).reshape(2, tokens // tok_rows, tok_rows, HD)


def per_device(
    acts,
    norm_gains,
    w_query,
    w_keyval,
    w_out,
    w_gate_up,
    w_down,
    expert_ids,
    gate_weights,
    segment_ids,
):
    tok_rows, width = acts.shape[1:]
    keyval = w_keyval[0].transpose(1, 0, 2)
    scratch = scratch_of(tok_rows, width, keyval.shape[1], w_gate_up.shape[1], w_down.shape[2])
    anywhere = pl.BlockSpec(memory_space=pl.ANY)
    handed = pl.pallas_call(
        functools.partial(layer_kernel, ARGS + tuple(scratch)),
        out_shape=jax.ShapeDtypeStruct((tok_rows, width), BF16),
        in_specs=[anywhere] * (len(ARGS) - 1),
        out_specs=pl.BlockSpec(memory_space=pltpu.VMEM),
        scratch_shapes=list(scratch.values()),
        compiler_params=pltpu.CompilerParams(
            collective_id=0, has_side_effects=True, vmem_limit_bytes=VMEM_MIB << 20
        ),
    )(
        acts, norm_gains, expert_ids[0].T, gate_weights[0].T, segment_ids,
        jnp.asarray(rope_tables(tok_rows * GROUP, tok_rows)), w_query, keyval, w_out, w_gate_up, w_down,
    )
    return handed[None]


def solution(mesh):
    placed = (
        P("section", "expert", None),
        P("section", None, None),
        P("section", None, "expert"),
        P("section", "expert", None, None),
        P("section", "expert", None),
        P("section", "expert", None, None),
        P("section", "expert", None, None),
        P("section", "expert", None),
        P("section", "expert", None),
        P("section", None),
    )
    return jax.shard_map(
        per_device if mesh.shape["expert"] == GROUP else per_device_general,
        mesh=mesh,
        in_specs=placed,
        out_specs=P("section", "expert", None),
        check_vma=False,
    )
```

```python
import functools
import math

import jax
import jax.numpy as jnp
import numpy as np
from jax import lax
from jax.experimental import pallas as pl
from jax.experimental.pallas import tpu as pltpu
from jax.sharding import PartitionSpec as P

MESH = pl.DeviceIdType.MESH

HD = 128
KV = 4
EXPERTS = 32
TOPK = 8
CAP = 24


EPS = 1e-06
ROPE_BASE = 1000000.0


def shifted_2(x, axis, by):
    length = lax.axis_size(axis)
    return lax.ppermute(x, axis, [(i, (i + by) % length) for i in range(length)])


def rms_scale(values, gain_row):
    mean_sq = jnp.mean(values * values, axis=-1, keepdims=True)
    return values * lax.rsqrt(mean_sq + EPS) * gain_row


def rotate(values, positions):
    half_width = values.shape[-1] // 2
    frequency = ROPE_BASE ** (-jnp.arange(half_width, dtype=jnp.float32) * 2.0 / values.shape[-1])
    angles = positions[:, None] * frequency[None, :]
    cosines = jnp.cos(angles)[:, None, :]
    sine_table = jnp.sin(angles)[:, None, :]
    leading = values[..., :half_width]
    trailing = values[..., half_width:]
    return jnp.concatenate(
        [leading * cosines - trailing * sine_table, trailing * cosines + leading * sine_table],
        axis=-1,
    )


def head_block(q_block, key_rows, value_rows, seg_block, seg_all, pos_block, pos_all, score_scale):
    scores = (
        jnp.einsum("qhd,kd->hqk", q_block, key_rows, preferred_element_type=jnp.float32)
        * score_scale
    )
    allowed = (seg_block[:, None] == seg_all[None, :]) & (pos_all[None, :] <= pos_block[:, None])
    scores = jnp.where(allowed[None], scores, -1e30)
    row_max = jnp.max(scores, axis=-1, keepdims=True)
    shifted = jnp.exp(scores - row_max)
    probability = (shifted / jnp.sum(shifted, axis=-1, keepdims=True)).astype(jnp.bfloat16)
    return jnp.einsum(
        "hqk,kd->qhd", probability, value_rows, preferred_element_type=jnp.float32
    ).astype(jnp.bfloat16)


def expert_rows(grouped, gate_up, down_proj):
    gate_up_out = jnp.einsum("necd,edf->necf", grouped, gate_up, preferred_element_type=jnp.float32)
    half_width = down_proj.shape[1]
    hidden = (jax.nn.silu(gate_up_out[..., :half_width]) * gate_up_out[..., half_width:]).astype(
        jnp.bfloat16
    )
    return jnp.einsum(
        "necf,efd->necd", hidden, down_proj, preferred_element_type=jnp.float32
    ).astype(jnp.bfloat16)


def send_back(results):
    return lax.all_to_all(results, "expert", split_axis=0, concat_axis=0, tiled=True)


def per_device_general(
    acts,
    norm_gains,
    w_query,
    w_keyval,
    w_out,
    w_gate_up,
    w_down,
    expert_ids,
    gate_weights,
    segment_ids,
):
    device_count = lax.axis_size("expert")
    my_index = lax.axis_index("expert")
    tok_rows = acts.shape[1]
    width = acts.shape[2]
    head_dev = w_query.shape[2] // HD
    local_experts = w_gate_up.shape[1]
    heads_total = head_dev * device_count
    gains = norm_gains[0]
    x_wide = acts[0].astype(jnp.float32)
    normed = rms_scale(x_wide, gains[0]).astype(jnp.bfloat16)
    kv_index = my_index * head_dev // (heads_total // KV)
    query_weight = w_query[0]
    gathered_keyval = lax.all_gather(w_keyval[0], "expert", axis=0, tiled=True)
    head_keyval = lax.dynamic_index_in_dim(gathered_keyval, kv_index, 1, keepdims=False)
    row_piece = lax.all_gather(normed, "expert", axis=0, tiled=True)
    piece_rows = row_piece.shape[0]
    positions = jnp.arange(piece_rows).astype(jnp.float32)
    query_piece_rows = row_piece.shape[0]
    query_positions = jnp.arange(query_piece_rows).astype(jnp.float32)
    queries = jnp.dot(row_piece, query_weight, preferred_element_type=jnp.float32).reshape(
        query_piece_rows, head_dev, HD
    )
    queries = (
        rotate(queries, query_positions)
        .astype(jnp.bfloat16)
        .reshape(query_piece_rows, head_dev * HD)
    )
    keyval = jnp.dot(row_piece, head_keyval, preferred_element_type=jnp.float32)
    key_rows = rotate(keyval[:, None, :HD], positions).astype(jnp.bfloat16).reshape(piece_rows, HD)
    value_rows = keyval[:, HD:].astype(jnp.bfloat16)
    projected = jnp.concatenate([queries, key_rows, value_rows], axis=1)
    tokens = projected.shape[0]
    all_queries = projected[:, : head_dev * HD].reshape(tokens, head_dev, HD)
    all_keys = projected[:, head_dev * HD : (head_dev + 1) * HD]
    all_values = projected[:, (head_dev + 1) * HD :]
    segments = segment_ids[0]
    all_positions = jnp.arange(tokens)
    q_rows = min(512, tokens)
    score_scale = 1.0 / math.sqrt(HD)

    def attend(first_row):
        q_block = lax.dynamic_slice_in_dim(all_queries, first_row, q_rows, 0)
        seg_block = lax.dynamic_slice_in_dim(segments, first_row, q_rows, 0)
        pos_block = first_row + jnp.arange(q_rows)
        return head_block(
            q_block,
            all_keys,
            all_values,
            seg_block,
            segments,
            pos_block,
            all_positions,
            score_scale,
        )

    block_starts = jnp.arange(tokens // q_rows) * q_rows
    attended = lax.map(attend, block_starts).reshape(tokens, head_dev * HD)
    out_weight = w_out[0]
    attention = lax.psum_scatter(
        jnp.dot(attended, out_weight, preferred_element_type=jnp.float32).astype(jnp.bfloat16),
        "expert",
        scatter_dimension=0,
        tiled=True,
    ).astype(jnp.float32)
    middle_wide = (x_wide + attention).astype(jnp.bfloat16).astype(jnp.float32)
    mixer_in = rms_scale(middle_wide, gains[1]).astype(jnp.bfloat16)
    routes_flat = expert_ids[0].reshape(-1)
    onehot = routes_flat[:, None] == jnp.arange(EXPERTS, dtype=jnp.int32)[None, :]
    order = jnp.arange(routes_flat.shape[0])
    below = (order[None, :] < order[:, None]).astype(jnp.bfloat16)
    earlier = jnp.dot(below, onehot.astype(jnp.bfloat16), preferred_element_type=jnp.float32)
    slot_rank = jnp.sum(jnp.where(onehot, earlier, 0.0), axis=1).astype(jnp.int32)
    slot_index = routes_flat * CAP + slot_rank
    routed = jnp.repeat(mixer_in, TOPK, axis=0)
    send_rows = (
        jnp.zeros((EXPERTS * CAP, width), jnp.bfloat16)
        .at[slot_index]
        .set(routed)
        .reshape(EXPERTS, CAP, width)
    )
    gate_up = w_gate_up[0]
    down_proj = w_down[0]
    received = lax.all_to_all(send_rows, "expert", split_axis=0, concat_axis=0, tiled=True)
    source_count = received.shape[0] // local_experts
    grouped = received.reshape(source_count, local_experts, received.shape[1], width)
    outputs = expert_rows(grouped, gate_up, down_proj)
    returned = send_back(outputs.reshape(received.shape))
    picked = (
        returned.reshape(EXPERTS * CAP, width)[slot_index]
        .astype(jnp.float32)
        .reshape(tok_rows, TOPK, width)
    )
    mixed = jnp.sum(picked * gate_weights[0][:, :, None], axis=1)
    result = (middle_wide + mixed).astype(jnp.bfloat16)
    handed = shifted_2(result, "section", 1)
    return handed[None]


LINE = 4
GROUP = 8
SIDES = 2
PIECES = 4
VMEM_MIB = 62
EARLY = 2
BF16 = jnp.bfloat16
F32 = jnp.float32


def remote(src, dst, send_sem, recv_sem, expert, section=None):
    if section is None:
        section = lax.axis_index("section")
    return pltpu.make_async_remote_copy(
        src_ref=src,
        dst_ref=dst,
        send_sem=send_sem,
        recv_sem=recv_sem,
        device_id=(section, expert),
        device_id_type=MESH,
    )


class Refs:
    def __init__(self, names, refs):
        for name, ref in zip(names, refs, strict=True):
            setattr(self, name, ref)


ARGS = (
    "acts", "gains", "ids", "gates", "segs", "table", "w_query", "keyval", "w_out", "w_gate_up",
    "w_down", "handed",
)


def scratch_of(tok_rows, width, kv_rows, local_experts, ff):
    piece = width // PIECES
    slots = LINE * CAP
    vmem, dma = pltpu.VMEM, pltpu.SemaphoreType.DMA
    return {
        "acts_v": vmem((tok_rows, width), BF16),
        "gains_v": vmem((2, 8, width), F32),
        "ids_v": vmem((TOPK, tok_rows), jnp.int32),
        "gates_v": vmem((TOPK, tok_rows), F32),
        "segs_v": vmem((8, tok_rows * GROUP), jnp.int32),
        "table_v": vmem((2, LINE, tok_rows, HD), F32),
        "wide_ids": vmem((TOPK, 128), jnp.int32),
        "wide_gates": vmem((TOPK, 128), F32),
        "own_gates": vmem((GROUP, 8, 128), F32),
        "all_gates": vmem((GROUP, 8, 128), F32),
        "allowed": vmem((LINE, tok_rows, 4 * tok_rows), F32),
        "rows": vmem((LINE, tok_rows, width), BF16),
        "whole_kv": vmem((kv_rows, KV, 2 * HD), BF16),
        "head_kv": vmem((KV, kv_rows, 2 * HD), BF16),
        "kv_weights": vmem((GROUP, kv_rows, 2 * HD), BF16),
        "q_weights": vmem((SIDES, width, HD), BF16),
        "out_weights": vmem((SIDES, HD, width), BF16),
        "queries": vmem((LINE, SIDES, tok_rows, HD), BF16),
        "key_values": vmem((GROUP, tok_rows, 2 * HD), BF16),
        "attended": vmem((LINE, tok_rows, SIDES * HD), BF16),
        "terms": vmem((PIECES, LINE, tok_rows, piece), BF16),
        "landed": vmem((PIECES, LINE + 1, tok_rows, piece), BF16),
        "total": vmem((tok_rows, piece), F32),
        "middle": vmem((PIECES, tok_rows, piece), BF16),
        "mixer": vmem((PIECES, SIDES, LINE, tok_rows, piece), BF16),
        "select": vmem((SIDES, local_experts, slots, LINE * tok_rows), BF16),
        "spread": vmem((SIDES, LINE * tok_rows, local_experts * slots), BF16),
        "by_slot": vmem((local_experts, SIDES * slots, 2), F32),
        "sums": vmem((local_experts, SIDES * slots, 2 * ff), F32),
        "hidden": vmem((local_experts, SIDES * slots, ff), BF16),
        "packed": vmem((SIDES, local_experts, slots, piece), BF16),
        "paired": vmem((PIECES, LINE, tok_rows, piece), BF16),
        "landed_back": vmem((PIECES, LINE, tok_rows, piece), BF16),
        "up_w": vmem((local_experts, width, 2 * ff), BF16),
        "down_w": vmem((local_experts, ff, width), BF16),
        "local_sem": dma((17 + 2 * local_experts,)),
        "rows_send": dma((LINE, 2)),
        "rows_recv": dma((LINE,)),
        "kv_send": dma((LINE,)),
        "pass_send": dma((LINE,)),
        "kv_recv": dma((GROUP,)),
        "q_sem": dma((2,)),
        "out_send": dma((PIECES,)),
        "out_recv": dma((PIECES,)),
        "gate_send": dma((GROUP,)),
        "gate_recv": dma((GROUP,)),
        "swap_send": dma((LINE,)),
        "swap_recv": dma((LINE,)),
        "term_send": dma((PIECES, LINE)),
        "term_recv": dma((PIECES, LINE + 1)),
        "mixer_send": dma((PIECES, LINE, 3)),
        "mixer_recv": dma((PIECES, SIDES, LINE)),
        "pair_send": dma((PIECES, LINE)),
        "pair_recv": dma((PIECES, LINE)),
        "share_send": dma((PIECES, LINE)),
        "share_recv": dma((PIECES, LINE)),
        "hand_send": dma((PIECES,)),
        "hand_recv": dma((PIECES,)),
    }


def turned(values, cosines, sines):
    return values * cosines + pltpu.roll(values, HD // 2, 1) * sines


def layer_kernel(names, *refs):
    r = Refs(names, refs)
    section, me = lax.axis_index("section"), lax.axis_index("expert")
    z, x = lax.div(me, 2), lax.rem(me, 2)
    partner = me + 1 - 2 * x
    can_up, can_down = z < LINE - 1, z > 0
    tok_rows, width = r.acts_v.shape
    piece = width // PIECES
    column = LINE * tok_rows
    local_experts, ff = r.down_w.shape[:2]
    slots = LINE * CAP
    pending = []

    def columns(c):
        return pl.ds(c * piece, piece)

    def send(condition, copy):
        pending.append((condition, copy))
        if condition is None:
            copy.start()
        else:
            pl.when(condition)(copy.start)

    def drain(sent):
        for condition, copy in sent:
            if condition is None:
                copy.wait_send()
            else:
                pl.when(condition)(copy.wait_send)

    sections = lax.axis_size("section")
    barrier = pltpu.get_barrier_semaphore()
    for step in range(1, GROUP):
        other = lax.rem(me + step, GROUP)
        pl.semaphore_signal(barrier, inc=1, device_id=(section, other), device_id_type=MESH)
    for step in (1, sections - 1):
        other = lax.rem(section + step, sections)
        pl.semaphore_signal(barrier, inc=1, device_id=(other, me), device_id_type=MESH)

    loads = []

    def load(src, dst):
        copy = pltpu.make_async_copy(src, dst, r.local_sem.at[len(loads)])
        copy.start()
        loads.append(copy)
        return copy

    acts_in = load(r.acts.at[0], r.acts_v)
    gains_in = [load(r.gains.at[0, pl.ds(g, 1)], r.gains_v.at[g, pl.ds(0, 1)]) for g in range(2)]
    ids_in = load(r.ids, r.ids_v)
    gates_in = load(r.gates, r.gates_v)
    segs_in = [load(r.segs, r.segs_v.at[pl.ds(row, 1)]) for row in range(8)]
    whole_kv_in = load(r.keyval.at[0], r.whole_kv)
    q_in = load(r.w_query.at[0], r.q_weights.at[x])
    table_in = load(r.table.at[x], r.table_v)
    out_in = load(r.w_out.at[0], r.out_weights.at[x])
    up_in = [load(r.w_gate_up.at[0, e], r.up_w.at[e]) for e in range(local_experts)]
    down_in = [load(r.w_down.at[0, e], r.down_w.at[e]) for e in range(local_experts)]

    acts_in.wait()
    for copy in gains_in:
        copy.wait()
    r.rows[z] = rms_scale(r.acts_v[...].astype(F32), r.gains_v[0, 0:1, :]).astype(BF16)
    pl.semaphore_wait(barrier, GROUP + 1)

    whole_kv_in.wait()
    for head in range(KV):
        r.head_kv[head] = r.whole_kv[:, head, :]
    r.kv_weights[me] = r.head_kv[z]

    def kv_pass(place, source):
        shard = place * 2 + x
        return remote(source, r.kv_weights.at[shard], r.pass_send.at[place], r.kv_recv.at[shard], partner)

    def kv_arrived(shard):
        remote(r.kv_weights.at[shard], r.kv_weights.at[shard], r.pass_send.at[0],
               r.kv_recv.at[shard], partner).wait_recv()

    def rows_copy(shard, up):
        return remote(r.rows.at[shard], r.rows.at[shard], r.rows_send.at[shard, 0 if up else 1],
                      r.rows_recv.at[shard], me + 2 if up else me - 2)

    send(None, kv_pass(z, r.head_kv.at[z]))
    for far in range(1, LINE):
        for place, there in ((z + far, z + far < LINE), (z - far, z - far >= 0)):
            send(there, remote(r.head_kv.at[place], r.kv_weights.at[me], r.kv_send.at[place],
                               r.kv_recv.at[me], place * 2 + x))
    send(can_up, rows_copy(z, True))
    send(can_down, rows_copy(z, False))
    q_swap = remote(r.w_query.at[0], r.q_weights.at[x], r.q_sem.at[0], r.q_sem.at[1], partner)
    send(None, q_swap)

    ids_in.wait()
    gates_in.wait()
    r.wide_ids[...] = jnp.full_like(r.wide_ids, -1)
    r.wide_gates[...] = jnp.zeros_like(r.wide_gates)
    r.wide_ids[:, :tok_rows] = r.ids_v[...]
    r.wide_gates[:, :tok_rows] = r.gates_v[...]
    wide_ids, wide_gates = r.wide_ids[...], r.wide_gates[...]
    row = lax.broadcasted_iota(jnp.int32, (GROUP * 8, 128), 0)
    numbers = jnp.where(lax.rem(row, 8) < local_experts, lax.div(row, 8) * local_experts + lax.rem(row, 8), -2)
    dense = jnp.zeros((GROUP * 8, 128), F32)
    for k in range(TOPK):
        dense += jnp.where(wide_ids[k : k + 1] == numbers, wide_gates[k : k + 1], 0.0)
    dense = jnp.where(lax.rem(z, 2) == 1, pltpu.roll(dense, tok_rows, 1), dense)
    for j in range(GROUP):
        r.own_gates[j] = dense[j * 8 : (j + 1) * 8]
    r.all_gates[me] = r.own_gates[me]

    def gate_copy(step):
        other = lax.rem(me + step, GROUP)
        return remote(r.own_gates.at[other], r.all_gates.at[me], r.gate_send.at[step],
                      r.gate_recv.at[step], other)

    for step in range(1, GROUP):
        send(None, gate_copy(step))

    for copy in segs_in:
        copy.wait()
    seg_wide = jnp.concatenate([r.segs_v[...].astype(F32)] * 16, axis=0)
    seg_tall = seg_wide.T.reshape(GROUP, tok_rows, 128)
    window = 4 * tok_rows
    firsts = [2 * max(place - 1, 0) for place in range(LINE)]
    for place, first in enumerate(firsts):
        own_segs = jnp.where(x == 0, seg_tall[2 * place], seg_tall[2 * place + 1])
        own_segs = jnp.concatenate([own_segs] * (window // 128), axis=1)
        near_segs = seg_wide[:tok_rows, first * tok_rows : first * tok_rows + window]
        q_position = (place * 2 + x) * tok_rows + lax.broadcasted_iota(jnp.int32, (tok_rows, window), 0)
        k_position = first * tok_rows + lax.broadcasted_iota(jnp.int32, (tok_rows, window), 1)
        allowed = (own_segs == near_segs) & (k_position <= q_position)
        r.allowed[place] = jnp.where(allowed, 1.0, 0.0)

    for far in range(1, LINE):
        for place, there in ((z - far, z - far >= 0), (z + far, z + far < LINE)):
            pl.when(there)(lambda place=place: kv_arrived(place * 2 + x))
            send(there, kv_pass(place, r.kv_weights.at[place * 2 + x]))

    def out_swap(c):
        part = r.out_weights.at[x, :, columns(c)]
        return remote(r.w_out.at[0, :, columns(c)], part, r.out_send.at[c], r.out_recv.at[c], partner)

    for c in range(EARLY):
        send(None, out_swap(c))
    for far in range(1, LINE):
        for place, there, onward, up in (
            (z - far, z - far >= 0, can_up, True),
            (z + far, z + far < LINE, can_down, False),
        ):
            pl.when(there)(lambda place=place, up=up: rows_copy(place, up).wait_recv())
            send(there & onward, rows_copy(place, up))

    table_in.wait()
    for place in range(LINE):
        kv_arrived(place * 2 + 1 - x)
    all_rows = r.rows[...].reshape(column, width)
    kv_out = jnp.dot(all_rows, r.kv_weights[...].reshape(width, 2 * HD), preferred_element_type=F32)

    def kv_swap(place, side):
        block = place * 2 + side
        return remote(r.key_values.at[block], r.key_values.at[block], r.swap_send.at[place],
                      r.swap_recv.at[place], partner)

    for place in range(LINE):
        block = place * 2 + x
        own = kv_out[place * tok_rows : (place + 1) * tok_rows]
        keys = turned(own[:, :HD], r.table_v[0, place], r.table_v[1, place])
        r.key_values[block, :, :HD] = keys.astype(BF16)
        r.key_values[block, :, HD:] = own[:, HD:].astype(BF16)
        send(None, kv_swap(place, x))
    for c in range(EARLY, PIECES):
        send(None, out_swap(c))
    q_in.wait()
    q_swap.wait_recv()
    for side in range(SIDES):
        q_out = jnp.dot(all_rows, r.q_weights[side], preferred_element_type=F32)
        for place in range(LINE):
            block = place * 2 + x
            own = q_out[place * tok_rows : (place + 1) * tok_rows]
            r.queries[place, side] = turned(own, r.table_v[0, place], r.table_v[1, place]).astype(BF16)
    for place in range(LINE):
        kv_swap(place, 1 - x).wait_recv()

    for place, first in enumerate(firsts):
        near = r.key_values[first : first + 4].reshape(window, 2 * HD)
        scores = lax.dot_general(
            r.queries[place].reshape(SIDES * tok_rows, HD), near[:, :HD], (((1,), (1,)), ((), ())),
            preferred_element_type=F32,
        ) * (1.0 / math.sqrt(HD))
        scores = jnp.where(r.allowed[place][None] > 0, scores.reshape(SIDES, tok_rows, window), -1e30)
        shifted = jnp.exp(scores - jnp.max(scores, axis=-1, keepdims=True))
        probability = (shifted / jnp.sum(shifted, axis=-1, keepdims=True)).astype(BF16)
        heads = jnp.dot(probability.reshape(SIDES * tok_rows, window), near[:, HD:],
                        preferred_element_type=F32).astype(BF16)
        for side in range(SIDES):
            r.attended[place, :, side * HD : (side + 1) * HD] = heads[side * tok_rows : (side + 1) * tok_rows]

    out_in.wait()

    def relay(c, far, up, own, landing, send_sem, recv_sem):
        place = z + far if up else z - far
        there = place < LINE if up else place >= 0
        behind = can_down if up else can_up
        slot = place if up or far > 1 else LINE
        out = remote(own(place), landing.at[c, slot], send_sem.at[c, place], recv_sem.at[c, slot],
                     me + 2 if up else me - 2)

        @pl.when(there)
        def _():
            ref = own(place)

            @pl.when(behind)
            def _():
                remote(own(place), landing.at[c, place], send_sem.at[c, place],
                       recv_sem.at[c, place], partner).wait_recv()
                ref[...] = (ref[...].astype(F32) + landing[c, place].astype(F32)).astype(BF16)

            out.start()

        pending.append((there, out))

    def settle(c, base, landing, recv_sem):
        r.total[...] = base

        @pl.when(can_down)
        def _():
            remote(landing.at[c, z], landing.at[c, z], r.hand_send.at[0], recv_sem.at[c, z],
                   partner).wait_recv()
            r.total[...] += landing[c, z].astype(F32)

        @pl.when(can_up)
        def _():
            remote(landing.at[c, LINE], landing.at[c, LINE], r.hand_send.at[0],
                   recv_sem.at[c, LINE], partner).wait_recv()
            r.total[...] += landing[c, LINE].astype(F32)

        return r.total[...]

    def mixer_copy(c, place, way):
        to = (me + 2, me - 2, partner)[way]
        return remote(r.mixer.at[c, x, place], r.mixer.at[c, x, place], r.mixer_send.at[c, place, way],
                      r.mixer_recv.at[c, x, place], to)

    def mixer_arrived(c, side, place):
        remote(r.mixer.at[c, side, place], r.mixer.at[c, side, place], r.hand_send.at[0],
               r.mixer_recv.at[c, side, place], partner).wait_recv()

    def term_start(c):
        out_swap(c).wait_recv()
        made = jnp.dot(r.attended[...].reshape(column, SIDES * HD),
                       r.out_weights[:, :, columns(c)].reshape(SIDES * HD, piece),
                       preferred_element_type=F32)
        r.terms[c] = made.astype(BF16).reshape(LINE, tok_rows, piece)

    def term_hop(c, far):
        for up in (True, False):
            relay(c, far, up, lambda place: r.terms.at[c, place], r.landed, r.term_send, r.term_recv)

    def term_end(c):
        base = r.acts_v[:, columns(c)].astype(F32) + r.terms[c, z].astype(F32)
        joined = settle(c, base, r.landed, r.term_recv).astype(BF16)
        r.middle[c] = joined
        r.mixer[c, x, z] = joined
        send(can_up, mixer_copy(c, z, 0))
        send(can_down, mixer_copy(c, z, 1))
        send(None, mixer_copy(c, z, 2))

    def mixer_hop(c, far):
        for place, there, onward, way in (
            (z - far, z - far >= 0, can_up, 0), (z + far, z + far < LINE, can_down, 1),
        ):
            pl.when(there)(lambda place=place: mixer_arrived(c, x, place))
            send(there & onward, mixer_copy(c, place, way))
            send(there, mixer_copy(c, place, 2))

    def route():
        for step in range(1, GROUP):
            gate_copy(step).wait_recv()
        row = lax.broadcasted_iota(jnp.int32, (column, column), 0)
        lane = lax.broadcasted_iota(jnp.int32, (column, column), 1)
        before = (row < lane) & (lax.div(row, tok_rows) == lax.div(lane, tok_rows))
        before = jnp.where(before, 1.0, 0.0).astype(BF16)
        first_slot = lax.div(lax.broadcasted_iota(jnp.int32, (8, column), 1), tok_rows) * CAP
        numbers = lax.broadcasted_iota(jnp.int32, (slots, column), 0)
        for side in range(SIDES):
            gates = jnp.concatenate(
                [r.all_gates[2 * j + side] + r.all_gates[2 * j + 2 + side] for j in range(0, LINE, 2)], axis=1
            )
            member = gates > 0
            rank = jnp.dot(jnp.where(member, 1.0, 0.0).astype(BF16), before, preferred_element_type=F32)
            slot_of = jnp.where(member, rank.astype(jnp.int32) + first_slot, -1)
            chosen = []
            for e in range(local_experts):
                mine = slot_of[e : e + 1] == numbers
                chosen.append(jnp.where(mine, 1.0, 0.0))
                r.select[side, e] = chosen[e].astype(BF16)
                r.by_slot[e, side * slots : (side + 1) * slots, 0:1] = jnp.sum(
                    jnp.where(mine, gates[e : e + 1], 0.0), axis=1, keepdims=True
                )
            chosen = jnp.concatenate(chosen, axis=0)
            r.spread[side] = chosen.T.astype(BF16)

    def gate_up(c):
        for place in range(LINE):
            mixer_arrived(c, 1 - x, place)
        if c == 0:
            for copy in up_in:
                copy.wait()
        gain = r.gains_v[1, 0:1, columns(c)]
        tile = min(256, ff)

        def one(e, carry):
            parts = []
            for side in range(SIDES):
                held = jnp.dot(r.select[side, e], r.mixer[c, side].reshape(column, piece),
                               preferred_element_type=F32)
                at = slice(side * slots, (side + 1) * slots)
                old = 0.0 if c == 0 else r.by_slot[e, at, 1:2]
                r.by_slot[e, at, 1:2] = old + jnp.sum(held * held, axis=1, keepdims=True)
                parts.append((held * gain).astype(BF16))
            taken = jnp.concatenate(parts, axis=0)
            for n in range(ff // tile):
                halves = []
                for half in range(2):
                    at = pl.ds(half * ff + n * tile, tile)
                    part = jnp.dot(taken, r.up_w[e, columns(c), at], preferred_element_type=F32)
                    if c > 0:
                        part = part + r.sums[e, :, at]
                    if c < PIECES - 1:
                        r.sums[e, :, at] = part
                    halves.append(part)
                if c == PIECES - 1:
                    scale = lax.rsqrt(r.by_slot[e, :, 1:2] * (1.0 / width) + EPS)
                    a, b = halves[0] * scale, halves[1] * scale
                    r.hidden[e, :, n * tile : (n + 1) * tile] = (jax.nn.silu(a) * b).astype(BF16)
            return carry

        lax.fori_loop(0, local_experts, one, 0, unroll=True)

    def ticks(stages, after=None):
        for tick in range(PIECES + len(stages) - 1):
            for stage, todo in enumerate(stages):
                if 0 <= tick - stage < PIECES:
                    todo(tick - stage)
            if after is not None and tick in after:
                after[tick]()

    hops = range(LINE - 1, 0, -1)

    def hop_stages(hop):
        return [lambda c, far=far: hop(c, far) for far in hops]

    def first_hop(c):
        term_start(c)
        term_hop(c, LINE - 1)

    ticks(
        [first_hop] + hop_stages(term_hop)[1:] + [term_end]
        + [lambda c, far=far: mixer_hop(c, far) for far in range(1, LINE)] + [gate_up],
        {0: route},
    )

    drain(pending)
    pending.clear()

    def hand(c):
        return remote(r.acts_v.at[:, columns(c)], r.handed.at[:, columns(c)], r.hand_send.at[c],
                      r.hand_recv.at[c], me, lax.rem(section + 1, sections))

    def pair_copy(c, place):
        return remote(r.mixer.at[c, 1 - x, place], r.paired.at[c, place], r.pair_send.at[c, place],
                      r.pair_recv.at[c, place], partner)

    def share_start(c):
        if c == 0:
            for copy in down_in:
                copy.wait()

        def one(e, carry):
            made = jnp.dot(r.hidden[e], r.down_w[e, :, columns(c)], preferred_element_type=F32)
            made = (made * r.by_slot[e, :, 0:1]).astype(BF16)
            for side in range(SIDES):
                r.packed[side, e] = made[side * slots : (side + 1) * slots]
            return carry

        lax.fori_loop(0, local_experts, one, 0, unroll=True)
        for side in range(SIDES):
            mixed = jnp.dot(r.spread[side], r.packed[side].reshape(local_experts * slots, piece),
                            preferred_element_type=F32)
            r.mixer[c, side] = mixed.astype(BF16).reshape(LINE, tok_rows, piece)
        for place in (0, 3, 1, 2):
            send(None, pair_copy(c, place))

    def pair_arrived(c, place):
        pair_copy(c, place).wait_recv()
        return r.paired.at[c, place]

    def others(far):
        return ((z + far, z + far < LINE), (z - far, z - far >= 0))

    def share_copy(c, place):
        return remote(r.mixer.at[c, x, place], r.landed_back.at[c, z], r.share_send.at[c, place],
                      r.share_recv.at[c, z], place * 2 + x)

    def share_send(c):
        for far in range(LINE - 1, 0, -1):
            for place, there in others(far):

                @pl.when(there)
                def _(place=place):
                    other = pair_arrived(c, place)[...].astype(F32)
                    r.mixer[c, x, place] = (r.mixer[c, x, place].astype(F32) + other).astype(BF16)

                send(there, share_copy(c, place))

    def share_end(c):
        other = pair_arrived(c, z)[...].astype(F32)
        r.total[...] = r.middle[c].astype(F32) + r.mixer[c, x, z].astype(F32) + other
        for far in range(1, LINE):
            for place, there in others(far):

                @pl.when(there)
                def _(place=place):
                    landing = r.landed_back.at[c, place]
                    remote(landing, landing, r.hand_send.at[0], r.share_recv.at[c, place], partner).wait_recv()
                    r.total[...] += landing[...].astype(F32)

        r.acts_v[:, columns(c)] = r.total[...].astype(BF16)
        send(None, hand(c))

    ticks([share_start, share_send, share_end])
    for c in range(PIECES):
        hand(c).wait_recv()
    drain(pending)


def rope_tables(tokens, tok_rows):
    half = HD // 2
    frequency = np.float32(ROPE_BASE) ** (-np.arange(half, dtype=np.float32) * np.float32(2.0 / HD))
    angles = np.arange(tokens, dtype=np.float32)[:, None] * frequency.astype(np.float32)[None, :]
    cosines, sines = np.cos(angles), np.sin(angles)
    tables = np.stack([np.concatenate([cosines, cosines], 1), np.concatenate([-sines, sines], 1)])
    tables = tables.astype(np.float32).reshape(2, tokens // (SIDES * tok_rows), SIDES, tok_rows, HD)
    return tables.transpose(2, 0, 1, 3, 4)


def per_device(
    acts,
    norm_gains,
    w_query,
    w_keyval,
    w_out,
    w_gate_up,
    w_down,
    expert_ids,
    gate_weights,
    segment_ids,
):
    tok_rows, width = acts.shape[1:]
    scratch = scratch_of(tok_rows, width, w_keyval.shape[1], w_gate_up.shape[1], w_down.shape[2])
    anywhere = pl.BlockSpec(memory_space=pl.ANY)
    handed = pl.pallas_call(
        functools.partial(layer_kernel, ARGS + tuple(scratch)),
        out_shape=jax.ShapeDtypeStruct((tok_rows, width), BF16),
        in_specs=[anywhere] * (len(ARGS) - 1),
        out_specs=pl.BlockSpec(memory_space=pltpu.VMEM),
        scratch_shapes=list(scratch.values()),
        compiler_params=pltpu.CompilerParams(
            collective_id=0, has_side_effects=True, vmem_limit_bytes=VMEM_MIB << 20
        ),
    )(
        acts, norm_gains, expert_ids[0].T, gate_weights[0].T, segment_ids,
        jnp.asarray(rope_tables(tok_rows * GROUP, tok_rows)), w_query, w_keyval, w_out, w_gate_up, w_down,
    )
    return handed[None]


def solution(mesh):
    placed = (
        P("section", "expert", None),
        P("section", None, None),
        P("section", None, "expert"),
        P("section", "expert", None, None),
        P("section", "expert", None),
        P("section", "expert", None, None),
        P("section", "expert", None, None),
        P("section", "expert", None),
        P("section", "expert", None),
        P("section", None),
    )
    return jax.shard_map(
        per_device if mesh.shape["expert"] == GROUP else per_device_general,
        mesh=mesh,
        in_specs=placed,
        out_specs=P("section", "expert", None),
        check_vma=False,
    )
```

```python
import functools
import math

import jax
import jax.numpy as jnp
import numpy as np
from jax import lax
from jax.experimental import pallas as pl
from jax.experimental.pallas import tpu as pltpu
from jax.sharding import PartitionSpec as P

MESH = pl.DeviceIdType.MESH

HD = 128
KV = 4
EXPERTS = 32
TOPK = 8
CAP = 24


EPS = 1e-06
ROPE_BASE = 1000000.0


def shifted_2(x, axis, by):
    length = lax.axis_size(axis)
    return lax.ppermute(x, axis, [(i, (i + by) % length) for i in range(length)])


def rms_scale(values, gain_row):
    mean_sq = jnp.mean(values * values, axis=-1, keepdims=True)
    return values * lax.rsqrt(mean_sq + EPS) * gain_row


def rotate(values, positions):
    half_width = values.shape[-1] // 2
    frequency = ROPE_BASE ** (-jnp.arange(half_width, dtype=jnp.float32) * 2.0 / values.shape[-1])
    angles = positions[:, None] * frequency[None, :]
    cosines = jnp.cos(angles)[:, None, :]
    sine_table = jnp.sin(angles)[:, None, :]
    leading = values[..., :half_width]
    trailing = values[..., half_width:]
    return jnp.concatenate(
        [leading * cosines - trailing * sine_table, trailing * cosines + leading * sine_table],
        axis=-1,
    )


def head_block(q_block, key_rows, value_rows, seg_block, seg_all, pos_block, pos_all, score_scale):
    scores = (
        jnp.einsum("qhd,kd->hqk", q_block, key_rows, preferred_element_type=jnp.float32)
        * score_scale
    )
    allowed = (seg_block[:, None] == seg_all[None, :]) & (pos_all[None, :] <= pos_block[:, None])
    scores = jnp.where(allowed[None], scores, -1e30)
    row_max = jnp.max(scores, axis=-1, keepdims=True)
    shifted = jnp.exp(scores - row_max)
    probability = (shifted / jnp.sum(shifted, axis=-1, keepdims=True)).astype(jnp.bfloat16)
    return jnp.einsum(
        "hqk,kd->qhd", probability, value_rows, preferred_element_type=jnp.float32
    ).astype(jnp.bfloat16)


def expert_rows(grouped, gate_up, down_proj):
    gate_up_out = jnp.einsum("necd,edf->necf", grouped, gate_up, preferred_element_type=jnp.float32)
    half_width = down_proj.shape[1]
    hidden = (jax.nn.silu(gate_up_out[..., :half_width]) * gate_up_out[..., half_width:]).astype(
        jnp.bfloat16
    )
    return jnp.einsum(
        "necf,efd->necd", hidden, down_proj, preferred_element_type=jnp.float32
    ).astype(jnp.bfloat16)


def send_back(results):
    return lax.all_to_all(results, "expert", split_axis=0, concat_axis=0, tiled=True)


def per_device_general(
    acts,
    norm_gains,
    w_query,
    w_keyval,
    w_out,
    w_gate_up,
    w_down,
    expert_ids,
    gate_weights,
    segment_ids,
):
    device_count = lax.axis_size("expert")
    my_index = lax.axis_index("expert")
    tok_rows = acts.shape[1]
    width = acts.shape[2]
    head_dev = w_query.shape[2] // HD
    local_experts = w_gate_up.shape[1]
    heads_total = head_dev * device_count
    gains = norm_gains[0]
    x_wide = acts[0].astype(jnp.float32)
    normed = rms_scale(x_wide, gains[0]).astype(jnp.bfloat16)
    kv_index = my_index * head_dev // (heads_total // KV)
    query_weight = w_query[0]
    gathered_keyval = lax.all_gather(w_keyval[0], "expert", axis=0, tiled=True)
    head_keyval = lax.dynamic_index_in_dim(gathered_keyval, kv_index, 1, keepdims=False)
    row_piece = lax.all_gather(normed, "expert", axis=0, tiled=True)
    piece_rows = row_piece.shape[0]
    positions = jnp.arange(piece_rows).astype(jnp.float32)
    query_piece_rows = row_piece.shape[0]
    query_positions = jnp.arange(query_piece_rows).astype(jnp.float32)
    queries = jnp.dot(row_piece, query_weight, preferred_element_type=jnp.float32).reshape(
        query_piece_rows, head_dev, HD
    )
    queries = (
        rotate(queries, query_positions)
        .astype(jnp.bfloat16)
        .reshape(query_piece_rows, head_dev * HD)
    )
    keyval = jnp.dot(row_piece, head_keyval, preferred_element_type=jnp.float32)
    key_rows = rotate(keyval[:, None, :HD], positions).astype(jnp.bfloat16).reshape(piece_rows, HD)
    value_rows = keyval[:, HD:].astype(jnp.bfloat16)
    projected = jnp.concatenate([queries, key_rows, value_rows], axis=1)
    tokens = projected.shape[0]
    all_queries = projected[:, : head_dev * HD].reshape(tokens, head_dev, HD)
    all_keys = projected[:, head_dev * HD : (head_dev + 1) * HD]
    all_values = projected[:, (head_dev + 1) * HD :]
    segments = segment_ids[0]
    all_positions = jnp.arange(tokens)
    q_rows = min(512, tokens)
    score_scale = 1.0 / math.sqrt(HD)

    def attend(first_row):
        q_block = lax.dynamic_slice_in_dim(all_queries, first_row, q_rows, 0)
        seg_block = lax.dynamic_slice_in_dim(segments, first_row, q_rows, 0)
        pos_block = first_row + jnp.arange(q_rows)
        return head_block(
            q_block,
            all_keys,
            all_values,
            seg_block,
            segments,
            pos_block,
            all_positions,
            score_scale,
        )

    block_starts = jnp.arange(tokens // q_rows) * q_rows
    attended = lax.map(attend, block_starts).reshape(tokens, head_dev * HD)
    out_weight = w_out[0]
    attention = lax.psum_scatter(
        jnp.dot(attended, out_weight, preferred_element_type=jnp.float32).astype(jnp.bfloat16),
        "expert",
        scatter_dimension=0,
        tiled=True,
    ).astype(jnp.float32)
    middle_wide = (x_wide + attention).astype(jnp.bfloat16).astype(jnp.float32)
    mixer_in = rms_scale(middle_wide, gains[1]).astype(jnp.bfloat16)
    routes_flat = expert_ids[0].reshape(-1)
    onehot = routes_flat[:, None] == jnp.arange(EXPERTS, dtype=jnp.int32)[None, :]
    order = jnp.arange(routes_flat.shape[0])
    below = (order[None, :] < order[:, None]).astype(jnp.bfloat16)
    earlier = jnp.dot(below, onehot.astype(jnp.bfloat16), preferred_element_type=jnp.float32)
    slot_rank = jnp.sum(jnp.where(onehot, earlier, 0.0), axis=1).astype(jnp.int32)
    slot_index = routes_flat * CAP + slot_rank
    routed = jnp.repeat(mixer_in, TOPK, axis=0)
    send_rows = (
        jnp.zeros((EXPERTS * CAP, width), jnp.bfloat16)
        .at[slot_index]
        .set(routed)
        .reshape(EXPERTS, CAP, width)
    )
    gate_up = w_gate_up[0]
    down_proj = w_down[0]
    received = lax.all_to_all(send_rows, "expert", split_axis=0, concat_axis=0, tiled=True)
    source_count = received.shape[0] // local_experts
    grouped = received.reshape(source_count, local_experts, received.shape[1], width)
    outputs = expert_rows(grouped, gate_up, down_proj)
    returned = send_back(outputs.reshape(received.shape))
    picked = (
        returned.reshape(EXPERTS * CAP, width)[slot_index]
        .astype(jnp.float32)
        .reshape(tok_rows, TOPK, width)
    )
    mixed = jnp.sum(picked * gate_weights[0][:, :, None], axis=1)
    result = (middle_wide + mixed).astype(jnp.bfloat16)
    handed = shifted_2(result, "section", 1)
    return handed[None]


LINE = 4
GROUP = 8
SIDES = 2
PIECES = 4
VMEM_MIB = 62
EARLY = 2
BF16 = jnp.bfloat16
F32 = jnp.float32


def remote(src, dst, send_sem, recv_sem, expert, section=None):
    if section is None:
        section = lax.axis_index("section")
    return pltpu.make_async_remote_copy(
        src_ref=src,
        dst_ref=dst,
        send_sem=send_sem,
        recv_sem=recv_sem,
        device_id=(section, expert),
        device_id_type=MESH,
    )


class Refs:
    def __init__(self, names, refs):
        for name, ref in zip(names, refs, strict=True):
            setattr(self, name, ref)


ARGS = (
    "acts", "gains", "ids", "gates", "segs", "table", "w_query", "keyval", "w_out", "w_gate_up",
    "w_down", "handed",
)


def scratch_of(tok_rows, width, kv_rows, local_experts, ff):
    piece = width // PIECES
    slots = LINE * CAP
    vmem, dma = pltpu.VMEM, pltpu.SemaphoreType.DMA
    return {
        "acts_v": vmem((tok_rows, width), BF16),
        "gains_v": vmem((2, 8, width), F32),
        "ids_v": vmem((TOPK, tok_rows), jnp.int32),
        "gates_v": vmem((TOPK, tok_rows), F32),
        "segs_v": vmem((8, tok_rows * GROUP), jnp.int32),
        "table_v": vmem((2, LINE, tok_rows, HD), F32),
        "wide_ids": vmem((TOPK, 128), jnp.int32),
        "wide_gates": vmem((TOPK, 128), F32),
        "own_gates": vmem((GROUP, 8, 128), F32),
        "all_gates": vmem((GROUP, 8, 128), F32),
        "allowed": vmem((LINE, tok_rows, 4 * tok_rows), F32),
        "rows": vmem((LINE, tok_rows, width), BF16),
        "whole_kv": vmem((kv_rows, KV, 2 * HD), BF16),
        "head_kv": vmem((KV, kv_rows, 2 * HD), BF16),
        "kv_weights": vmem((GROUP, kv_rows, 2 * HD), BF16),
        "q_weights": vmem((SIDES, width, HD), BF16),
        "out_weights": vmem((SIDES, HD, width), BF16),
        "queries": vmem((LINE, SIDES, tok_rows, HD), BF16),
        "key_values": vmem((GROUP, tok_rows, 2 * HD), BF16),
        "attended": vmem((LINE, tok_rows, SIDES * HD), BF16),
        "terms": vmem((PIECES, LINE, tok_rows, piece), BF16),
        "landed": vmem((PIECES, LINE + 1, tok_rows, piece), BF16),
        "total": vmem((tok_rows, piece), F32),
        "middle": vmem((PIECES, tok_rows, piece), BF16),
        "mixer": vmem((PIECES, SIDES, LINE, tok_rows, piece), BF16),
        "select": vmem((SIDES, local_experts, slots, LINE * tok_rows), BF16),
        "spread": vmem((SIDES, LINE * tok_rows, local_experts * slots), BF16),
        "by_slot": vmem((local_experts, SIDES * slots, 2), F32),
        "sums": vmem((local_experts, SIDES * slots, 2 * ff), F32),
        "hidden": vmem((local_experts, SIDES * slots, ff), BF16),
        "packed": vmem((SIDES, local_experts, slots, piece), BF16),
        "paired": vmem((PIECES, LINE, tok_rows, piece), BF16),
        "landed_back": vmem((PIECES, LINE, tok_rows, piece), BF16),
        "up_w": vmem((local_experts, width, 2 * ff), BF16),
        "down_w": vmem((local_experts, ff, width), BF16),
        "local_sem": dma((17 + 2 * local_experts,)),
        "rows_send": dma((LINE, 2)),
        "rows_recv": dma((LINE,)),
        "kv_send": dma((LINE,)),
        "pass_send": dma((LINE,)),
        "kv_recv": dma((GROUP,)),
        "q_sem": dma((2,)),
        "out_send": dma((PIECES,)),
        "out_recv": dma((PIECES,)),
        "gate_send": dma((GROUP,)),
        "gate_recv": dma((GROUP,)),
        "swap_send": dma((LINE,)),
        "swap_recv": dma((LINE,)),
        "term_send": dma((PIECES, LINE)),
        "term_recv": dma((PIECES, LINE + 1)),
        "mixer_send": dma((PIECES, LINE, 3)),
        "mixer_recv": dma((PIECES, SIDES, LINE)),
        "pair_send": dma((PIECES, LINE)),
        "pair_recv": dma((PIECES, LINE)),
        "share_send": dma((PIECES, LINE)),
        "share_recv": dma((PIECES, LINE)),
        "hand_send": dma((PIECES,)),
        "hand_recv": dma((PIECES,)),
    }


def turned(values, cosines, sines):
    return values * cosines + pltpu.roll(values, HD // 2, 1) * sines


def layer_kernel(names, *refs):
    r = Refs(names, refs)
    section, me = lax.axis_index("section"), lax.axis_index("expert")
    z, x = lax.div(me, 2), lax.rem(me, 2)
    partner = me + 1 - 2 * x
    can_up, can_down = z < LINE - 1, z > 0
    tok_rows, width = r.acts_v.shape
    piece = width // PIECES
    column = LINE * tok_rows
    local_experts, ff = r.down_w.shape[:2]
    slots = LINE * CAP
    pending = []

    def columns(c):
        return pl.ds(c * piece, piece)

    def send(condition, copy):
        pending.append((condition, copy))
        if condition is None:
            copy.start()
        else:
            pl.when(condition)(copy.start)

    def drain(sent):
        for condition, copy in sent:
            if condition is None:
                copy.wait_send()
            else:
                pl.when(condition)(copy.wait_send)

    sections = lax.axis_size("section")
    barrier = pltpu.get_barrier_semaphore()
    for step in range(1, GROUP):
        other = lax.rem(me + step, GROUP)
        pl.semaphore_signal(barrier, inc=1, device_id=(section, other), device_id_type=MESH)
    for step in (1, sections - 1):
        other = lax.rem(section + step, sections)
        pl.semaphore_signal(barrier, inc=1, device_id=(other, me), device_id_type=MESH)

    loads = []

    def load(src, dst):
        copy = pltpu.make_async_copy(src, dst, r.local_sem.at[len(loads)])
        copy.start()
        loads.append(copy)
        return copy

    acts_in = load(r.acts.at[0], r.acts_v)
    gains_in = [load(r.gains.at[0, pl.ds(g, 1)], r.gains_v.at[g, pl.ds(0, 1)]) for g in range(2)]
    ids_in = load(r.ids, r.ids_v)
    gates_in = load(r.gates, r.gates_v)
    segs_in = [load(r.segs, r.segs_v.at[pl.ds(row, 1)]) for row in range(8)]
    whole_kv_in = load(r.keyval.at[0], r.whole_kv)
    q_in = load(r.w_query.at[0], r.q_weights.at[x])
    table_in = load(r.table.at[x], r.table_v)
    out_in = load(r.w_out.at[0], r.out_weights.at[x])
    up_in = [load(r.w_gate_up.at[0, e], r.up_w.at[e]) for e in range(local_experts)]
    down_in = [load(r.w_down.at[0, e], r.down_w.at[e]) for e in range(local_experts)]

    acts_in.wait()
    for copy in gains_in:
        copy.wait()
    r.rows[z] = rms_scale(r.acts_v[...].astype(F32), r.gains_v[0, 0:1, :]).astype(BF16)
    pl.semaphore_wait(barrier, GROUP + 1)

    whole_kv_in.wait()
    for head in range(KV):
        r.head_kv[head] = r.whole_kv[:, head, :]
    r.kv_weights[me] = r.head_kv[z]

    def kv_pass(place, source):
        shard = place * 2 + x
        return remote(source, r.kv_weights.at[shard], r.pass_send.at[place], r.kv_recv.at[shard], partner)

    def kv_arrived(shard):
        remote(r.kv_weights.at[shard], r.kv_weights.at[shard], r.pass_send.at[0],
               r.kv_recv.at[shard], partner).wait_recv()

    def rows_copy(shard, up):
        return remote(r.rows.at[shard], r.rows.at[shard], r.rows_send.at[shard, 0 if up else 1],
                      r.rows_recv.at[shard], me + 2 if up else me - 2)

    send(None, kv_pass(z, r.head_kv.at[z]))
    for far in range(1, LINE):
        for place, there in ((z + far, z + far < LINE), (z - far, z - far >= 0)):
            send(there, remote(r.head_kv.at[place], r.kv_weights.at[me], r.kv_send.at[place],
                               r.kv_recv.at[me], place * 2 + x))
    send(can_up, rows_copy(z, True))
    send(can_down, rows_copy(z, False))
    q_swap = remote(r.w_query.at[0], r.q_weights.at[x], r.q_sem.at[0], r.q_sem.at[1], partner)
    send(None, q_swap)

    ids_in.wait()
    gates_in.wait()
    r.wide_ids[...] = jnp.full_like(r.wide_ids, -1)
    r.wide_gates[...] = jnp.zeros_like(r.wide_gates)
    r.wide_ids[:, :tok_rows] = r.ids_v[...]
    r.wide_gates[:, :tok_rows] = r.gates_v[...]
    wide_ids, wide_gates = r.wide_ids[...], r.wide_gates[...]
    row = lax.broadcasted_iota(jnp.int32, (GROUP * 8, 128), 0)
    numbers = jnp.where(lax.rem(row, 8) < local_experts, lax.div(row, 8) * local_experts + lax.rem(row, 8), -2)
    dense = jnp.zeros((GROUP * 8, 128), F32)
    for k in range(TOPK):
        dense += jnp.where(wide_ids[k : k + 1] == numbers, wide_gates[k : k + 1], 0.0)
    dense = jnp.where(lax.rem(z, 2) == 1, pltpu.roll(dense, tok_rows, 1), dense)
    for j in range(GROUP):
        r.own_gates[j] = dense[j * 8 : (j + 1) * 8]
    r.all_gates[me] = r.own_gates[me]

    def gate_copy(step):
        other = lax.rem(me + step, GROUP)
        return remote(r.own_gates.at[other], r.all_gates.at[me], r.gate_send.at[step],
                      r.gate_recv.at[step], other)

    for step in range(1, GROUP):
        send(None, gate_copy(step))

    for copy in segs_in:
        copy.wait()
    seg_wide = jnp.concatenate([r.segs_v[...].astype(F32)] * 16, axis=0)
    seg_tall = seg_wide.T.reshape(GROUP, tok_rows, 128)
    window = 4 * tok_rows
    firsts = [2 * max(place - 1, 0) for place in range(LINE)]
    for place, first in enumerate(firsts):
        own_segs = jnp.where(x == 0, seg_tall[2 * place], seg_tall[2 * place + 1])
        own_segs = jnp.concatenate([own_segs] * (window // 128), axis=1)
        near_segs = seg_wide[:tok_rows, first * tok_rows : first * tok_rows + window]
        q_position = (place * 2 + x) * tok_rows + lax.broadcasted_iota(jnp.int32, (tok_rows, window), 0)
        k_position = first * tok_rows + lax.broadcasted_iota(jnp.int32, (tok_rows, window), 1)
        allowed = (own_segs == near_segs) & (k_position <= q_position)
        r.allowed[place] = jnp.where(allowed, 1.0, 0.0)

    for far in range(1, LINE):
        for place, there in ((z - far, z - far >= 0), (z + far, z + far < LINE)):
            pl.when(there)(lambda place=place: kv_arrived(place * 2 + x))
            send(there, kv_pass(place, r.kv_weights.at[place * 2 + x]))

    def out_swap(c):
        part = r.out_weights.at[x, :, columns(c)]
        return remote(r.w_out.at[0, :, columns(c)], part, r.out_send.at[c], r.out_recv.at[c], partner)

    for c in range(EARLY):
        send(None, out_swap(c))
    for far in range(1, LINE):
        for place, there, onward, up in (
            (z - far, z - far >= 0, can_up, True),
            (z + far, z + far < LINE, can_down, False),
        ):
            pl.when(there)(lambda place=place, up=up: rows_copy(place, up).wait_recv())
            send(there & onward, rows_copy(place, up))

    table_in.wait()
    for place in range(LINE):
        kv_arrived(place * 2 + 1 - x)
    all_rows = r.rows[...].reshape(column, width)
    kv_out = jnp.dot(all_rows, r.kv_weights[...].reshape(width, 2 * HD), preferred_element_type=F32)

    def kv_swap(place, side):
        block = place * 2 + side
        return remote(r.key_values.at[block], r.key_values.at[block], r.swap_send.at[place],
                      r.swap_recv.at[place], partner)

    for place in range(LINE):
        block = place * 2 + x
        own = kv_out[place * tok_rows : (place + 1) * tok_rows]
        keys = turned(own[:, :HD], r.table_v[0, place], r.table_v[1, place])
        r.key_values[block, :, :HD] = keys.astype(BF16)
        r.key_values[block, :, HD:] = own[:, HD:].astype(BF16)
        send(None, kv_swap(place, x))
    for c in range(EARLY, PIECES):
        send(None, out_swap(c))
    q_in.wait()
    q_swap.wait_recv()
    for side in range(SIDES):
        q_out = jnp.dot(all_rows, r.q_weights[side], preferred_element_type=F32)
        for place in range(LINE):
            block = place * 2 + x
            own = q_out[place * tok_rows : (place + 1) * tok_rows]
            r.queries[place, side] = turned(own, r.table_v[0, place], r.table_v[1, place]).astype(BF16)
    for place in range(LINE):
        kv_swap(place, 1 - x).wait_recv()

    for place, first in enumerate(firsts):
        near = r.key_values[first : first + 4].reshape(window, 2 * HD)
        scores = lax.dot_general(
            r.queries[place].reshape(SIDES * tok_rows, HD), near[:, :HD], (((1,), (1,)), ((), ())),
            preferred_element_type=F32,
        ) * (1.0 / math.sqrt(HD))
        scores = jnp.where(r.allowed[place][None] > 0, scores.reshape(SIDES, tok_rows, window), -1e30)
        shifted = jnp.exp(scores - jnp.max(scores, axis=-1, keepdims=True))
        probability = (shifted / jnp.sum(shifted, axis=-1, keepdims=True)).astype(BF16)
        heads = jnp.dot(probability.reshape(SIDES * tok_rows, window), near[:, HD:],
                        preferred_element_type=F32).astype(BF16)
        for side in range(SIDES):
            r.attended[place, :, side * HD : (side + 1) * HD] = heads[side * tok_rows : (side + 1) * tok_rows]

    out_in.wait()

    def relay(c, far, up, own, landing, send_sem, recv_sem):
        place = z + far if up else z - far
        there = place < LINE if up else place >= 0
        behind = can_down if up else can_up
        slot = place if up or far > 1 else LINE
        out = remote(own(place), landing.at[c, slot], send_sem.at[c, place], recv_sem.at[c, slot],
                     me + 2 if up else me - 2)

        @pl.when(there)
        def _():
            ref = own(place)

            @pl.when(behind)
            def _():
                remote(own(place), landing.at[c, place], send_sem.at[c, place],
                       recv_sem.at[c, place], partner).wait_recv()
                ref[...] = (ref[...].astype(F32) + landing[c, place].astype(F32)).astype(BF16)

            out.start()

        pending.append((there, out))

    def settle(c, base, landing, recv_sem):
        r.total[...] = base

        @pl.when(can_down)
        def _():
            remote(landing.at[c, z], landing.at[c, z], r.hand_send.at[0], recv_sem.at[c, z],
                   partner).wait_recv()
            r.total[...] += landing[c, z].astype(F32)

        @pl.when(can_up)
        def _():
            remote(landing.at[c, LINE], landing.at[c, LINE], r.hand_send.at[0],
                   recv_sem.at[c, LINE], partner).wait_recv()
            r.total[...] += landing[c, LINE].astype(F32)

        return r.total[...]

    def mixer_copy(c, place, way):
        to = (me + 2, me - 2, partner)[way]
        return remote(r.mixer.at[c, x, place], r.mixer.at[c, x, place], r.mixer_send.at[c, place, way],
                      r.mixer_recv.at[c, x, place], to)

    def mixer_arrived(c, side, place):
        remote(r.mixer.at[c, side, place], r.mixer.at[c, side, place], r.hand_send.at[0],
               r.mixer_recv.at[c, side, place], partner).wait_recv()

    def term_start(c):
        out_swap(c).wait_recv()
        made = jnp.dot(r.attended[...].reshape(column, SIDES * HD),
                       r.out_weights[:, :, columns(c)].reshape(SIDES * HD, piece),
                       preferred_element_type=F32)
        r.terms[c] = made.astype(BF16).reshape(LINE, tok_rows, piece)

    def term_hop(c, far):
        for up in (True, False):
            relay(c, far, up, lambda place: r.terms.at[c, place], r.landed, r.term_send, r.term_recv)

    def term_end(c):
        base = r.acts_v[:, columns(c)].astype(F32) + r.terms[c, z].astype(F32)
        joined = settle(c, base, r.landed, r.term_recv).astype(BF16)
        r.middle[c] = joined
        r.mixer[c, x, z] = joined
        send(can_up, mixer_copy(c, z, 0))
        send(can_down, mixer_copy(c, z, 1))
        send(None, mixer_copy(c, z, 2))

    def mixer_hop(c, far):
        for place, there, onward, way in (
            (z - far, z - far >= 0, can_up, 0), (z + far, z + far < LINE, can_down, 1),
        ):
            pl.when(there)(lambda place=place: mixer_arrived(c, x, place))
            send(there & onward, mixer_copy(c, place, way))
            send(there, mixer_copy(c, place, 2))

    def route():
        for step in range(1, GROUP):
            gate_copy(step).wait_recv()
        row = lax.broadcasted_iota(jnp.int32, (column, column), 0)
        lane = lax.broadcasted_iota(jnp.int32, (column, column), 1)
        before = (row < lane) & (lax.div(row, tok_rows) == lax.div(lane, tok_rows))
        before = jnp.where(before, 1.0, 0.0).astype(BF16)
        first_slot = lax.div(lax.broadcasted_iota(jnp.int32, (8, column), 1), tok_rows) * CAP
        numbers = lax.broadcasted_iota(jnp.int32, (slots, column), 0)
        for side in range(SIDES):
            gates = jnp.concatenate(
                [r.all_gates[2 * j + side] + r.all_gates[2 * j + 2 + side] for j in range(0, LINE, 2)], axis=1
            )
            member = gates > 0
            rank = jnp.dot(jnp.where(member, 1.0, 0.0).astype(BF16), before, preferred_element_type=F32)
            slot_of = jnp.where(member, rank.astype(jnp.int32) + first_slot, -1)
            chosen = []
            for e in range(local_experts):
                mine = slot_of[e : e + 1] == numbers
                chosen.append(jnp.where(mine, 1.0, 0.0))
                r.select[side, e] = chosen[e].astype(BF16)
                r.by_slot[e, side * slots : (side + 1) * slots, 0:1] = jnp.sum(
                    jnp.where(mine, gates[e : e + 1], 0.0), axis=1, keepdims=True
                )
            chosen = jnp.concatenate(chosen, axis=0)
            r.spread[side] = chosen.T.astype(BF16)

    def gate_up(c):
        for place in range(LINE):
            mixer_arrived(c, 1 - x, place)
        if c == 0:
            for copy in up_in:
                copy.wait()
        gain = r.gains_v[1, 0:1, columns(c)]
        tile = min(256, ff)

        def one(e, carry):
            parts = []
            for side in range(SIDES):
                held = jnp.dot(r.select[side, e], r.mixer[c, side].reshape(column, piece),
                               preferred_element_type=F32)
                at = slice(side * slots, (side + 1) * slots)
                old = 0.0 if c == 0 else r.by_slot[e, at, 1:2]
                r.by_slot[e, at, 1:2] = old + jnp.sum(held * held, axis=1, keepdims=True)
                parts.append((held * gain).astype(BF16))
            taken = jnp.concatenate(parts, axis=0)
            for n in range(ff // tile):
                halves = []
                for half in range(2):
                    at = pl.ds(half * ff + n * tile, tile)
                    part = jnp.dot(taken, r.up_w[e, columns(c), at], preferred_element_type=F32)
                    if c > 0:
                        part = part + r.sums[e, :, at]
                    if c < PIECES - 1:
                        r.sums[e, :, at] = part
                    halves.append(part)
                if c == PIECES - 1:
                    scale = lax.rsqrt(r.by_slot[e, :, 1:2] * (1.0 / width) + EPS)
                    a, b = halves[0] * scale, halves[1] * scale
                    r.hidden[e, :, n * tile : (n + 1) * tile] = (jax.nn.silu(a) * b).astype(BF16)
            return carry

        lax.fori_loop(0, local_experts, one, 0, unroll=True)

    def ticks(stages, after=None, ahead=0):
        for tick in range(PIECES + len(stages) - 1):
            for stage, todo in enumerate(stages):
                for c in range(PIECES):
                    if tick == (c + stage if stage else max(c - ahead, 0)):
                        todo(c)
            if after is not None and tick in after:
                after[tick]()

    hops = range(LINE - 1, 0, -1)

    def hop_stages(hop):
        return [lambda c, far=far: hop(c, far) for far in hops]

    def first_hop(c):
        term_start(c)
        term_hop(c, LINE - 1)

    ticks(
        [first_hop] + hop_stages(term_hop)[1:] + [term_end]
        + [lambda c, far=far: mixer_hop(c, far) for far in range(1, LINE)] + [gate_up],
        {0: route},
    )

    drain(pending)
    pending.clear()

    def hand(c):
        return remote(r.acts_v.at[:, columns(c)], r.handed.at[:, columns(c)], r.hand_send.at[c],
                      r.hand_recv.at[c], me, lax.rem(section + 1, sections))

    def pair_copy(c, place):
        return remote(r.mixer.at[c, 1 - x, place], r.paired.at[c, place], r.pair_send.at[c, place],
                      r.pair_recv.at[c, place], partner)

    def share_start(c):
        if c == 0:
            for copy in down_in:
                copy.wait()

        def one(e, carry):
            made = jnp.dot(r.hidden[e], r.down_w[e, :, columns(c)], preferred_element_type=F32)
            made = (made * r.by_slot[e, :, 0:1]).astype(BF16)
            for side in range(SIDES):
                r.packed[side, e] = made[side * slots : (side + 1) * slots]
            return carry

        lax.fori_loop(0, local_experts, one, 0, unroll=True)
        for side in range(SIDES):
            mixed = jnp.dot(r.spread[side], r.packed[side].reshape(local_experts * slots, piece),
                            preferred_element_type=F32)
            r.mixer[c, side] = mixed.astype(BF16).reshape(LINE, tok_rows, piece)
        for place in (0, 3, 1, 2):
            send(None, pair_copy(c, place))

    def pair_arrived(c, place):
        pair_copy(c, place).wait_recv()
        return r.paired.at[c, place]

    def others(far):
        return ((z + far, z + far < LINE), (z - far, z - far >= 0))

    def share_copy(c, place):
        return remote(r.mixer.at[c, x, place], r.landed_back.at[c, z], r.share_send.at[c, place],
                      r.share_recv.at[c, z], place * 2 + x)

    def share_send(c):
        for far in range(LINE - 1, 0, -1):
            for place, there in others(far):

                @pl.when(there)
                def _(place=place):
                    other = pair_arrived(c, place)[...].astype(F32)
                    r.mixer[c, x, place] = (r.mixer[c, x, place].astype(F32) + other).astype(BF16)

                send(there, share_copy(c, place))

    def share_end(c):
        other = pair_arrived(c, z)[...].astype(F32)
        r.total[...] = r.middle[c].astype(F32) + r.mixer[c, x, z].astype(F32) + other
        for far in range(1, LINE):
            for place, there in others(far):

                @pl.when(there)
                def _(place=place):
                    landing = r.landed_back.at[c, place]
                    remote(landing, landing, r.hand_send.at[0], r.share_recv.at[c, place], partner).wait_recv()
                    r.total[...] += landing[...].astype(F32)

        r.acts_v[:, columns(c)] = r.total[...].astype(BF16)
        send(None, hand(c))

    ticks([share_start, share_send, share_end], ahead=1)
    for c in range(PIECES):
        hand(c).wait_recv()
    drain(pending)


def rope_tables(tokens, tok_rows):
    half = HD // 2
    frequency = np.float32(ROPE_BASE) ** (-np.arange(half, dtype=np.float32) * np.float32(2.0 / HD))
    angles = np.arange(tokens, dtype=np.float32)[:, None] * frequency.astype(np.float32)[None, :]
    cosines, sines = np.cos(angles), np.sin(angles)
    tables = np.stack([np.concatenate([cosines, cosines], 1), np.concatenate([-sines, sines], 1)])
    tables = tables.astype(np.float32).reshape(2, tokens // (SIDES * tok_rows), SIDES, tok_rows, HD)
    return tables.transpose(2, 0, 1, 3, 4)


def per_device(
    acts,
    norm_gains,
    w_query,
    w_keyval,
    w_out,
    w_gate_up,
    w_down,
    expert_ids,
    gate_weights,
    segment_ids,
):
    tok_rows, width = acts.shape[1:]
    scratch = scratch_of(tok_rows, width, w_keyval.shape[1], w_gate_up.shape[1], w_down.shape[2])
    anywhere = pl.BlockSpec(memory_space=pl.ANY)
    handed = pl.pallas_call(
        functools.partial(layer_kernel, ARGS + tuple(scratch)),
        out_shape=jax.ShapeDtypeStruct((tok_rows, width), BF16),
        in_specs=[anywhere] * (len(ARGS) - 1),
        out_specs=pl.BlockSpec(memory_space=pltpu.VMEM),
        scratch_shapes=list(scratch.values()),
        compiler_params=pltpu.CompilerParams(
            collective_id=0, has_side_effects=True, vmem_limit_bytes=VMEM_MIB << 20
        ),
    )(
        acts, norm_gains, expert_ids[0].T, gate_weights[0].T, segment_ids,
        jnp.asarray(rope_tables(tok_rows * GROUP, tok_rows)), w_query, w_keyval, w_out, w_gate_up, w_down,
    )
    return handed[None]


def solution(mesh):
    placed = (
        P("section", "expert", None),
        P("section", None, None),
        P("section", None, "expert"),
        P("section", "expert", None, None),
        P("section", "expert", None),
        P("section", "expert", None, None),
        P("section", "expert", None, None),
        P("section", "expert", None),
        P("section", "expert", None),
        P("section", None),
    )
    return jax.shard_map(
        per_device if mesh.shape["expert"] == GROUP else per_device_general,
        mesh=mesh,
        in_specs=placed,
        out_specs=P("section", "expert", None),
        check_vma=False,
    )
```

```python
import functools
import math

import jax
import jax.numpy as jnp
import numpy as np
from jax import lax
from jax.experimental import pallas as pl
from jax.experimental.pallas import tpu as pltpu
from jax.sharding import PartitionSpec as P

MESH = pl.DeviceIdType.MESH

HD = 128
KV = 4
EXPERTS = 32
TOPK = 8
CAP = 24


EPS = 1e-06
ROPE_BASE = 1000000.0


def shifted_2(x, axis, by):
    length = lax.axis_size(axis)
    return lax.ppermute(x, axis, [(i, (i + by) % length) for i in range(length)])


def rms_scale(values, gain_row):
    mean_sq = jnp.mean(values * values, axis=-1, keepdims=True)
    return values * lax.rsqrt(mean_sq + EPS) * gain_row


def rotate(values, positions):
    half_width = values.shape[-1] // 2
    frequency = ROPE_BASE ** (-jnp.arange(half_width, dtype=jnp.float32) * 2.0 / values.shape[-1])
    angles = positions[:, None] * frequency[None, :]
    cosines = jnp.cos(angles)[:, None, :]
    sine_table = jnp.sin(angles)[:, None, :]
    leading = values[..., :half_width]
    trailing = values[..., half_width:]
    return jnp.concatenate(
        [leading * cosines - trailing * sine_table, trailing * cosines + leading * sine_table],
        axis=-1,
    )


def head_block(q_block, key_rows, value_rows, seg_block, seg_all, pos_block, pos_all, score_scale):
    scores = (
        jnp.einsum("qhd,kd->hqk", q_block, key_rows, preferred_element_type=jnp.float32)
        * score_scale
    )
    allowed = (seg_block[:, None] == seg_all[None, :]) & (pos_all[None, :] <= pos_block[:, None])
    scores = jnp.where(allowed[None], scores, -1e30)
    row_max = jnp.max(scores, axis=-1, keepdims=True)
    shifted = jnp.exp(scores - row_max)
    probability = (shifted / jnp.sum(shifted, axis=-1, keepdims=True)).astype(jnp.bfloat16)
    return jnp.einsum(
        "hqk,kd->qhd", probability, value_rows, preferred_element_type=jnp.float32
    ).astype(jnp.bfloat16)


def expert_rows(grouped, gate_up, down_proj):
    gate_up_out = jnp.einsum("necd,edf->necf", grouped, gate_up, preferred_element_type=jnp.float32)
    half_width = down_proj.shape[1]
    hidden = (jax.nn.silu(gate_up_out[..., :half_width]) * gate_up_out[..., half_width:]).astype(
        jnp.bfloat16
    )
    return jnp.einsum(
        "necf,efd->necd", hidden, down_proj, preferred_element_type=jnp.float32
    ).astype(jnp.bfloat16)


def send_back(results):
    return lax.all_to_all(results, "expert", split_axis=0, concat_axis=0, tiled=True)


def per_device_general(
    acts,
    norm_gains,
    w_query,
    w_keyval,
    w_out,
    w_gate_up,
    w_down,
    expert_ids,
    gate_weights,
    segment_ids,
):
    device_count = lax.axis_size("expert")
    my_index = lax.axis_index("expert")
    tok_rows = acts.shape[1]
    width = acts.shape[2]
    head_dev = w_query.shape[2] // HD
    local_experts = w_gate_up.shape[1]
    heads_total = head_dev * device_count
    gains = norm_gains[0]
    x_wide = acts[0].astype(jnp.float32)
    normed = rms_scale(x_wide, gains[0]).astype(jnp.bfloat16)
    kv_index = my_index * head_dev // (heads_total // KV)
    query_weight = w_query[0]
    gathered_keyval = lax.all_gather(w_keyval[0], "expert", axis=0, tiled=True)
    head_keyval = lax.dynamic_index_in_dim(gathered_keyval, kv_index, 1, keepdims=False)
    row_piece = lax.all_gather(normed, "expert", axis=0, tiled=True)
    piece_rows = row_piece.shape[0]
    positions = jnp.arange(piece_rows).astype(jnp.float32)
    query_piece_rows = row_piece.shape[0]
    query_positions = jnp.arange(query_piece_rows).astype(jnp.float32)
    queries = jnp.dot(row_piece, query_weight, preferred_element_type=jnp.float32).reshape(
        query_piece_rows, head_dev, HD
    )
    queries = (
        rotate(queries, query_positions)
        .astype(jnp.bfloat16)
        .reshape(query_piece_rows, head_dev * HD)
    )
    keyval = jnp.dot(row_piece, head_keyval, preferred_element_type=jnp.float32)
    key_rows = rotate(keyval[:, None, :HD], positions).astype(jnp.bfloat16).reshape(piece_rows, HD)
    value_rows = keyval[:, HD:].astype(jnp.bfloat16)
    projected = jnp.concatenate([queries, key_rows, value_rows], axis=1)
    tokens = projected.shape[0]
    all_queries = projected[:, : head_dev * HD].reshape(tokens, head_dev, HD)
    all_keys = projected[:, head_dev * HD : (head_dev + 1) * HD]
    all_values = projected[:, (head_dev + 1) * HD :]
    segments = segment_ids[0]
    all_positions = jnp.arange(tokens)
    q_rows = min(512, tokens)
    score_scale = 1.0 / math.sqrt(HD)

    def attend(first_row):
        q_block = lax.dynamic_slice_in_dim(all_queries, first_row, q_rows, 0)
        seg_block = lax.dynamic_slice_in_dim(segments, first_row, q_rows, 0)
        pos_block = first_row + jnp.arange(q_rows)
        return head_block(
            q_block,
            all_keys,
            all_values,
            seg_block,
            segments,
            pos_block,
            all_positions,
            score_scale,
        )

    block_starts = jnp.arange(tokens // q_rows) * q_rows
    attended = lax.map(attend, block_starts).reshape(tokens, head_dev * HD)
    out_weight = w_out[0]
    attention = lax.psum_scatter(
        jnp.dot(attended, out_weight, preferred_element_type=jnp.float32).astype(jnp.bfloat16),
        "expert",
        scatter_dimension=0,
        tiled=True,
    ).astype(jnp.float32)
    middle_wide = (x_wide + attention).astype(jnp.bfloat16).astype(jnp.float32)
    mixer_in = rms_scale(middle_wide, gains[1]).astype(jnp.bfloat16)
    routes_flat = expert_ids[0].reshape(-1)
    onehot = routes_flat[:, None] == jnp.arange(EXPERTS, dtype=jnp.int32)[None, :]
    order = jnp.arange(routes_flat.shape[0])
    below = (order[None, :] < order[:, None]).astype(jnp.bfloat16)
    earlier = jnp.dot(below, onehot.astype(jnp.bfloat16), preferred_element_type=jnp.float32)
    slot_rank = jnp.sum(jnp.where(onehot, earlier, 0.0), axis=1).astype(jnp.int32)
    slot_index = routes_flat * CAP + slot_rank
    routed = jnp.repeat(mixer_in, TOPK, axis=0)
    send_rows = (
        jnp.zeros((EXPERTS * CAP, width), jnp.bfloat16)
        .at[slot_index]
        .set(routed)
        .reshape(EXPERTS, CAP, width)
    )
    gate_up = w_gate_up[0]
    down_proj = w_down[0]
    received = lax.all_to_all(send_rows, "expert", split_axis=0, concat_axis=0, tiled=True)
    source_count = received.shape[0] // local_experts
    grouped = received.reshape(source_count, local_experts, received.shape[1], width)
    outputs = expert_rows(grouped, gate_up, down_proj)
    returned = send_back(outputs.reshape(received.shape))
    picked = (
        returned.reshape(EXPERTS * CAP, width)[slot_index]
        .astype(jnp.float32)
        .reshape(tok_rows, TOPK, width)
    )
    mixed = jnp.sum(picked * gate_weights[0][:, :, None], axis=1)
    result = (middle_wide + mixed).astype(jnp.bfloat16)
    handed = shifted_2(result, "section", 1)
    return handed[None]


LINE = 4
GROUP = 8
SIDES = 2
PIECES = 4
VMEM_MIB = 62
EARLY = 2
BF16 = jnp.bfloat16
F32 = jnp.float32


def remote(src, dst, send_sem, recv_sem, expert, section=None):
    if section is None:
        section = lax.axis_index("section")
    return pltpu.make_async_remote_copy(
        src_ref=src,
        dst_ref=dst,
        send_sem=send_sem,
        recv_sem=recv_sem,
        device_id=(section, expert),
        device_id_type=MESH,
    )


class Refs:
    def __init__(self, names, refs):
        for name, ref in zip(names, refs, strict=True):
            setattr(self, name, ref)


ARGS = (
    "acts", "gains", "ids", "gates", "segs", "table", "w_query", "keyval", "w_out", "w_gate_up",
    "w_down", "handed",
)


def scratch_of(tok_rows, width, kv_rows, local_experts, ff):
    piece = width // PIECES
    slots = LINE * CAP
    vmem, dma = pltpu.VMEM, pltpu.SemaphoreType.DMA
    return {
        "acts_v": vmem((tok_rows, width), BF16),
        "gains_v": vmem((2, 8, width), F32),
        "ids_v": vmem((TOPK, tok_rows), jnp.int32),
        "gates_v": vmem((TOPK, tok_rows), F32),
        "segs_v": vmem((8, tok_rows * GROUP), jnp.int32),
        "table_v": vmem((2, LINE, tok_rows, HD), F32),
        "wide_ids": vmem((TOPK, 128), jnp.int32),
        "wide_gates": vmem((TOPK, 128), F32),
        "own_gates": vmem((GROUP, 8, 128), F32),
        "all_gates": vmem((GROUP, 8, 128), F32),
        "allowed": vmem((LINE, tok_rows, 4 * tok_rows), F32),
        "rows": vmem((LINE, tok_rows, width), BF16),
        "whole_kv": vmem((kv_rows, KV, 2 * HD), BF16),
        "head_kv": vmem((KV, kv_rows, 2 * HD), BF16),
        "kv_weights": vmem((GROUP, kv_rows, 2 * HD), BF16),
        "q_weights": vmem((SIDES, width, HD), BF16),
        "out_weights": vmem((SIDES, HD, width), BF16),
        "queries": vmem((LINE, SIDES, tok_rows, HD), BF16),
        "key_values": vmem((GROUP, tok_rows, 2 * HD), BF16),
        "attended": vmem((LINE, tok_rows, SIDES * HD), BF16),
        "terms": vmem((PIECES, LINE, tok_rows, piece), BF16),
        "landed": vmem((PIECES, LINE + 1, tok_rows, piece), BF16),
        "total": vmem((tok_rows, piece), F32),
        "middle": vmem((PIECES, tok_rows, piece), BF16),
        "mixer": vmem((PIECES, SIDES, LINE, tok_rows, piece), BF16),
        "select": vmem((SIDES, local_experts, slots, LINE * tok_rows), BF16),
        "spread": vmem((SIDES, LINE * tok_rows, local_experts * slots), BF16),
        "by_slot": vmem((local_experts, SIDES * slots, 2), F32),
        "sums": vmem((local_experts, SIDES * slots, 2 * ff), F32),
        "hidden": vmem((local_experts, SIDES * slots, ff), BF16),
        "packed": vmem((SIDES, local_experts, slots, piece), BF16),
        "paired": vmem((PIECES, LINE, tok_rows, piece), BF16),
        "landed_back": vmem((PIECES, LINE, tok_rows, piece), BF16),
        "up_w": vmem((local_experts, width, 2 * ff), BF16),
        "down_w": vmem((local_experts, ff, width), BF16),
        "local_sem": dma((17 + 2 * local_experts,)),
        "rows_send": dma((LINE, 2)),
        "rows_recv": dma((LINE,)),
        "kv_send": dma((LINE,)),
        "pass_send": dma((LINE,)),
        "kv_recv": dma((GROUP,)),
        "q_sem": dma((2,)),
        "out_send": dma((PIECES,)),
        "out_recv": dma((PIECES,)),
        "gate_send": dma((GROUP,)),
        "gate_recv": dma((GROUP,)),
        "swap_send": dma((LINE,)),
        "swap_recv": dma((LINE,)),
        "term_send": dma((PIECES, LINE)),
        "term_recv": dma((PIECES, LINE + 1)),
        "mixer_send": dma((PIECES, LINE, 3)),
        "mixer_recv": dma((PIECES, SIDES, LINE)),
        "pair_send": dma((PIECES, LINE)),
        "pair_recv": dma((PIECES, LINE)),
        "share_send": dma((PIECES, LINE)),
        "share_recv": dma((PIECES, LINE)),
        "hand_send": dma((PIECES,)),
        "hand_recv": dma((PIECES,)),
    }


def turned(values, cosines, sines):
    return values * cosines + pltpu.roll(values, HD // 2, 1) * sines


def layer_kernel(names, *refs):
    r = Refs(names, refs)
    section, me = lax.axis_index("section"), lax.axis_index("expert")
    z, x = lax.div(me, 2), lax.rem(me, 2)
    partner = me + 1 - 2 * x
    can_up, can_down = z < LINE - 1, z > 0
    tok_rows, width = r.acts_v.shape
    piece = width // PIECES
    column = LINE * tok_rows
    local_experts, ff = r.down_w.shape[:2]
    slots = LINE * CAP
    pending = []

    def columns(c):
        return pl.ds(c * piece, piece)

    def send(condition, copy):
        pending.append((condition, copy))
        if condition is None:
            copy.start()
        else:
            pl.when(condition)(copy.start)

    def drain(sent):
        for condition, copy in sent:
            if condition is None:
                copy.wait_send()
            else:
                pl.when(condition)(copy.wait_send)

    sections = lax.axis_size("section")
    barrier = pltpu.get_barrier_semaphore()
    for step in range(1, GROUP):
        other = lax.rem(me + step, GROUP)
        pl.semaphore_signal(barrier, inc=1, device_id=(section, other), device_id_type=MESH)
    for step in (1, sections - 1):
        other = lax.rem(section + step, sections)
        pl.semaphore_signal(barrier, inc=1, device_id=(other, me), device_id_type=MESH)

    loads = []

    def load(src, dst):
        copy = pltpu.make_async_copy(src, dst, r.local_sem.at[len(loads)])
        copy.start()
        loads.append(copy)
        return copy

    acts_in = load(r.acts.at[0], r.acts_v)
    gains_in = [load(r.gains.at[0, pl.ds(g, 1)], r.gains_v.at[g, pl.ds(0, 1)]) for g in range(2)]
    ids_in = load(r.ids, r.ids_v)
    gates_in = load(r.gates, r.gates_v)
    segs_in = [load(r.segs, r.segs_v.at[pl.ds(row, 1)]) for row in range(8)]
    whole_kv_in = load(r.keyval.at[0], r.whole_kv)
    q_in = load(r.w_query.at[0], r.q_weights.at[x])
    table_in = load(r.table.at[x], r.table_v)
    out_in = load(r.w_out.at[0], r.out_weights.at[x])
    up_in = [load(r.w_gate_up.at[0, e], r.up_w.at[e]) for e in range(local_experts)]
    down_in = [load(r.w_down.at[0, e], r.down_w.at[e]) for e in range(local_experts)]

    acts_in.wait()
    for copy in gains_in:
        copy.wait()
    r.rows[z] = rms_scale(r.acts_v[...].astype(F32), r.gains_v[0, 0:1, :]).astype(BF16)
    pl.semaphore_wait(barrier, GROUP + 1)

    whole_kv_in.wait()
    for head in range(KV):
        r.head_kv[head] = r.whole_kv[:, head, :]
    r.kv_weights[me] = r.head_kv[z]

    def kv_pass(place, source):
        shard = place * 2 + x
        return remote(source, r.kv_weights.at[shard], r.pass_send.at[place], r.kv_recv.at[shard], partner)

    def kv_arrived(shard):
        remote(r.kv_weights.at[shard], r.kv_weights.at[shard], r.pass_send.at[0],
               r.kv_recv.at[shard], partner).wait_recv()

    def rows_copy(shard, up):
        return remote(r.rows.at[shard], r.rows.at[shard], r.rows_send.at[shard, 0 if up else 1],
                      r.rows_recv.at[shard], me + 2 if up else me - 2)

    send(None, kv_pass(z, r.head_kv.at[z]))
    for far in range(1, LINE):
        for place, there in ((z + far, z + far < LINE), (z - far, z - far >= 0)):
            send(there, remote(r.head_kv.at[place], r.kv_weights.at[me], r.kv_send.at[place],
                               r.kv_recv.at[me], place * 2 + x))
    send(can_up, rows_copy(z, True))
    send(can_down, rows_copy(z, False))
    q_swap = remote(r.w_query.at[0], r.q_weights.at[x], r.q_sem.at[0], r.q_sem.at[1], partner)
    send(None, q_swap)

    ids_in.wait()
    gates_in.wait()
    r.wide_ids[...] = jnp.full_like(r.wide_ids, -1)
    r.wide_gates[...] = jnp.zeros_like(r.wide_gates)
    r.wide_ids[:, :tok_rows] = r.ids_v[...]
    r.wide_gates[:, :tok_rows] = r.gates_v[...]
    wide_ids, wide_gates = r.wide_ids[...], r.wide_gates[...]
    row = lax.broadcasted_iota(jnp.int32, (GROUP * 8, 128), 0)
    numbers = jnp.where(lax.rem(row, 8) < local_experts, lax.div(row, 8) * local_experts + lax.rem(row, 8), -2)
    dense = jnp.zeros((GROUP * 8, 128), F32)
    for k in range(TOPK):
        dense += jnp.where(wide_ids[k : k + 1] == numbers, wide_gates[k : k + 1], 0.0)
    dense = jnp.where(lax.rem(z, 2) == 1, pltpu.roll(dense, tok_rows, 1), dense)
    for j in range(GROUP):
        r.own_gates[j] = dense[j * 8 : (j + 1) * 8]
    r.all_gates[me] = r.own_gates[me]

    def gate_copy(step):
        other = lax.rem(me + step, GROUP)
        return remote(r.own_gates.at[other], r.all_gates.at[me], r.gate_send.at[step],
                      r.gate_recv.at[step], other)

    for step in range(1, GROUP):
        send(None, gate_copy(step))

    for copy in segs_in:
        copy.wait()
    seg_wide = jnp.concatenate([r.segs_v[...].astype(F32)] * 16, axis=0)
    seg_tall = seg_wide.T.reshape(GROUP, tok_rows, 128)
    window = 4 * tok_rows
    firsts = [2 * max(place - 1, 0) for place in range(LINE)]
    for place, first in enumerate(firsts):
        own_segs = jnp.where(x == 0, seg_tall[2 * place], seg_tall[2 * place + 1])
        own_segs = jnp.concatenate([own_segs] * (window // 128), axis=1)
        near_segs = seg_wide[:tok_rows, first * tok_rows : first * tok_rows + window]
        q_position = (place * 2 + x) * tok_rows + lax.broadcasted_iota(jnp.int32, (tok_rows, window), 0)
        k_position = first * tok_rows + lax.broadcasted_iota(jnp.int32, (tok_rows, window), 1)
        allowed = (own_segs == near_segs) & (k_position <= q_position)
        r.allowed[place] = jnp.where(allowed, 1.0, 0.0)

    for far in range(1, LINE):
        for place, there in ((z - far, z - far >= 0), (z + far, z + far < LINE)):
            pl.when(there)(lambda place=place: kv_arrived(place * 2 + x))
            send(there, kv_pass(place, r.kv_weights.at[place * 2 + x]))

    def out_swap(c):
        part = r.out_weights.at[x, :, columns(c)]
        return remote(r.w_out.at[0, :, columns(c)], part, r.out_send.at[c], r.out_recv.at[c], partner)

    for c in range(EARLY):
        send(None, out_swap(c))
    for far in range(1, LINE):
        for place, there, onward, up in (
            (z - far, z - far >= 0, can_up, True),
            (z + far, z + far < LINE, can_down, False),
        ):
            pl.when(there)(lambda place=place, up=up: rows_copy(place, up).wait_recv())
            send(there & onward, rows_copy(place, up))

    table_in.wait()
    for place in range(LINE):
        kv_arrived(place * 2 + 1 - x)
    all_rows = r.rows[...].reshape(column, width)
    kv_out = jnp.dot(all_rows, r.kv_weights[...].reshape(width, 2 * HD), preferred_element_type=F32)

    def kv_swap(place, side):
        block = place * 2 + side
        return remote(r.key_values.at[block], r.key_values.at[block], r.swap_send.at[place],
                      r.swap_recv.at[place], partner)

    for place in range(LINE):
        block = place * 2 + x
        own = kv_out[place * tok_rows : (place + 1) * tok_rows]
        keys = turned(own[:, :HD], r.table_v[0, place], r.table_v[1, place])
        r.key_values[block, :, :HD] = keys.astype(BF16)
        r.key_values[block, :, HD:] = own[:, HD:].astype(BF16)
        send(None, kv_swap(place, x))
    for c in range(EARLY, PIECES):
        send(None, out_swap(c))
    q_in.wait()
    q_swap.wait_recv()
    for side in range(SIDES):
        q_out = jnp.dot(all_rows, r.q_weights[side], preferred_element_type=F32)
        for place in range(LINE):
            block = place * 2 + x
            own = q_out[place * tok_rows : (place + 1) * tok_rows]
            r.queries[place, side] = turned(own, r.table_v[0, place], r.table_v[1, place]).astype(BF16)
    for place in range(LINE):
        kv_swap(place, 1 - x).wait_recv()

    for place, first in enumerate(firsts):
        near = r.key_values[first : first + 4].reshape(window, 2 * HD)
        scores = lax.dot_general(
            r.queries[place].reshape(SIDES * tok_rows, HD), near[:, :HD], (((1,), (1,)), ((), ())),
            preferred_element_type=F32,
        ) * (1.0 / math.sqrt(HD))
        scores = jnp.where(r.allowed[place][None] > 0, scores.reshape(SIDES, tok_rows, window), -1e30)
        shifted = jnp.exp(scores - jnp.max(scores, axis=-1, keepdims=True))
        probability = (shifted / jnp.sum(shifted, axis=-1, keepdims=True)).astype(BF16)
        heads = jnp.dot(probability.reshape(SIDES * tok_rows, window), near[:, HD:],
                        preferred_element_type=F32).astype(BF16)
        for side in range(SIDES):
            r.attended[place, :, side * HD : (side + 1) * HD] = heads[side * tok_rows : (side + 1) * tok_rows]

    out_in.wait()

    def relay(c, far, up, own, landing, send_sem, recv_sem):
        place = z + far if up else z - far
        there = place < LINE if up else place >= 0
        behind = can_down if up else can_up
        slot = place if up or far > 1 else LINE
        out = remote(own(place), landing.at[c, slot], send_sem.at[c, place], recv_sem.at[c, slot],
                     me + 2 if up else me - 2)

        @pl.when(there)
        def _():
            ref = own(place)

            @pl.when(behind)
            def _():
                remote(own(place), landing.at[c, place], send_sem.at[c, place],
                       recv_sem.at[c, place], partner).wait_recv()
                ref[...] = (ref[...].astype(F32) + landing[c, place].astype(F32)).astype(BF16)

            out.start()

        pending.append((there, out))

    def settle(c, base, landing, recv_sem):
        r.total[...] = base

        @pl.when(can_down)
        def _():
            remote(landing.at[c, z], landing.at[c, z], r.hand_send.at[0], recv_sem.at[c, z],
                   partner).wait_recv()
            r.total[...] += landing[c, z].astype(F32)

        @pl.when(can_up)
        def _():
            remote(landing.at[c, LINE], landing.at[c, LINE], r.hand_send.at[0],
                   recv_sem.at[c, LINE], partner).wait_recv()
            r.total[...] += landing[c, LINE].astype(F32)

        return r.total[...]

    def mixer_copy(c, place, way):
        to = (me + 2, me - 2, partner)[way]
        return remote(r.mixer.at[c, x, place], r.mixer.at[c, x, place], r.mixer_send.at[c, place, way],
                      r.mixer_recv.at[c, x, place], to)

    def mixer_arrived(c, side, place):
        remote(r.mixer.at[c, side, place], r.mixer.at[c, side, place], r.hand_send.at[0],
               r.mixer_recv.at[c, side, place], partner).wait_recv()

    def term_start(c):
        out_swap(c).wait_recv()
        made = jnp.dot(r.attended[...].reshape(column, SIDES * HD),
                       r.out_weights[:, :, columns(c)].reshape(SIDES * HD, piece),
                       preferred_element_type=F32)
        r.terms[c] = made.astype(BF16).reshape(LINE, tok_rows, piece)

    def term_hop(c, far):
        for up in (True, False):
            relay(c, far, up, lambda place: r.terms.at[c, place], r.landed, r.term_send, r.term_recv)

    def term_end(c):
        base = r.acts_v[:, columns(c)].astype(F32) + r.terms[c, z].astype(F32)
        joined = settle(c, base, r.landed, r.term_recv).astype(BF16)
        r.middle[c] = joined
        r.mixer[c, x, z] = joined
        send(can_up, mixer_copy(c, z, 0))
        send(can_down, mixer_copy(c, z, 1))
        send(None, mixer_copy(c, z, 2))

    def mixer_hop(c, far):
        for place, there, onward, way in (
            (z - far, z - far >= 0, can_up, 0), (z + far, z + far < LINE, can_down, 1),
        ):
            pl.when(there)(lambda place=place: mixer_arrived(c, x, place))
            send(there & onward, mixer_copy(c, place, way))
            send(there, mixer_copy(c, place, 2))

    def route():
        for step in range(1, GROUP):
            gate_copy(step).wait_recv()
        row = lax.broadcasted_iota(jnp.int32, (column, column), 0)
        lane = lax.broadcasted_iota(jnp.int32, (column, column), 1)
        before = (row < lane) & (lax.div(row, tok_rows) == lax.div(lane, tok_rows))
        before = jnp.where(before, 1.0, 0.0).astype(BF16)
        first_slot = lax.div(lax.broadcasted_iota(jnp.int32, (8, column), 1), tok_rows) * CAP
        numbers = lax.broadcasted_iota(jnp.int32, (slots, column), 0)
        for side in range(SIDES):
            gates = jnp.concatenate(
                [r.all_gates[2 * j + side] + r.all_gates[2 * j + 2 + side] for j in range(0, LINE, 2)], axis=1
            )
            member = gates > 0
            rank = jnp.dot(jnp.where(member, 1.0, 0.0).astype(BF16), before, preferred_element_type=F32)
            slot_of = jnp.where(member, rank.astype(jnp.int32) + first_slot, -1)
            chosen = []
            for e in range(local_experts):
                mine = slot_of[e : e + 1] == numbers
                chosen.append(jnp.where(mine, 1.0, 0.0))
                r.select[side, e] = chosen[e].astype(BF16)
                r.by_slot[e, side * slots : (side + 1) * slots, 0:1] = jnp.sum(
                    jnp.where(mine, gates[e : e + 1], 0.0), axis=1, keepdims=True
                )
            chosen = jnp.concatenate(chosen, axis=0)
            r.spread[side] = chosen.T.astype(BF16)

    def gate_up(c):
        for place in range(LINE):
            mixer_arrived(c, 1 - x, place)
        if c == 0:
            for copy in up_in:
                copy.wait()
        gain = r.gains_v[1, 0:1, columns(c)]
        tile = min(256, ff)

        def one(e, carry):
            parts = []
            for side in range(SIDES):
                held = jnp.dot(r.select[side, e], r.mixer[c, side].reshape(column, piece),
                               preferred_element_type=F32)
                at = slice(side * slots, (side + 1) * slots)
                old = 0.0 if c == 0 else r.by_slot[e, at, 1:2]
                r.by_slot[e, at, 1:2] = old + jnp.sum(held * held, axis=1, keepdims=True)
                parts.append((held * gain).astype(BF16))
            taken = jnp.concatenate(parts, axis=0)
            for n in range(ff // tile):
                halves = []
                for half in range(2):
                    at = pl.ds(half * ff + n * tile, tile)
                    part = jnp.dot(taken, r.up_w[e, columns(c), at], preferred_element_type=F32)
                    if c > 0:
                        part = part + r.sums[e, :, at]
                    if c < PIECES - 1:
                        r.sums[e, :, at] = part
                    halves.append(part)
                if c == PIECES - 1:
                    scale = lax.rsqrt(r.by_slot[e, :, 1:2] * (1.0 / width) + EPS)
                    a, b = halves[0] * scale, halves[1] * scale
                    r.hidden[e, :, n * tile : (n + 1) * tile] = (jax.nn.silu(a) * b).astype(BF16)
            return carry

        lax.fori_loop(0, local_experts, one, 0, unroll=True)

    def ticks(stages, after=None, ahead=0):
        for tick in range(PIECES + len(stages) - 1):
            for stage, todo in enumerate(stages):
                for c in range(PIECES):
                    if tick == (c + stage if stage else max(c - ahead, 0)):
                        todo(c)
            if after is not None and tick in after:
                after[tick]()

    hops = range(LINE - 1, 0, -1)

    def hop_stages(hop):
        return [lambda c, far=far: hop(c, far) for far in hops]

    def first_hop(c):
        term_start(c)
        term_hop(c, LINE - 1)

    ticks(
        [first_hop] + hop_stages(term_hop)[1:] + [term_end]
        + [lambda c, far=far: mixer_hop(c, far) for far in range(1, LINE)] + [gate_up],
        {0: route},
    )

    drain(pending)
    pending.clear()

    def hand(c):
        return remote(r.acts_v.at[:, columns(c)], r.handed.at[:, columns(c)], r.hand_send.at[c],
                      r.hand_recv.at[c], me, lax.rem(section + 1, sections))

    def pair_copy(c, place):
        return remote(r.mixer.at[c, 1 - x, place], r.paired.at[c, place], r.pair_send.at[c, place],
                      r.pair_recv.at[c, place], partner)

    def share_start(c):
        if c == 0:
            for copy in down_in:
                copy.wait()

        def one(e, carry):
            made = jnp.dot(r.hidden[e], r.down_w[e, :, columns(c)], preferred_element_type=F32)
            made = (made * r.by_slot[e, :, 0:1]).astype(BF16)
            for side in range(SIDES):
                r.packed[side, e] = made[side * slots : (side + 1) * slots]
            return carry

        lax.fori_loop(0, local_experts, one, 0, unroll=True)
        for side in range(SIDES):
            mixed = jnp.dot(r.spread[side], r.packed[side].reshape(local_experts * slots, piece),
                            preferred_element_type=F32)
            r.mixer[c, side] = mixed.astype(BF16).reshape(LINE, tok_rows, piece)
        for far in range(LINE - 1, 0, -1):
            for place, there in others(far):
                send(there, pair_copy(c, place))
        send(None, pair_copy(c, z))

    def pair_arrived(c, place):
        pair_copy(c, place).wait_recv()
        return r.paired.at[c, place]

    def others(far):
        return ((z + far, z + far < LINE), (z - far, z - far >= 0))

    def share_copy(c, place):
        return remote(r.mixer.at[c, x, place], r.landed_back.at[c, z], r.share_send.at[c, place],
                      r.share_recv.at[c, z], place * 2 + x)

    def share_send(c):
        for far in range(LINE - 1, 0, -1):
            for place, there in others(far):

                @pl.when(there)
                def _(place=place):
                    other = pair_arrived(c, place)[...].astype(F32)
                    r.mixer[c, x, place] = (r.mixer[c, x, place].astype(F32) + other).astype(BF16)

                send(there, share_copy(c, place))

    def share_end(c):
        other = pair_arrived(c, z)[...].astype(F32)
        r.total[...] = r.middle[c].astype(F32) + r.mixer[c, x, z].astype(F32) + other
        for far in range(1, LINE):
            for place, there in others(far):

                @pl.when(there)
                def _(place=place):
                    landing = r.landed_back.at[c, place]
                    remote(landing, landing, r.hand_send.at[0], r.share_recv.at[c, place], partner).wait_recv()
                    r.total[...] += landing[...].astype(F32)

        r.acts_v[:, columns(c)] = r.total[...].astype(BF16)
        send(None, hand(c))

    ticks([share_start, share_send, share_end], ahead=1)
    for c in range(PIECES):
        hand(c).wait_recv()
    drain(pending)


def rope_tables(tokens, tok_rows):
    half = HD // 2
    frequency = np.float32(ROPE_BASE) ** (-np.arange(half, dtype=np.float32) * np.float32(2.0 / HD))
    angles = np.arange(tokens, dtype=np.float32)[:, None] * frequency.astype(np.float32)[None, :]
    cosines, sines = np.cos(angles), np.sin(angles)
    tables = np.stack([np.concatenate([cosines, cosines], 1), np.concatenate([-sines, sines], 1)])
    tables = tables.astype(np.float32).reshape(2, tokens // (SIDES * tok_rows), SIDES, tok_rows, HD)
    return tables.transpose(2, 0, 1, 3, 4)


def per_device(
    acts,
    norm_gains,
    w_query,
    w_keyval,
    w_out,
    w_gate_up,
    w_down,
    expert_ids,
    gate_weights,
    segment_ids,
):
    tok_rows, width = acts.shape[1:]
    scratch = scratch_of(tok_rows, width, w_keyval.shape[1], w_gate_up.shape[1], w_down.shape[2])
    anywhere = pl.BlockSpec(memory_space=pl.ANY)
    handed = pl.pallas_call(
        functools.partial(layer_kernel, ARGS + tuple(scratch)),
        out_shape=jax.ShapeDtypeStruct((tok_rows, width), BF16),
        in_specs=[anywhere] * (len(ARGS) - 1),
        out_specs=pl.BlockSpec(memory_space=pltpu.VMEM),
        scratch_shapes=list(scratch.values()),
        compiler_params=pltpu.CompilerParams(
            collective_id=0, has_side_effects=True, vmem_limit_bytes=VMEM_MIB << 20
        ),
    )(
        acts, norm_gains, expert_ids[0].T, gate_weights[0].T, segment_ids,
        jnp.asarray(rope_tables(tok_rows * GROUP, tok_rows)), w_query, w_keyval, w_out, w_gate_up, w_down,
    )
    return handed[None]


def solution(mesh):
    placed = (
        P("section", "expert", None),
        P("section", None, None),
        P("section", None, "expert"),
        P("section", "expert", None, None),
        P("section", "expert", None),
        P("section", "expert", None, None),
        P("section", "expert", None, None),
        P("section", "expert", None),
        P("section", "expert", None),
        P("section", None),
    )
    return jax.shard_map(
        per_device if mesh.shape["expert"] == GROUP else per_device_general,
        mesh=mesh,
        in_specs=placed,
        out_specs=P("section", "expert", None),
        check_vma=False,
    )
```
